32 devices in a mesh: nodes: 16 (over z, y, x), stream: 2 (over core).
Axes of the slice: x: 2, y: 2, z: 4, core: 2. Of those that a mesh axis runs over, the one named last changes fastest.
Arguments:
- features: bfloat16 [5120, 1024], P('nodes'), may hold values from -6 to 6
- neighbours: int32 [5120, 50], P('nodes', 'stream'), may hold values from 0 to 5119, as said below
- present: int32 [5120, 50], P('nodes', 'stream'), may hold values from 0 to 1, as said below
- importance: int32 [5120, 50], P('nodes', 'stream'), may hold values from 1 to 64
- q_weight: bfloat16 [1024, 1024], replicated, may hold values from -0.1875 to 0.1875
- q_bias: float32 [1024], replicated, may hold values from -3 to 3
- w_weight: bfloat16 [2048, 1024], P('stream'), may hold values from -0.1875 to 0.1875
- w_bias: float32 [1024], replicated, may hold values from -3 to 3
- cotangent: bfloat16 [5120, 1024], P('nodes'), may hold values from -6 to 6
Outputs:
- embeddings: float32 [5120, 1024], P('nodes')
- feature_grad: float32 [5120, 1024], P('nodes', 'stream')
- q_weight_grad: float32 [1024, 1024], replicated
- q_bias_grad: float32 [1024], replicated
- w_weight_grad: float32 [2048, 1024], P('stream')
- w_bias_grad: float32 [1024], replicated
The draws below stay inside these ranges and needn't reach their ends.
Inputs may be any that keep to these rules, and one draw needn't show every extreme that they name: `neighbours`: number a device's nodes' slots of one half of the 50 slots node by node, j = local node * 25 + slot within the half; slot j names a row of the block of 320 rows of device j % 16 of nodes, so that each device's block is named exactly 500 times by each device and half; a row may be named several times. Each node has between 5 and 50 present slots.
All inputs are finite; a program needn't handle non-finite values.
Results may differ from the reference program's by a relative error of at most 0.014.
The reference program's roundings to bfloat16 on the way count: a program that leaves them out, or rounds other values in their place, can miss the bound.
Values may be sent and summed in bfloat16 or wider, within the bound.
No kernel may reach another device: no remote copies, remote signals or barrier semaphores. Data moves between devices by JAX's collectives and lax.ppermute only.
A program may use at most 128 MiB of HBM per device.

```python
import jax
import jax.numpy as jnp
from jax import lax

D = 1024
SLOTS = 50
HALF_SLOTS = 25
NODE_DEV = 320
NODES = 5120


def draw_neighbours(key, part):
    block_count = NODES // NODE_DEV
    half_total = NODE_DEV * HALF_SLOTS

    def one_half(row_key):
        owning_shards = jnp.arange(half_total, dtype=jnp.int32) % block_count
        local_rows = jax.random.randint(row_key, (half_total,), 0, NODE_DEV, dtype=jnp.int32)
        return (owning_shards * NODE_DEV + local_rows).reshape(NODE_DEV, HALF_SLOTS)

    def one_block(block_key):
        split_keys = jax.random.split(block_key, 2)
        first_half = one_half(split_keys[0])
        second_half = one_half(split_keys[1])
        return jnp.concatenate([first_half, second_half], axis=1)
    block_keys = jax.random.split(key, block_count)
    return jax.vmap(one_block)(block_keys).reshape(NODES, SLOTS)


def draw_present(key, part):
    count_key, order_key = jax.random.split(jax.random.fold_in(key, 11), 2)
    counts = jax.random.randint(count_key, (NODES,), 5, SLOTS + 1, dtype=jnp.int32)

    def one_order(row_key):
        return jax.random.permutation(row_key, SLOTS).astype(jnp.int32)
    ranks = jax.vmap(one_order)(jax.random.split(order_key, NODES))
    return (ranks < counts[:, None]).astype(jnp.int32)


def draw_importance(key, part):
    powers = jax.random.randint(jax.random.fold_in(key, 23), (NODES, SLOTS), 0, 7, dtype=jnp.int32)
    return jnp.left_shift(jnp.ones((NODES, SLOTS), jnp.int32), powers)


def block_levels(stream_key, extent, pieces, least, top_value):
    loudness, own = 1.0, jax.random.fold_in(stream_key, 6)
    for axis_at, parts in pieces:
        steps = jnp.exp(jax.random.uniform(jax.random.fold_in(own, axis_at), (parts,), jnp.float32, least / len(pieces), top_value / len(pieces)))
        loudness = loudness * jnp.repeat(steps, extent[axis_at] // parts).reshape([-1 if axis == axis_at else 1 for axis in range(len(extent))])
    return loudness


def centred(rng, shape, width, limit, pieces=(), kind=jnp.bfloat16):
    level = block_levels(rng, shape, pieces, -0.22, 0.18) if pieces else 1.0
    entries = jax.random.normal(rng, shape, jnp.float32) * width * level
    return jnp.minimum(jnp.maximum(entries, -limit), limit).astype(kind)


def setup_inputs(seed: int = 0) -> dict:
    arg_keys = jax.random.split(jax.random.key(seed), 10)
    features = centred(arg_keys[0], (NODES, D), 1.0, 6.0, ((0, 16),))
    neighbours = draw_neighbours(jax.random.fold_in(arg_keys[9], 71), 0)
    present = draw_present(jax.random.fold_in(arg_keys[9], 71), 0)
    importance = draw_importance(jax.random.fold_in(arg_keys[9], 71), 0)
    q_weight = centred(arg_keys[4], (D, D), D ** -0.5, 0.1875)
    q_bias = centred(arg_keys[5], (D,), 0.5, 3.0, (), jnp.float32)
    w_weight = centred(arg_keys[6], (2 * D, D), D ** -0.5, 0.1875, ((0, 2),))
    w_bias = centred(arg_keys[7], (D,), 0.5, 3.0, (), jnp.float32)
    cotangent = centred(arg_keys[8], (NODES, D), 1.0, 6.0, ((0, 16),))
    return {"features": features, "neighbours": neighbours, "present": present, "importance": importance, "q_weight": q_weight, "q_bias": q_bias, "w_weight": w_weight, "w_bias": w_bias, "cotangent": cotangent}


@jax.custom_vjp
def low(v):
    return lax.optimization_barrier(v.astype(jnp.bfloat16)).astype(jnp.float32)

@jax.custom_vjp
def low_back(v):
    return v

def low_keep(v):
    return (low(v), None)

def low_pass(kept, grad):
    return (grad,)

def back_keep(v):
    return (v, None)

def back_low(kept, grad):
    return (low(grad),)
low.defvjp(low_keep, low_pass)
low_back.defvjp(back_keep, back_low)

def reference(features, neighbours, present, importance, q_weight, q_bias, w_weight, w_bias, cotangent):
    top_importance = lax.Precision.HIGHEST
    weights = (present * importance).astype(jnp.float32)
    weight_sum = lax.optimization_barrier(jnp.sum(weights, axis=1))
    block_nodes = min(256, NODES)
    block_count = NODES // block_nodes
    id_blocks = neighbours.reshape(block_count, block_nodes, SLOTS)
    weight_blocks = weights.reshape(block_count, block_nodes, SLOTS)
    sum_blocks = weight_sum.reshape(block_count, block_nodes)

    def forward_pass(table, q_matrix, q_shift, w_matrix, w_shift):

        def block_mean(inputs):
            row_ids, importance_block_weights, block_sums = inputs
            collected_rows = low_back(table[row_ids].reshape(block_nodes * SLOTS, D))
            hidden_pre = low_back(jnp.dot(collected_rows, q_matrix, precision=top_importance) + q_shift)
            hidden_state = jax.nn.relu(hidden_pre).reshape(block_nodes, SLOTS, D)
            weighted_numerator = jnp.einsum('tz,tzo->to', importance_block_weights, hidden_state, precision=top_importance)
            return weighted_numerator / block_sums[:, None]
        aggregate = lax.map(jax.checkpoint(block_mean), (id_blocks, weight_blocks, sum_blocks)).reshape(NODES, D)
        aggregate_low = low(aggregate)
        linear = low_back(jnp.dot(table, w_matrix[:D], precision=top_importance) + jnp.dot(aggregate_low, w_matrix[D:], precision=top_importance) + w_shift)
        relu_out = jax.nn.relu(linear)
        return relu_out * lax.rsqrt(lax.optimization_barrier(jnp.mean(relu_out * relu_out, axis=1, keepdims=True)) + 1e-06)
    primals = (features.astype(jnp.float32), q_weight.astype(jnp.float32), q_bias, w_weight.astype(jnp.float32), w_bias)
    embeddings, pullback = jax.vjp(forward_pass, *primals)
    grads = pullback(cotangent.astype(jnp.float32))
    return (embeddings, grads[0], grads[1], grads[2], grads[3], grads[4])
```

```python
import jax
import jax.numpy as jnp
from jax import lax
from jax.experimental import pallas as pl
from jax.experimental.pallas import tpu as pltpu
from jax.sharding import PartitionSpec as P

PLANE = 4
TILE = 16


def slot_matrix_kernel(lists_ref, out_ref):
    turns, width = lists_ref.shape[1], out_ref.shape[1]
    ids = [lists_ref[0, turn : turn + 1, :] >> 7 for turn in range(turns)]
    weights = [(lists_ref[0, turn : turn + 1, :] & 127).astype(jnp.float32) for turn in range(turns)]

    @pl.loop(0, out_ref.shape[0] // TILE)
    def _(step):
        row_at = lax.broadcasted_iota(jnp.int32, (TILE, width), 0) + step * TILE
        total = jnp.zeros((TILE, width), jnp.float32)
        for listed, weight in zip(ids, weights):
            total = total + jnp.where(listed == row_at, weight, 0.0)
        out_ref[pl.ds(pl.multiple_of(step * TILE, TILE), TILE), :] = total.astype(jnp.bfloat16)


def slot_matrix(lists, rows):
    lines, turns, width = lists.shape
    return pl.pallas_call(
        slot_matrix_kernel,
        name="slot_matrix",
        out_shape=jax.ShapeDtypeStruct((lines * rows, width), jnp.bfloat16),
        grid=(lines,),
        in_specs=[pl.BlockSpec((1, turns, width), lambda line: (line, 0, 0))],
        out_specs=pl.BlockSpec((rows, width), lambda line: (line, 0)),
        cost_estimate=pl.CostEstimate(
            flops=3 * turns * lines * rows * width,
            bytes_accessed=2 * lines * rows * width,
            transcendentals=0,
        ),
    )(lists)


def on_device(
    features, neighbours, present, importance, q_weight, q_bias, w_weight, w_bias, cotangent
):
    rows, dim = features.shape
    slots = neighbours.shape[1]
    count = lax.axis_size("nodes")
    lines = count // PLANE
    node = lax.axis_index("nodes")
    core = lax.axis_index("stream")
    half_rows, half_dim = rows // 2, dim // 2
    f32, bf16 = jnp.float32, jnp.bfloat16

    def swap(value, bit):
        return lax.ppermute(value, "nodes", [(i, i ^ bit) for i in range(count)])

    def trade(value):
        return lax.ppermute(value, "stream", [(0, 1), (1, 0)])

    def own_half(value, axis):
        size = value.shape[axis] // 2
        return lax.dynamic_slice_in_dim(value, core * size, size, axis)

    def joined(mine, other, axis):
        return jnp.where(
            core == 0,
            jnp.concatenate([mine, other], axis),
            jnp.concatenate([other, mine], axis),
        )

    mine = own_half(features, 0)
    parts = {0: mine}
    bit = lines // 2
    while bit:
        for at in list(parts):
            parts[at ^ bit] = swap(parts[at], bit * PLANE)
        bit //= 2
    line_rows = [features] + [joined(parts[at], trade(parts[at]), 0) for at in range(1, lines)]

    per_block = -(-slots // count)
    packed = ((neighbours % rows) * 128 + present * importance).T
    block_at = jnp.arange(count, dtype=jnp.int32)[:, None]
    node_at = jnp.arange(rows, dtype=jnp.int32)[None, :]
    first = (block_at - slots * node_at) % count
    chosen = []
    for turn in range(per_block):
        slot = first + count * turn
        chosen.append(
            jnp.sum(
                jnp.where(
                    slot[None] == jnp.arange(slots, dtype=jnp.int32)[:, None, None],
                    packed[:, None, :],
                    0,
                ),
                axis=0,
            )
        )
    chosen = jnp.stack(chosen)
    chosen = jnp.concatenate([chosen, trade(chosen)], 0)
    weight_sum = jnp.sum((chosen & 127), axis=(0, 1)).astype(f32)
    named = {0: chosen}
    for bit in (2, 1):
        for at in list(named):
            named[at ^ bit] = swap(named[at], bit)
    lists = jnp.stack([named[at] for at in range(PLANE)])
    lists = lists.reshape(PLANE, 2 * per_block, lines, PLANE, rows)
    lists = lax.dynamic_index_in_dim(lists, node % PLANE, 3, False)
    order = (node // PLANE) ^ jnp.arange(lines)
    lists = jnp.take(lists, order, axis=2)
    lists = jnp.transpose(lists, (2, 1, 0, 3)).reshape(lines, 2 * per_block, PLANE * rows)
    matrix = slot_matrix(lists, rows)

    w_other = trade(w_weight)
    w_self = jnp.where(core == 0, w_weight, w_other)
    w_near = jnp.where(core == 0, w_other, w_weight)
    q_half = own_half(q_weight, 1)
    bias_half = own_half(q_bias, 0)

    high, low = [], []
    for shard in line_rows:
        hidden = jax.nn.relu(jnp.dot(shard, q_half, preferred_element_type=f32) + bias_half)
        top = lax.reduce_precision(hidden, 8, 7)
        high.append(top.astype(bf16))
        low.append((hidden - top).astype(bf16))
    high = jnp.concatenate(high, 0)
    low = jnp.concatenate(low, 0)

    def across(lhs, rhs):
        return lax.dot_general(lhs, rhs, (((0,), (0,)), ((), ())), preferred_element_type=f32)

    def times_t(lhs, rhs):
        return lax.dot_general(lhs, rhs, (((1,), (1,)), ((), ())), preferred_element_type=f32)

    partial = (across(matrix, high) + across(matrix, low)).reshape(PLANE, rows, half_dim)
    quarter = half_dim // 2
    left, right = partial[:, :, :quarter], partial[:, :, quarter:]
    got_x = swap(jnp.stack([left[1], left[3]]), 1)
    got_y = swap(jnp.stack([right[2], right[3]]), 2)
    last_y = swap(left[2] + got_x[1], 2)
    last_x = swap(right[1] + got_y[1], 1)
    numerator = jnp.concatenate(
        [left[0] + got_x[0] + last_y, right[0] + got_y[0] + last_x], axis=1
    )
    mean_half = (numerator / weight_sum[:, None]).astype(bf16)
    aggregate = joined(mean_half, trade(mean_half), 1)

    linear = (
        jnp.dot(features, w_self, preferred_element_type=f32)
        + jnp.dot(aggregate, w_near, preferred_element_type=f32)
        + w_bias
    )
    relu_out = jax.nn.relu(linear)
    scale = lax.rsqrt(jnp.mean(relu_out * relu_out, axis=1, keepdims=True) + 1e-06)
    embeddings = relu_out * scale
    grad_out = cotangent.astype(f32)
    grad_relu = scale * grad_out - relu_out * (scale * scale * scale) * jnp.mean(
        relu_out * grad_out, axis=1, keepdims=True
    )
    grad_linear = jnp.where(linear > 0, grad_relu, 0.0).astype(bf16)

    near_half = own_half(w_near, 0)
    grad_sum = (times_t(grad_linear, near_half) / weight_sum[:, None]).astype(bf16)
    from_x = swap(grad_sum, 1)
    from_y = swap(grad_sum, 2)
    diagonal = jnp.concatenate(
        [swap(from_x[:half_rows], 2), swap(from_y[half_rows:], 1)], axis=0
    )
    plane_grad = jnp.concatenate([grad_sum, from_x, from_y, diagonal], axis=0)

    def halves(value):
        middle = value.shape[-1] // 2
        return value[..., :middle], value[..., middle:]

    def summed(value):
        height, width = value.shape
        blocks = value.astype(bf16).reshape(count, height // count, width)
        order = node ^ jnp.arange(count)
        blocks = jnp.take(blocks, order, axis=0).reshape(lines, PLANE, height // count, width)

        def plus(one, two):
            return (one.astype(f32) + two.astype(f32)).astype(bf16)

        one, two = halves(blocks)
        got_one = swap(one[:, 1::2], 1)
        got_two = swap(two[:, 2:], 2)
        one = plus(one[:, 0::2], got_one)
        two = plus(two[:, :2], got_two)
        got_one = swap(one[:, 1], 2)
        got_two = swap(two[:, 1], 1)
        piece = jnp.concatenate([plus(one[:, 0], got_one), plus(two[:, 0], got_two)], -1)
        piece = {at: piece[at] for at in range(lines)}
        bit = 1
        while bit < lines:
            for at in sorted(piece, reverse=True):
                if at & bit:
                    piece[at ^ bit] = plus(piece[at ^ bit], swap(piece.pop(at), bit * PLANE))
            bit *= 2
        bit = lines // 2
        while bit:
            for at in list(piece):
                piece[at ^ bit] = swap(piece[at], bit * PLANE)
            bit //= 2
        piece = jnp.stack([piece[at] for at in range(lines)])
        one, two = halves(piece)
        one_y = swap(one, 2)
        two_x = swap(two, 1)
        one = jnp.stack([one, one_y], 1)
        two = jnp.stack([two, two_x], 1)
        one_x = swap(one, 1)
        two_y = swap(two, 2)
        one = jnp.stack([one[:, 0], one_x[:, 0], one[:, 1], one_x[:, 1]], 1)
        two = jnp.concatenate([two, two_y], 1)
        whole = jnp.concatenate([one, two], -1).reshape(count, height // count, width)
        return jnp.take(whole, order, axis=0).reshape(height, width).astype(f32)

    def summed_row(value):
        bit = 1
        while bit < count:
            value = value + swap(value, bit)
            bit *= 2
        return value

    stream_input = jnp.where(core == 0, features, aggregate)
    w_grad = summed(across(stream_input, grad_linear))
    w_bias_local = jnp.sum(grad_linear.astype(f32), axis=0)

    grad_rows = jnp.where(
        high > 0, jnp.dot(matrix, plane_grad, preferred_element_type=f32), 0.0
    )
    q_bias_half = jnp.sum(grad_rows, axis=0)
    grad_rows = grad_rows.astype(bf16)
    q_half_grad = summed(across(jnp.concatenate(line_rows, 0), grad_rows))
    biases = summed_row(jnp.stack([w_bias_local[:half_dim], w_bias_local[half_dim:], q_bias_half]))
    w_bias_grad = biases[:2].reshape(dim)
    q_bias_grad = joined(biases[2], trade(biases[2]), 0)
    q_grad = joined(q_half_grad, trade(q_half_grad), 1)

    owned = {at: grad_rows[at * rows : (at + 1) * rows] for at in range(lines)}
    bit = 1
    while bit < lines:
        for at in sorted(owned, reverse=True):
            if at & bit:
                came = swap(owned.pop(at), bit * PLANE)
                owned[at ^ bit] = (owned[at ^ bit].astype(f32) + came.astype(f32)).astype(bf16)
        bit *= 2
    row_half = owned[0]
    row_grad = joined(row_half, trade(row_half), 1)
    feature_grad = times_t(grad_linear, own_half(w_self, 0)) + times_t(
        row_grad, own_half(q_weight, 0)
    )
    return (embeddings, feature_grad, q_grad, q_bias_grad, w_grad, w_bias_grad)


def solution(mesh):
    in_specs = (
        P("nodes", None),
        P("nodes", "stream"),
        P("nodes", "stream"),
        P("nodes", "stream"),
        P(),
        P(),
        P("stream", None),
        P(),
        P("nodes", None),
    )
    out_specs = (P("nodes", None), P("nodes", "stream"), P(), P(), P("stream", None), P())
    return jax.shard_map(
        on_device, mesh=mesh, in_specs=in_specs, out_specs=out_specs, check_vma=False
    )
```

```python
import jax
import jax.numpy as jnp
from jax import lax
from jax.experimental import pallas as pl
from jax.experimental.pallas import tpu as pltpu
from jax.sharding import PartitionSpec as P

PLANE = 4
TILE = 16
PIECES = 2 * PLANE - 1
VMEM_BYTES = 48 * 1024 * 1024
ALL_VMEM = 60 * 1024 * 1024
F32, BF16, I32 = jnp.float32, jnp.bfloat16, jnp.int32


def across(lhs, rhs):
    return lax.dot_general(lhs, rhs, (((0,), (0,)), ((), ())), preferred_element_type=F32)


def times_t(lhs, rhs):
    return lax.dot_general(lhs, rhs, (((1,), (1,)), ((), ())), preferred_element_type=F32)


def aligned(start, size):
    start = start if isinstance(start, int) else pl.multiple_of(start, size)
    return pl.ds(start, size)


def spaced(space, arrays):
    return [pl.BlockSpec(memory_space=space) for _ in arrays]


def array(shape, dtype):
    return jax.ShapeDtypeStruct(shape, dtype)


def call(kernel, name, outs, place, near, far=(), scratch=(), flops=0, far_outs=0,
         limit=VMEM_BYTES, light=False):
    operands = list(near) + list(far)
    moved = sum(a.size * a.dtype.itemsize for a in operands + list(outs))
    if light:
        flops, moved = 1, 1
    return pl.pallas_call(
        kernel,
        name=name,
        out_shape=list(outs),
        in_specs=spaced(pltpu.SMEM, [place]) + spaced(pltpu.VMEM, near) + spaced(pltpu.HBM, far),
        out_specs=spaced(pltpu.VMEM, outs[: len(outs) - far_outs])
        + spaced(pltpu.HBM, outs[len(outs) - far_outs :]),
        scratch_shapes=list(scratch),
        compiler_params=pltpu.CompilerParams(vmem_limit_bytes=limit),
        cost_estimate=pl.CostEstimate(
            flops=int(flops), bytes_accessed=int(moved), transcendentals=0
        ),
    )(place, *operands)


def reversed_bits(value, bits):
    out = 0
    for bit in range(bits):
        out = out | (((value >> bit) & 1) << (bits - 1 - bit))
    return out


def away(core, slot, bits):
    return jnp.where(core == 0, reversed_bits(slot, bits), slot)


def bits_of(size):
    return size.bit_length() - 1


def bias_rows(value):
    top = value.astype(BF16).astype(F32)
    row_at = lax.broadcasted_iota(I32, (TILE, value.shape[1]), 0)
    return jnp.where(row_at == 0, top, jnp.where(row_at == 1, value - top, 0.0)).astype(BF16)


def stacked(parts, target, sem, first=0):
    copies, at = [], 0
    for index, part in enumerate(parts):
        span = pl.ds(at, part.shape[0])
        copies.append(pltpu.make_async_copy(part, target.at[span, :], sem.at[first + index]))
        at += part.shape[0]
    return copies


def start_all(copies):
    for copy in copies:
        copy.start()


def wait_all(copies):
    for copy in copies:
        copy.wait()


def sort_slots(place, neighbours, present, importance, count):
    rows, slots = neighbours.shape
    turns = -(-slots // count)
    arrays = [neighbours.T, present.T, importance.T]

    def kernel(place_ref, *refs):
        out_ref, neighbours_ref, present_ref, importance_ref, sem = refs[3:]
        copies = [
            pltpu.make_async_copy(part, target, sem.at[index])
            for index, (part, target) in enumerate(zip(refs[:3], refs[4:7]))
        ]
        start_all(copies)
        wait_all(copies)
        slot_at = lax.broadcasted_iota(I32, (slots, rows), 0)
        node_at = lax.broadcasted_iota(I32, (slots, rows), 1)
        block = (node_at * slots + slot_at) & (count - 1)
        row = neighbours_ref[...] - rows * block
        packed = row * 128 + present_ref[...] * importance_ref[...]
        block_at = lax.broadcasted_iota(I32, (count, rows), 0)
        node_at = lax.broadcasted_iota(I32, (count, rows), 1)
        first = (block_at - slots * node_at) & (count - 1)
        for turn in range(turns):
            total = jnp.zeros((count, rows), I32)
            for slot in range(slots):
                at = slot - count * turn
                if 0 <= at < count:
                    total = jnp.where(first == at, packed[slot : slot + 1, :], total)
            out_ref[turn * count : (turn + 1) * count, :] = total

    (out,) = call(
        kernel, "sort_slots", [array((turns * count, rows), I32)], place, [], arrays,
        [pltpu.VMEM((slots, rows), I32)] * 3 + [pltpu.SemaphoreType.DMA((3,))], limit=ALL_VMEM,
    )
    return out


def slot_matrix(place, lists, count):
    tall, rows = lists[0].shape
    lines, width, turns = count // PLANE, PLANE * rows, tall // count

    def kernel(place_ref, own_ref, next_ref, rest_ref, sums_ref, far_ref, out_ref, sem):
        slot_refs = [(own_ref, 0), (next_ref, 0), (rest_ref, 0), (rest_ref, tall)]
        core, spot, line = place_ref[1], place_ref[0] % PLANE, place_ref[0] // PLANE
        sums = [
            jnp.sum((ref[at : at + tall, :] & 127).astype(F32), axis=0, keepdims=True)
            for ref, at in slot_refs
        ]
        sums = jnp.broadcast_to(jnp.concatenate(sums, axis=1), (8, width))
        sums_ref[...] = sums.T
        for at in range(lines):
            block = (line ^ at) * PLANE + spot
            ids, weights = [], []
            for turn in range(turns):
                listed = jnp.concatenate(
                    [ref[pl.ds(at + turn * count + block, 1), :] for ref, at in slot_refs],
                    axis=1,
                )
                ids.append(listed >> 7)
                weights.append((listed & 127).astype(F32))
            shift = core * (rows // 2) if at else 0

            @pl.loop(0, rows // TILE)
            def _(step):
                base = step * TILE + shift
                base = jnp.where(base >= rows, base - rows, base)
                row_at = lax.broadcasted_iota(I32, (TILE, width), 0) + base
                total = jnp.zeros((TILE, width), F32)
                for listed, weight in zip(ids, weights):
                    total = total + jnp.where(listed == row_at, weight, 0.0)
                out_ref[aligned(at * rows + step * TILE, TILE), :] = total.astype(BF16)

            span = pl.ds(at * rows, rows)
            pltpu.make_async_copy(out_ref.at[span, :], far_ref.at[span, :], sem.at[at]).start()
        for at in range(lines):
            span = pl.ds(at * rows, rows)
            pltpu.make_async_copy(out_ref.at[span, :], far_ref.at[span, :], sem.at[at]).wait()

    sums, matrix = call(
        kernel, "slot_matrix", [array((width, 8), F32), array((lines * rows, width), BF16)],
        place, lists,
        scratch=[pltpu.VMEM((lines * rows, width), BF16), pltpu.SemaphoreType.DMA((lines,))],
        flops=3 * turns * lines * rows * width, far_outs=1, limit=ALL_VMEM, light=True,
    )
    return matrix, sums


def hidden_of(rows, q_ref, bias_ref):
    hidden = jnp.maximum(jnp.dot(rows, q_ref[...], preferred_element_type=F32) + bias_ref[...], 0.0)
    top = hidden.astype(BF16)
    return top, (hidden - top.astype(F32)).astype(BF16)


def hidden_rows(place, pieces, q_half, bias_half):
    total, half = sum(piece.shape[0] for piece in pieces), q_half.shape[1]

    def kernel(place_ref, q_ref, bias_ref, *refs):
        parts, (high_out, low_out, high_ref, low_ref, rows_ref, sem) = (
            refs[: len(pieces)], refs[len(pieces) :]
        )
        copies = stacked(parts, rows_ref, sem)
        start_all(copies)
        wait_all(copies)
        high_ref[...], low_ref[...] = hidden_of(rows_ref[...], q_ref, bias_ref)
        copies = [
            pltpu.make_async_copy(high_ref, high_out, sem.at[0]),
            pltpu.make_async_copy(low_ref, low_out, sem.at[1]),
        ]
        start_all(copies)
        wait_all(copies)

    return call(
        kernel, "hidden_rows", [array((total, half), BF16)] * 2, place, [q_half, bias_half], pieces,
        [pltpu.VMEM((total, half), BF16)] * 2 + [
            pltpu.VMEM((total, q_half.shape[0]), BF16),
            pltpu.SemaphoreType.DMA((max(len(pieces), 2),)),
        ],
        flops=2 * total * q_half.size, far_outs=2, limit=ALL_VMEM,
    )


def lane_span(start, size):
    low = start // 128 * 128
    high = -(-(start + size) // 128) * 128
    return low, high - low, start - low


def first_sums(place, pieces, early_high, early_low, q_half, bias_half, matrix):
    early, half = early_high.shape
    late = sum(piece.shape[0] for piece in pieces)
    total, width = matrix.shape
    count, part = len(pieces), width // PLANE
    low, span_width, skip = lane_span(width - part, part)

    def kernel(place_ref, q_ref, bias_ref, *refs):
        (matrix_in, high_in, low_in), refs = refs[:3], refs[3:]
        parts, refs = refs[:count], refs[count:]
        send_ref, high_out, low_out, rows_ref, high_ref, low_ref, matrix_ref, sem = refs
        copies = stacked(parts, rows_ref, sem)
        others = [
            pltpu.make_async_copy(
                matrix_in.at[:, pl.ds(low, span_width)], matrix_ref, sem.at[count]
            )
        ]
        others += stacked([high_in], high_ref, sem, count + 1)
        others += stacked([low_in], low_ref, sem, count + 2)
        start_all(copies + others)
        wait_all(copies)
        high_ref[early:, :], low_ref[early:, :] = hidden_of(rows_ref[...], q_ref, bias_ref)
        span = pl.ds(early, late)
        outs = [
            pltpu.make_async_copy(high_ref.at[span, :], high_out, sem.at[0]),
            pltpu.make_async_copy(low_ref.at[span, :], low_out, sem.at[1]),
        ]
        start_all(outs)
        wait_all(others)
        total_sum = across(matrix_ref[...], high_ref[...]) + across(matrix_ref[...], low_ref[...])
        send_ref[...] = total_sum[skip : skip + part, :]
        wait_all(outs)

    return call(
        kernel, "first_sums",
        [array((part, half), F32)] + [array((late, half), BF16)] * 2,
        place, [q_half, bias_half], [matrix, early_high, early_low] + list(pieces),
        [
            pltpu.VMEM((late, q_half.shape[0]), BF16),
            pltpu.VMEM((total, half), BF16),
            pltpu.VMEM((total, half), BF16),
            pltpu.VMEM((total, span_width), BF16),
            pltpu.SemaphoreType.DMA((count + 3,)),
        ],
        flops=2 * late * q_half.size + 4 * total * part * half, far_outs=2, limit=ALL_VMEM,
    )


def more_sums(place, highs, lows, matrix, first, slots):
    total = matrix.shape[0]
    part = matrix.shape[1] // PLANE
    width = slots * part
    start, span_width, skip = lane_span(first * part, width)
    half, count = highs[0].shape[1], len(highs)

    def kernel(place_ref, matrix_in, *refs):
        keep_ref, high_ref, low_ref, matrix_ref, sem = refs[2 * count :]
        copies = [
            pltpu.make_async_copy(
                matrix_in.at[:, pl.ds(start, span_width)], matrix_ref, sem.at[2 * count]
            )
        ]
        copies += stacked(refs[:count], high_ref, sem)
        copies += stacked(refs[count : 2 * count], low_ref, sem, count)
        start_all(copies)
        wait_all(copies)
        total_sum = across(matrix_ref[...], high_ref[...]) + across(matrix_ref[...], low_ref[...])
        keep_ref[...] = total_sum[skip : skip + width, :]

    (keep,) = call(
        kernel, "more_sums", [array((width, half), F32)], place, [],
        [matrix] + list(highs) + list(lows),
        [
            pltpu.VMEM((total, half), BF16),
            pltpu.VMEM((total, half), BF16),
            pltpu.VMEM((total, span_width), BF16),
            pltpu.SemaphoreType.DMA((2 * count + 1,)),
        ],
        flops=4 * total * width * half, limit=ALL_VMEM,
    )
    return keep


def plane_slices(place, features, mine, other):
    rows, dim = features.shape
    half, width = dim // 2, dim // PLANE

    def kernel(place_ref, features_ref, mine_ref, other_ref, own_ref, next_ref, send_ref):
        core, spot = place_ref[1], place_ref[0] % PLANE
        targets = [own_ref, next_ref, send_ref.at[pl.ds(0, rows), :], send_ref.at[pl.ds(rows, rows), :]]
        for slot, target in enumerate(targets):
            to = spot ^ away(core, slot, 2)

            @pl.when(core == 0)
            def _():
                target[...] = features_ref[:, aligned(to * width, width)]

            within = aligned(to % 2 * width, width)

            @pl.when((core == 1) & (to < 2))
            def _():
                target[...] = other_ref[:, within]

            @pl.when((core == 1) & (to >= 2))
            def _():
                target[...] = mine_ref[:, within]

    outs = [array((rows, width), BF16)] * 2 + [array((2 * rows, width), BF16)]
    return call(kernel, "plane_slices", outs, place, [features, mine, other])


def node_step(place, mine, other, self_part, cotangent, w_weight, w_other):
    rows, half = mine.shape
    dim = 2 * half

    def kernel(
        place_ref, mine_ref, other_ref, self_ref, cotangent_ref, w_in, w_other_in,
        embeddings_ref, grad_ref, half_ref, lhs_ref, linear_ref, near_ref, sem,
    ):
        core = place_ref[1]

        @pl.when(core == 0)
        def _():
            pltpu.make_async_copy(w_other_in, near_ref, sem).start()

        @pl.when(core == 1)
        def _():
            pltpu.make_async_copy(w_in, near_ref, sem).start()

        lhs_ref[:, aligned(core * half, half)] = mine_ref[...]
        lhs_ref[:, aligned((1 - core) * half, half)] = other_ref[...]
        pltpu.make_async_copy(w_in, near_ref, sem).wait()
        linear_ref[...] = self_ref[...] + jnp.dot(
            lhs_ref[...], near_ref[...], preferred_element_type=F32
        )

        @pl.loop(0, rows // TILE, unroll=4)
        def _(step):
            at = aligned(step * TILE, TILE)
            linear = linear_ref[at, :]
            relu_out = jnp.maximum(linear, 0.0)
            scale = lax.rsqrt(jnp.mean(relu_out * relu_out, axis=1, keepdims=True) + 1e-06)
            embeddings_ref[at, :] = relu_out * scale
            grad_out = cotangent_ref[at, :].astype(F32)
            inner = jnp.mean(relu_out * grad_out, axis=1, keepdims=True)
            grad_relu = scale * grad_out - relu_out * (scale * scale * scale) * inner
            grad_ref[at, :] = jnp.where(linear > 0, grad_relu, 0.0).astype(BF16)

        half_ref[...] = grad_ref[aligned(core * (rows // 2), rows // 2), :]

    outs = [
        array((rows, dim), F32), array((rows, dim), BF16), array((rows // 2, dim), BF16),
    ]
    return call(
        kernel, "node_step", outs, place, [mine, other, self_part, cotangent],
        [w_weight, w_other],
        [
            pltpu.VMEM((rows, dim), BF16), pltpu.VMEM((rows, dim), F32),
            pltpu.VMEM((dim, dim), BF16), pltpu.SemaphoreType.DMA(()),
        ],
        flops=2 * rows * dim * dim,
    )


def plane_copies(core, rows, pieces, target, sem):
    own, traded = pieces[0], pieces[PLANE]
    half = rows // 2
    copies = [pltpu.make_async_copy(own, target.at[pl.ds(0, rows), :], sem.at[0])]
    for slot in range(1, PLANE):
        mine = pieces[slot]
        other = traded.at[pl.ds((reversed_bits(slot, 2) - 1) * half, half), :]
        for index, (part, at) in enumerate(((mine, core), (other, 1 - core))):
            spot = pl.multiple_of(slot * rows + at * half, TILE)
            copies.append(
                pltpu.make_async_copy(
                    part, target.at[pl.ds(spot, half), :], sem.at[2 * slot - 1 + index]
                )
            )
    return copies


def self_weight(place, pieces, slices):
    rows, dim = pieces[0].shape
    width = slices[0].shape[1]

    def kernel(place_ref, *refs):
        parts, slots, out_ref = refs[:5], refs[5:9], refs[9]
        grads_ref, lhs_ref, sem, slice_sem = refs[10:]
        copies = plane_copies(place_ref[1], rows, parts, grads_ref, sem)
        own, far, near, last = slots
        spans = [own, last.at[pl.ds(0, rows), :], far.at[pl.ds(0, rows), :], last.at[pl.ds(rows, rows), :]]
        for slot, part in enumerate(spans):
            copies.append(
                pltpu.make_async_copy(part, lhs_ref.at[pl.ds(slot * rows, rows), :], slice_sem.at[slot])
            )
        for copy in copies:
            copy.start()
        for copy in copies:
            copy.wait()
        out_ref[:width, :] = across(lhs_ref[...], grads_ref[...]).astype(BF16)
        bias = jnp.sum(grads_ref[...].astype(F32), axis=0, keepdims=True)
        out_ref[width:, :] = bias_rows(bias)

    (out,) = call(
        kernel, "self_weight", [array((width + TILE, dim), BF16)], place, [],
        list(pieces) + list(slices),
        [
            pltpu.VMEM((PLANE * rows, dim), BF16),
            pltpu.VMEM((PLANE * rows, width), BF16),
            pltpu.SemaphoreType.DMA((PIECES,)),
            pltpu.SemaphoreType.DMA((PLANE,)),
        ],
        flops=2 * PLANE * rows * dim * width,
    )
    return out


def row_grad(place, sums, pieces, near_half, matrix, highs, line_parts, lines):
    rows, dim = pieces[0].shape
    half = near_half.shape[0]
    total, nodes, width = lines * rows, PLANE * rows, dim // PLANE

    def kernel(place_ref, sums_ref, near_ref, *refs):
        parts, refs = refs[:5], refs[5:]
        matrix_in, high_parts, refs = refs[0], refs[1 : 1 + len(highs)], refs[1 + len(highs) :]
        row_parts, refs = refs[: len(line_parts)], refs[len(line_parts) :]
        stay_ref, late_ref, go_ref, keep_ref, send_ref, refs = *refs[:5], refs[5:]
        grads_ref, rows_ref, sum_ref, hidden_ref, matrix_ref, high_ref = refs[:6]
        sem, row_sem, matrix_sem = refs[6:]
        core, spot = place_ref[1], place_ref[0] % PLANE
        copies = plane_copies(core, rows, parts, grads_ref, sem)
        row_copies = stacked(row_parts, rows_ref, row_sem)
        matrix_copies = stacked([matrix_in], matrix_ref, matrix_sem)
        matrix_copies += stacked(high_parts, high_ref, matrix_sem, 1)
        start_all(copies + matrix_copies + row_copies)
        for slot in range(PLANE):
            wait_all(copies[max(2 * slot - 1, 0) : 2 * slot + 1])
            span = slice(slot * rows, (slot + 1) * rows)
            grad = times_t(grads_ref[span, :], near_ref[...])
            sum_ref[span, :] = (grad / sums_ref[span, 0:1]).astype(BF16)
        wait_all(matrix_copies)
        bias = jnp.zeros((1, half), F32)
        for at in range(lines):
            span = slice(at * rows, (at + 1) * rows)
            grad = jnp.dot(matrix_ref[span, :], sum_ref[...], preferred_element_type=F32)
            grad = jnp.where(high_ref[span, :].astype(F32) > 0, grad, 0.0)
            bias = bias + jnp.sum(grad, axis=0, keepdims=True)
            hidden_ref[span, :] = grad.astype(BF16)
        for slot in range(lines):
            at = away(core, slot, bits_of(lines))
            to = slot * rows
            for ref in (stay_ref, late_ref, go_ref):
                if 0 <= to < ref.shape[0]:
                    break
                to -= ref.shape[0]
            ref[to : to + rows, :] = hidden_ref[aligned(at * rows, rows), :]
        wait_all(row_copies)
        for slot in range(PLANE):
            to = spot ^ away(core, slot, 2)
            ref, at = (keep_ref, send_ref)[slot // 2], slot % 2 * width
            ref[at : at + width, :] = across(
                rows_ref[:, aligned(to * width, width)], hidden_ref[...]
            ).astype(BF16)
        for ref in (keep_ref, send_ref):
            ref[2 * width :, :] = bias_rows(bias)

    outs = [array((total // 2, half), BF16)] + [array((total // 4, half), BF16)] * 2
    outs += [array((dim // 2 + TILE, half), BF16)] * 2
    return call(
        kernel, "row_grad", outs, place, [sums, near_half],
        list(pieces) + [matrix] + list(highs) + list(line_parts),
        [
            pltpu.VMEM((nodes, dim), BF16),
            pltpu.VMEM((total, dim), BF16),
            pltpu.VMEM((nodes, half), BF16),
            pltpu.VMEM((total, half), BF16),
            pltpu.VMEM((total, nodes), BF16),
            pltpu.VMEM((total, half), BF16),
            pltpu.SemaphoreType.DMA((PIECES,)),
            pltpu.SemaphoreType.DMA((len(line_parts),)),
            pltpu.SemaphoreType.DMA((1 + len(highs),)),
        ],
        flops=2 * nodes * dim * half + 2 * total * nodes * half + 2 * total * dim * half,
    )


def fold(place, keep, came):
    height, width = keep.shape[0] - TILE, keep.shape[1]
    part = height // 2

    def kernel(place_ref, keep_ref, came_ref, stay_ref, go_ref):
        bias = keep_ref[height:, :].astype(F32) + came_ref[height:, :].astype(F32)
        bias = bias_rows(bias[0:1] + bias[1:2])
        for ref, at in ((stay_ref, 0), (go_ref, part)):
            span = slice(at, at + part)
            ref[:part, :] = (keep_ref[span, :].astype(F32) + came_ref[span, :].astype(F32)).astype(BF16)
            ref[part:, :] = bias

    return call(
        kernel, "fold", [array((part + TILE, width), BF16)] * 2, place, [keep, came]
    )


def merge(place, keep, came):
    height, width = keep.shape[0] - TILE, keep.shape[1]

    def kernel(place_ref, keep_ref, came_ref, out_ref):
        out_ref[...] = (keep_ref[...].astype(F32) + came_ref[...].astype(F32)).astype(BF16)
        bias = keep_ref[height:, :].astype(F32) + came_ref[height:, :].astype(F32)
        out_ref[height:, :] = bias_rows(bias[0:1] + bias[1:2])

    (out,) = call(kernel, "merge", [array(keep.shape, BF16)], place, [keep, came])
    return out


def unpack(place, sides):
    tall, width = sides[0][0].shape
    height = tall // 2

    def kernel(place_ref, *refs):
        out_ref = refs[-1]
        spot = place_ref[0] % PLANE
        for side in range(len(sides)):
            core = place_ref[1] ^ side
            cols = aligned(core * width, width) if len(sides) > 1 else slice(None)
            for slot in range(PLANE):
                block = spot ^ away(core, slot, 2)
                start = slot % 2 * height
                out_ref[aligned(block * height, height), cols] = refs[2 * side + slot // 2][
                    start : start + height, :
                ].astype(F32)

    (out,) = call(
        kernel, "unpack", [array((2 * tall, width * len(sides)), F32)], place,
        [part for side in sides for part in side],
    )
    return out


def on_device(
    features, neighbours, present, importance, q_weight, q_bias, w_weight, w_bias, cotangent
):
    rows, dim = features.shape
    count = lax.axis_size("nodes")
    lines = count // PLANE
    line_bits = bits_of(lines)
    node = lax.axis_index("nodes")
    core = lax.axis_index("stream")
    place = jnp.stack([node, core]).astype(I32)
    half_rows = rows // 2
    fence = lax.optimization_barrier

    def swap(value, bit, other_bit=None):
        bits = (bit, bit if other_bit is None else other_bit)
        pairs = [
            (2 * at + side, 2 * (at ^ bits[side]) + side) for at in range(count) for side in (0, 1)
        ]
        return lax.ppermute(value, ("nodes", "stream"), pairs)

    def plane_swap(value, step):
        return swap(value, 1 << step, 2 >> step)

    def line_swap(value, step):
        return swap(value, PLANE << step, PLANE << (line_bits - 1 - step))

    def trade(value):
        return lax.ppermute(value, "stream", [(0, 1), (1, 0)])

    def own_half(value, axis):
        size = value.shape[axis] // 2
        return lax.dynamic_slice_in_dim(value, core * size, size, axis)

    def joined(mine, other, axis):
        return jnp.where(
            core == 0,
            jnp.concatenate([mine, other], axis),
            jnp.concatenate([other, mine], axis),
        )

    parts = {0: own_half(features, 0)}
    parts[lines // 2] = swap(parts[0], lines // 2 * PLANE)

    lists = sort_slots(place, neighbours, present, importance, count)
    lists = [jnp.concatenate([lists, trade(lists)], 0)]
    lists.append(plane_swap(lists[0], 1))
    lists.append(plane_swap(jnp.concatenate(lists, 0), 0))
    matrix, weight_sums = slot_matrix(place, lists, count)
    matrix, parts[lines // 2] = fence((matrix, parts[lines // 2]))
    bit = lines // 4
    while bit:
        for at in sorted(parts, reverse=True):
            parts[at ^ bit] = swap(parts[at], bit * PLANE)
        bit //= 2
    w_other = trade(w_weight)

    line_parts = [features]
    for at in range(1, lines - 1):
        line_parts += [parts[at], trade(parts[at])]
    q_half = own_half(q_weight, 1)
    bias_half = own_half(q_bias, 0)[None]
    high, low = hidden_rows(place, line_parts, q_half, bias_half)
    matrix, high, low, final = fence((matrix, high, low, parts[lines - 1]))
    line_parts += [final, trade(final)]
    send, *late = first_sums(place, line_parts[-2:], high, low, q_half, bias_half, matrix)
    highs, lows = [high, late[0]], [low, late[1]]

    came = plane_swap(send, 0)
    middle = more_sums(place, highs, lows, matrix, 1, 2)
    came, middle = fence((came, middle))
    last = plane_swap(middle[:rows] + came, 1)
    came_own = plane_swap(middle[rows:], 0)
    keep = more_sums(place, highs, lows, matrix, 0, 1)
    w_self = jnp.where(core == 0, w_weight, w_other)
    w_near = jnp.where(core == 0, w_other, w_weight)
    self_part = jnp.dot(features, w_self, preferred_element_type=F32) + w_bias
    ready = (self_part, own_half(w_near, 0), own_half(w_self, 0), own_half(q_weight, 0), keep)
    last, ready = fence((last, ready))
    self_part, near_half, self_half, q_rows, keep = ready
    mean_half = ((keep + came_own + last) / weight_sums[:rows, 0:1]).astype(BF16)

    mean_other = trade(mean_half)
    own_slice, next_slice, send_slices = plane_slices(place, features, mean_half, mean_other)
    far_slices = plane_swap(send_slices, 0)
    embeddings, grad_linear, grad_half = node_step(
        place, mean_half, mean_other, self_part, cotangent, w_weight, w_other
    )
    grad_half, far_slices = fence((grad_half, far_slices))

    one, two = plane_swap(grad_half, 1), plane_swap(grad_half, 0)
    last_slices = plane_swap(jnp.concatenate([next_slice, far_slices[rows:]], 0), 1)
    one, two = fence((one, two))
    three = plane_swap(one, 0)
    three, last_slices = fence((three, last_slices))
    pieces = [grad_linear, one, two, three, trade(jnp.concatenate([one, two, three], 0))]
    slices = [own_slice, far_slices, next_slice, last_slices]
    w_part = self_weight(place, pieces, slices)
    pieces, w_part = fence((pieces, w_part))

    stay, late, go, q_keep, q_send = row_grad(
        place, weight_sums, pieces, near_half, matrix, highs, line_parts, lines
    )
    w_came = line_swap(w_part, 0)
    stay, late, go, q_keep, q_send, w_came = fence((stay, late, go, q_keep, q_send, w_came))

    def last_sum(keep, came):
        height = keep.shape[0] - TILE
        total = keep.astype(F32) + came.astype(F32)
        return total[:height].astype(BF16), total[height] + total[height + 1]

    def grow(piece, came):
        return jnp.concatenate([piece, came], 0)

    biases = {}

    def steps_of(name, first, line_steps):
        def fold_step(state):
            return fold(place, *state)

        def merge_step(state):
            total = merge(place, *state)
            return total, total

        def last_step(state):
            piece, biases[name] = last_sum(*state)
            return piece, piece

        def grow_step(state):
            piece = grow(*state)
            return piece, piece

        steps = [(fold_step, plane_swap, 1)] if first else []
        steps += [(merge_step, line_swap, step) for step in line_steps]
        return steps + [(last_step, plane_swap, 1), (grow_step, plane_swap, 0)]

    q_steps = steps_of("q", True, range(line_bits))
    w_steps = steps_of("w", False, range(1, line_bits))
    w_steps.insert(line_bits - 1, None)

    q_state, w_state = (q_keep, plane_swap(q_send, 0)), (w_part, w_came)
    last_round = len(q_steps)
    rows_came, row_round = {}, last_round - 2
    for index in range(last_round + 1):
        rows_send = None
        if index == row_round:
            rows_send = go
        if index == row_round + 1:
            rows_send = late
        if index == row_round + 2:
            half = stay.shape[0] // 2
            rows_send = (stay[half:].astype(F32) + rows_came[row_round].astype(F32)).astype(BF16)
        if index:
            kind, exchange, step = q_steps[index - 1]
            keep, send = kind(q_state)
            if rows_send is not None:
                send, rows_send = fence((send, rows_send))
            q_state = (keep, exchange(send, step))
        if rows_send is not None:
            rows_came[index] = line_swap(rows_send, max(index - row_round - 1, 0))
        w_step = w_steps[index] if index < len(w_steps) else None
        if w_step is not None:
            kind, exchange, step = w_step
            keep, send = kind(w_state)
            w_state = (keep, exchange(send, step))
        w_open = index in (line_bits - 2, len(w_steps) - 1)
        if index < last_round and w_open:
            q_state, go, late, rows_came = fence((q_state, go, late, rows_came))
        elif index < last_round:
            q_state, w_state, go, late, rows_came = fence((q_state, w_state, go, late, rows_came))
    w_grad = unpack(place, [list(w_state)])
    q_plane, q_last = q_state
    rows_late, rows_next = rows_came[row_round + 1], rows_came[row_round + 2]
    q_grad = unpack(place, [[q_plane, q_last], [trade(q_plane), trade(q_last)]])
    w_bias_grad, q_bias_half = biases["w"], biases["q"]
    q_bias_grad = joined(q_bias_half, trade(q_bias_half), 0)

    half = stay.shape[0] // 2
    came_sum = rows_late.astype(F32) + rows_next.astype(F32)
    stay = stay[:half]
    for step in range(2, line_bits):
        half = came_sum.shape[0] // 2
        next_came = line_swap((stay[half:].astype(F32) + came_sum[half:]).astype(BF16), step)
        stay, came_sum = stay[:half], came_sum[:half] + next_came.astype(F32)
    came_sum = joined(came_sum[:half_rows], came_sum[half_rows:], 0)
    row_half = (stay.astype(F32) + came_sum).astype(BF16)
    row_full = joined(row_half, trade(row_half), 1)
    feature_grad = times_t(grad_linear, self_half) + times_t(row_full, q_rows)
    return (embeddings, feature_grad, q_grad, q_bias_grad, w_grad, w_bias_grad)


def solution(mesh):
    in_specs = (
        P("nodes", None),
        P("nodes", "stream"),
        P("nodes", "stream"),
        P("nodes", "stream"),
        P(),
        P(),
        P("stream", None),
        P(),
        P("nodes", None),
    )
    out_specs = (P("nodes", None), P("nodes", "stream"), P(), P(), P("stream", None), P())
    return jax.shard_map(
        on_device, mesh=mesh, in_specs=in_specs, out_specs=out_specs, check_vma=False
    )
```

```python
import jax
import jax.numpy as jnp
from jax import lax
from jax.experimental import pallas as pl
from jax.experimental.pallas import tpu as pltpu
from jax.sharding import PartitionSpec as P

PLANE = 4
TILE = 16
PIECES = 2 * PLANE - 1
VMEM_BYTES = 48 * 1024 * 1024
ALL_VMEM = 67_000_000
F32, BF16, I32 = jnp.float32, jnp.bfloat16, jnp.int32


def across(lhs, rhs):
    return lax.dot_general(lhs, rhs, (((0,), (0,)), ((), ())), preferred_element_type=F32)


def times_t(lhs, rhs):
    return lax.dot_general(lhs, rhs, (((1,), (1,)), ((), ())), preferred_element_type=F32)


def aligned(start, size):
    start = start if isinstance(start, int) else pl.multiple_of(start, size)
    return pl.ds(start, size)


def spaced(space, arrays):
    return [pl.BlockSpec(memory_space=space) for _ in arrays]


def array(shape, dtype):
    return jax.ShapeDtypeStruct(shape, dtype)


def call(kernel, name, outs, place, near, far=(), scratch=(), flops=0, far_outs=0,
         limit=VMEM_BYTES, light=False):
    operands = list(near) + list(far)
    moved = sum(a.size * a.dtype.itemsize for a in operands + list(outs))
    if light:
        flops, moved = 1, 1
    return pl.pallas_call(
        kernel,
        name=name,
        out_shape=list(outs),
        in_specs=spaced(pltpu.SMEM, [place]) + spaced(pltpu.VMEM, near) + spaced(pltpu.HBM, far),
        out_specs=spaced(pltpu.VMEM, outs[: len(outs) - far_outs])
        + spaced(pltpu.HBM, outs[len(outs) - far_outs :]),
        scratch_shapes=list(scratch),
        compiler_params=pltpu.CompilerParams(vmem_limit_bytes=limit),
        cost_estimate=pl.CostEstimate(
            flops=int(flops), bytes_accessed=int(moved), transcendentals=0
        ),
    )(place, *operands)


def reversed_bits(value, bits):
    out = 0
    for bit in range(bits):
        out = out | (((value >> bit) & 1) << (bits - 1 - bit))
    return out


def away(core, slot, bits):
    return jnp.where(core == 0, reversed_bits(slot, bits), slot)


def bits_of(size):
    return size.bit_length() - 1


def line_side(place_ref, lines):
    line = place_ref[0] // PLANE
    return jnp.where(place_ref[1] == 0, line & 1, line // (lines // 2))


def bias_rows(value):
    top = value.astype(BF16).astype(F32)
    row_at = lax.broadcasted_iota(I32, (TILE, value.shape[1]), 0)
    return jnp.where(row_at == 0, top, jnp.where(row_at == 1, value - top, 0.0)).astype(BF16)


def stacked(parts, target, sem, first=0):
    copies, at = [], 0
    for index, part in enumerate(parts):
        span = pl.ds(at, part.shape[0])
        copies.append(pltpu.make_async_copy(part, target.at[span, :], sem.at[first + index]))
        at += part.shape[0]
    return copies


def line_copies(parts, target, sem):
    own, parts = parts[0], parts[1:]
    mine, other = parts[: len(parts) // 2], parts[len(parts) // 2 :]
    rows, bits = own.shape[0], len(mine)
    half = rows // 2
    copies = [pltpu.make_async_copy(own, target.at[pl.ds(0, rows), :], sem.at[0])]
    for slot in range(1, 1 << bits):
        for index, (stages, at) in enumerate(((mine, slot), (other, reversed_bits(slot, bits)))):
            stage = at.bit_length() - 1
            view = stages[stage].at[pl.ds((at - (1 << stage)) * half, half), :]
            spot = target.at[pl.ds(slot * rows + index * half, half), :]
            copies.append(pltpu.make_async_copy(view, spot, sem.at[2 * slot - 1 + index]))
    return copies


def start_all(copies):
    for copy in copies:
        copy.start()


def wait_all(copies):
    for copy in copies:
        copy.wait()


def sort_slots(place, neighbours, present, importance, count):
    rows, slots = neighbours.shape
    turns = -(-slots // count)
    arrays = [neighbours.T, present.T, importance.T]

    def kernel(place_ref, *refs):
        out_ref, neighbours_ref, present_ref, importance_ref, sem = refs[3:]
        copies = [
            pltpu.make_async_copy(part, target, sem.at[index])
            for index, (part, target) in enumerate(zip(refs[:3], refs[4:7]))
        ]
        start_all(copies)
        wait_all(copies)
        slot_at = lax.broadcasted_iota(I32, (slots, rows), 0)
        node_at = lax.broadcasted_iota(I32, (slots, rows), 1)
        block = (node_at * slots + slot_at) & (count - 1)
        row = neighbours_ref[...] - rows * block
        packed = row * 128 + present_ref[...] * importance_ref[...]
        block_at = lax.broadcasted_iota(I32, (count, rows), 0)
        node_at = lax.broadcasted_iota(I32, (count, rows), 1)
        first = (block_at - slots * node_at) & (count - 1)
        for turn in range(turns):
            total = jnp.zeros((count, rows), I32)
            for slot in range(slots):
                at = slot - count * turn
                if 0 <= at < count:
                    total = jnp.where(first == at, packed[slot : slot + 1, :], total)
            out_ref[turn * count : (turn + 1) * count, :] = total

    (out,) = call(
        kernel, "sort_slots", [array((turns * count, rows), I32)], place, [], arrays,
        [pltpu.VMEM((slots, rows), I32)] * 3 + [pltpu.SemaphoreType.DMA((3,))], limit=ALL_VMEM,
    )
    return out


def slot_matrix(place, lists, count):
    tall, rows = lists[0].shape
    lines, width, turns = count // PLANE, PLANE * rows, tall // count

    def kernel(place_ref, own_ref, next_ref, rest_ref, sums_ref, far_ref, out_ref, sem):
        slot_refs = [(own_ref, 0), (next_ref, 0), (rest_ref, 0), (rest_ref, tall)]
        core, spot, line = place_ref[1], place_ref[0] % PLANE, place_ref[0] // PLANE
        sums = [
            jnp.sum((ref[at : at + tall, :] & 127).astype(F32), axis=0, keepdims=True)
            for ref, at in slot_refs
        ]
        sums = jnp.broadcast_to(jnp.concatenate(sums, axis=1), (8, width))
        sums_ref[...] = sums.T
        for at in range(lines):
            block = (line ^ away(core, at, bits_of(lines))) * PLANE + spot
            ids, weights = [], []
            for turn in range(turns):
                listed = jnp.concatenate(
                    [ref[pl.ds(at + turn * count + block, 1), :] for ref, at in slot_refs],
                    axis=1,
                )
                ids.append(((listed >> 7) - rows // 2).astype(F32).astype(BF16))
                weights.append((listed & 127).astype(F32).astype(BF16))
            shift = core * (rows // 2) if at else 0

            @pl.loop(0, rows // TILE)
            def _(step):
                base = step * TILE + shift
                base = jnp.where(base >= rows, base - rows, base)
                row_at = lax.broadcasted_iota(I32, (TILE, width), 0) + (base - rows // 2)
                row_at = row_at.astype(F32).astype(BF16)
                zero = jnp.zeros((TILE, width), BF16)
                total = zero
                for listed, weight in zip(ids, weights):
                    total = total + jnp.where(listed == row_at, weight, zero)
                out_ref[aligned(at * rows + step * TILE, TILE), :] = total

            span = pl.ds(at * rows, rows)
            pltpu.make_async_copy(out_ref.at[span, :], far_ref.at[span, :], sem.at[at]).start()
        for at in range(lines):
            span = pl.ds(at * rows, rows)
            pltpu.make_async_copy(out_ref.at[span, :], far_ref.at[span, :], sem.at[at]).wait()

    sums, matrix = call(
        kernel, "slot_matrix", [array((width, 8), F32), array((lines * rows, width), BF16)],
        place, lists,
        scratch=[pltpu.VMEM((lines * rows, width), BF16), pltpu.SemaphoreType.DMA((lines,))],
        flops=3 * turns * lines * rows * width, far_outs=1, limit=ALL_VMEM, light=True,
    )
    return matrix, sums


def half_copy(core, q_in, q_ref, sem):
    half = q_ref.shape[1]
    return pltpu.make_async_copy(q_in.at[:, aligned(core * half, half)], q_ref, sem)


def hidden_of(core, rows, q_ref, bias_ref):
    half = q_ref.shape[1]
    bias = bias_ref[:, aligned(core * half, half)]
    hidden = jnp.maximum(jnp.dot(rows, q_ref[...], preferred_element_type=F32) + bias, 0.0)
    top = hidden.astype(BF16)
    return top, (hidden - top.astype(F32)).astype(BF16)


def lane_span(start, size):
    low = start // 128 * 128
    high = -(-(start + size) // 128) * 128
    return low, high - low, start - low


def first_sums(place, line_parts, q_weight, q_bias, matrix):
    rows, dim = line_parts[0].shape
    total, width = matrix.shape
    half, part, count = dim // 2, width // PLANE, len(line_parts)
    lines = total // rows
    low, span_width, skip = lane_span(width - part, part)

    def kernel(place_ref, bias_ref, q_in, matrix_in, *refs):
        parts, refs = refs[:count], refs[count:]
        send_ref, high_out, low_out, rows_ref, high_ref, low_ref, matrix_ref, q_ref = refs[:8]
        row_sem, sem = refs[8:]
        core = place_ref[1]
        q_copy = half_copy(core, q_in, q_ref, sem.at[0])
        matrix_copy = pltpu.make_async_copy(
            matrix_in.at[:, pl.ds(low, span_width)], matrix_ref, sem.at[1]
        )
        copies = line_copies(parts, rows_ref, row_sem)
        start_all([q_copy] + copies + [matrix_copy])
        q_copy.wait()
        for at in range(lines):
            wait_all(copies[max(2 * at - 1, 0) : 2 * at + 1])
            span = slice(at * rows, (at + 1) * rows)
            high_ref[span, :], low_ref[span, :] = hidden_of(
                core, rows_ref[span, :], q_ref, bias_ref
            )
        outs = [
            pltpu.make_async_copy(high_ref, high_out, sem.at[2]),
            pltpu.make_async_copy(low_ref, low_out, sem.at[3]),
        ]
        start_all(outs)
        matrix_copy.wait()
        total_sum = across(matrix_ref[...], high_ref[...]) + across(matrix_ref[...], low_ref[...])
        send_ref[...] = total_sum[skip : skip + part, :]
        wait_all(outs)

    return call(
        kernel, "first_sums",
        [array((part, half), F32)] + [array((total, half), BF16)] * 2,
        place, [q_bias], [q_weight, matrix] + list(line_parts),
        [
            pltpu.VMEM((total, dim), BF16),
            pltpu.VMEM((total, half), BF16),
            pltpu.VMEM((total, half), BF16),
            pltpu.VMEM((total, span_width), BF16),
            pltpu.VMEM((dim, half), BF16),
            pltpu.SemaphoreType.DMA((2 * lines - 1,)),
            pltpu.SemaphoreType.DMA((4,)),
        ],
        flops=2 * total * dim * half + 4 * total * part * half, far_outs=2, limit=ALL_VMEM,
    )


def more_sums(place, highs, lows, matrix, first, slots):
    total = matrix.shape[0]
    part = matrix.shape[1] // PLANE
    width = slots * part
    start, span_width, skip = lane_span(first * part, width)
    half, count = highs[0].shape[1], len(highs)

    def kernel(place_ref, matrix_in, *refs):
        parts, refs = refs[: 2 * count], refs[2 * count :]
        sum_refs, refs = refs[:slots], refs[slots:]
        high_ref, low_ref, matrix_ref, sem = refs
        copies = [
            pltpu.make_async_copy(
                matrix_in.at[:, pl.ds(start, span_width)], matrix_ref, sem.at[2 * count]
            )
        ]
        copies += stacked(parts[:count], high_ref, sem)
        copies += stacked(parts[count:], low_ref, sem, count)
        start_all(copies)
        wait_all(copies)
        total_sum = across(matrix_ref[...], high_ref[...]) + across(matrix_ref[...], low_ref[...])
        for slot, sum_ref in enumerate(sum_refs):
            at = skip + slot * part
            sum_ref[...] = total_sum[at : at + part, :]

    return call(
        kernel, "more_sums", [array((part, half), F32)] * slots, place, [],
        [matrix] + list(highs) + list(lows),
        [
            pltpu.VMEM((total, half), BF16),
            pltpu.VMEM((total, half), BF16),
            pltpu.VMEM((total, span_width), BF16),
            pltpu.SemaphoreType.DMA((2 * count + 1,)),
        ],
        flops=4 * total * width * half, limit=ALL_VMEM,
    )


def pick_copy(core, first, second, target, sem, rows=None):
    views = [ref if rows is None else ref.at[rows, :] for ref in (first, second)]
    for side, view in enumerate(views):

        @pl.when(core == side)
        def _():
            pltpu.make_async_copy(view, target, sem).start()

    return pltpu.make_async_copy(views[0], target, sem)


def self_product(place, features, w_weight, w_other, w_bias):
    rows, dim = features.shape

    def kernel(place_ref, features_ref, bias_ref, w_in, w_other_in, out_ref, w_ref, sem):
        pick_copy(place_ref[1], w_in, w_other_in, w_ref, sem).wait()
        out_ref[...] = bias_ref[...] + jnp.dot(
            features_ref[...], w_ref[...], preferred_element_type=F32
        )

    (out,) = call(
        kernel, "self_product", [array((rows, dim), F32)], place, [features, w_bias],
        [w_weight, w_other], [pltpu.VMEM((dim, dim), BF16), pltpu.SemaphoreType.DMA(())],
        flops=2 * rows * dim * dim,
    )
    return out


def row_sums(place, stay, late, come):
    rows, half = late.shape

    def kernel(place_ref, stay_ref, late_ref, come_ref, out_ref):
        for part in range(2):
            span = slice(part * rows // 2, (part + 1) * rows // 2)
            came = late_ref[span, :].astype(F32) + come_ref[span, :].astype(F32)
            at = aligned((place_ref[1] ^ part) * (rows // 2), rows // 2)
            out_ref[at, :] = (stay_ref[at, :].astype(F32) + came).astype(BF16)

    (out,) = call(kernel, "row_sums", [array((rows, half), BF16)], place, [stay, late, come])
    return out


def feature_step(place, grad_linear, mine, other, w_weight, w_other, q_weight):
    rows, dim = grad_linear.shape
    half = dim // 2

    def kernel(
        place_ref, grad_ref, mine_ref, other_ref, w_in, w_other_in, q_in, out_ref, w_ref, q_ref, sem
    ):
        core = place_ref[1]
        span = aligned(core * half, half)
        q_copy = pltpu.make_async_copy(q_in.at[span, :], q_ref, sem.at[1])
        q_copy.start()
        pick_copy(core, w_in, w_other_in, w_ref, sem.at[0], span).wait()
        total = times_t(grad_ref[...], w_ref[...])
        q_copy.wait()
        total += times_t(mine_ref[...], q_ref[:, span])
        out_ref[...] = total + times_t(other_ref[...], q_ref[:, aligned((1 - core) * half, half)])

    (out,) = call(
        kernel, "feature_step", [array((rows, half), F32)], place, [grad_linear, mine, other],
        [w_weight, w_other, q_weight],
        [pltpu.VMEM((half, dim), BF16)] * 2 + [pltpu.SemaphoreType.DMA((2,))],
        flops=4 * rows * dim * half,
    )
    return out


def plane_slices(place, features, mine, other):
    rows, dim = features.shape
    half, width = dim // 2, dim // PLANE

    def kernel(place_ref, features_ref, mine_ref, other_ref, own_ref, next_ref, send_ref):
        core, spot = place_ref[1], place_ref[0] % PLANE
        targets = [own_ref, next_ref, send_ref.at[pl.ds(0, rows), :], send_ref.at[pl.ds(rows, rows), :]]
        for slot, target in enumerate(targets):
            to = spot ^ away(core, slot, 2)

            @pl.when(core == 0)
            def _():
                target[...] = features_ref[:, aligned(to * width, width)]

            within = aligned(to % 2 * width, width)

            @pl.when((core == 1) & (to < 2))
            def _():
                target[...] = other_ref[:, within]

            @pl.when((core == 1) & (to >= 2))
            def _():
                target[...] = mine_ref[:, within]

    outs = [array((rows, width), BF16)] * 2 + [array((2 * rows, width), BF16)]
    return call(kernel, "plane_slices", outs, place, [features, mine, other])


def node_step(place, mine, other, self_part, cotangent, w_weight, w_other):
    rows, half = mine.shape
    dim = 2 * half

    def kernel(
        place_ref, mine_ref, other_ref, self_ref, cotangent_ref, w_in, w_other_in,
        embeddings_ref, grad_ref, half_ref, lhs_ref, linear_ref, near_ref, sem,
    ):
        core = place_ref[1]
        near_copy = pick_copy(core, w_other_in, w_in, near_ref, sem)
        lhs_ref[:, aligned(core * half, half)] = mine_ref[...]
        lhs_ref[:, aligned((1 - core) * half, half)] = other_ref[...]
        near_copy.wait()
        linear_ref[...] = self_ref[...] + jnp.dot(
            lhs_ref[...], near_ref[...], preferred_element_type=F32
        )

        @pl.loop(0, rows // TILE, unroll=4)
        def _(step):
            at = aligned(step * TILE, TILE)
            linear = linear_ref[at, :]
            relu_out = jnp.maximum(linear, 0.0)
            scale = lax.rsqrt(jnp.mean(relu_out * relu_out, axis=1, keepdims=True) + 1e-06)
            embeddings_ref[at, :] = relu_out * scale
            grad_out = cotangent_ref[at, :].astype(F32)
            inner = jnp.mean(relu_out * grad_out, axis=1, keepdims=True)
            grad_relu = scale * grad_out - relu_out * (scale * scale * scale) * inner
            grad_ref[at, :] = jnp.where(linear > 0, grad_relu, 0.0).astype(BF16)

        half_ref[...] = grad_ref[aligned(core * (rows // 2), rows // 2), :]

    outs = [
        array((rows, dim), F32), array((rows, dim), BF16), array((rows // 2, dim), BF16),
    ]
    return call(
        kernel, "node_step", outs, place, [mine, other, self_part, cotangent],
        [w_weight, w_other],
        [
            pltpu.VMEM((rows, dim), BF16), pltpu.VMEM((rows, dim), F32),
            pltpu.VMEM((dim, dim), BF16), pltpu.SemaphoreType.DMA(()),
        ],
        flops=2 * rows * dim * dim,
    )


def plane_copies(core, rows, pieces, target, sem):
    own = pieces[0]
    half = rows // 2
    copies = [pltpu.make_async_copy(own, target.at[pl.ds(0, rows), :], sem.at[0])]
    for slot in range(1, PLANE):
        mine = pieces[slot]
        other = pieces[PLANE - 1 + reversed_bits(slot, 2)]
        for index, (part, at) in enumerate(((mine, core), (other, 1 - core))):
            spot = pl.multiple_of(slot * rows + at * half, TILE)
            copies.append(
                pltpu.make_async_copy(
                    part, target.at[pl.ds(spot, half), :], sem.at[2 * slot - 1 + index]
                )
            )
    return copies


def self_weight(place, pieces, slices, lines):
    rows, dim = pieces[0].shape
    width = slices[0].shape[1]

    def kernel(place_ref, *refs):
        parts, refs = refs[:PIECES], refs[PIECES:]
        slots, outs = refs[:4], refs[4:6]
        grads_ref, lhs_ref, sum_ref, sem, slice_sem = refs[6:]
        copies = plane_copies(place_ref[1], rows, parts, grads_ref, sem)
        own, far, near, last = slots
        spans = [own, last.at[pl.ds(0, rows), :], far.at[pl.ds(0, rows), :], last.at[pl.ds(rows, rows), :]]
        for slot, part in enumerate(spans):
            copies.append(
                pltpu.make_async_copy(part, lhs_ref.at[pl.ds(slot * rows, rows), :], slice_sem.at[slot])
            )
        for copy in copies:
            copy.start()
        for copy in copies:
            copy.wait()
        sum_ref[...] = across(lhs_ref[...], grads_ref[...])
        bias = bias_rows(jnp.sum(grads_ref[...].astype(F32), axis=0, keepdims=True))
        first = line_side(place_ref, lines)
        for slot, out_ref in enumerate(outs):
            out_ref[: width // 2, :] = sum_ref[
                aligned((first ^ slot) * (width // 2), width // 2), :
            ].astype(BF16)
            out_ref[width // 2 :, :] = bias

    return call(
        kernel, "self_weight", [array((width // 2 + TILE, dim), BF16)] * 2, place, [],
        list(pieces) + list(slices),
        [
            pltpu.VMEM((PLANE * rows, dim), BF16),
            pltpu.VMEM((PLANE * rows, width), BF16),
            pltpu.VMEM((width, dim), F32),
            pltpu.SemaphoreType.DMA((PIECES,)),
            pltpu.SemaphoreType.DMA((PLANE,)),
        ],
        flops=2 * PLANE * rows * dim * width,
    )


def row_grad(place, sums, pieces, w_weight, w_other, matrix, high, line_parts, lines):
    rows, dim = pieces[0].shape
    half = dim // 2
    total, nodes, width = lines * rows, PLANE * rows, dim // PLANE

    def kernel(place_ref, sums_ref, matrix_in, high_in, w_in, w_other_in, *refs):
        parts, refs = refs[:PIECES], refs[PIECES:]
        row_parts, refs = refs[: len(line_parts)], refs[len(line_parts) :]
        stay_ref, late_ref, go_ref, keep_ref, send_ref, refs = *refs[:5], refs[5:]
        grads_ref, rows_ref, sum_ref, hidden_ref, near_ref, matrix_ref, high_ref = refs[:7]
        sem, row_sem, near_sem, line_sem = refs[7:]
        core, spot = place_ref[1], place_ref[0] % PLANE
        copies = plane_copies(core, rows, parts, grads_ref, sem)
        row_copies = line_copies(row_parts, rows_ref, row_sem)
        near_copy = pick_copy(
            core, w_other_in, w_in, near_ref, near_sem, aligned(core * half, half)
        )
        line_sums = [
            pltpu.make_async_copy(matrix_in, matrix_ref, line_sem.at[0]),
            pltpu.make_async_copy(high_in, high_ref, line_sem.at[1]),
        ]
        start_all(copies + line_sums + row_copies)
        near_copy.wait()
        for slot in range(PLANE):
            wait_all(copies[max(2 * slot - 1, 0) : 2 * slot + 1])
            span = slice(slot * rows, (slot + 1) * rows)
            grad = times_t(grads_ref[span, :], near_ref[...])
            sum_ref[span, :] = (grad / sums_ref[span, 0:1]).astype(BF16)
        wait_all(line_sums)
        bias = jnp.zeros((1, half), F32)
        for at in range(lines):
            span = slice(at * rows, (at + 1) * rows)
            grad = jnp.dot(matrix_ref[span, :], sum_ref[...], preferred_element_type=F32)
            grad = jnp.where(high_ref[span, :].astype(F32) > 0, grad, 0.0)
            bias = bias + jnp.sum(grad, axis=0, keepdims=True)
            hidden_ref[span, :] = grad.astype(BF16)
        for slot in range(lines):
            at = to = slot * rows
            for ref in (stay_ref, late_ref, go_ref):
                if 0 <= to < ref.shape[0]:
                    break
                to -= ref.shape[0]
            ref[to : to + rows, :] = hidden_ref[at : at + rows, :]
        wait_all(row_copies)
        for slot in range(PLANE):
            to = spot ^ away(core, slot, 2)
            ref, at = (keep_ref, send_ref)[slot // 2], slot % 2 * width
            ref[at : at + width, :] = across(
                rows_ref[:, aligned(to * width, width)], hidden_ref[...]
            ).astype(BF16)
        for ref in (keep_ref, send_ref):
            ref[2 * width :, :] = bias_rows(bias)

    outs = [array((total // 2, half), BF16)] + [array((total // 4, half), BF16)] * 2
    outs += [array((dim // 2 + TILE, half), BF16)] * 2
    return call(
        kernel, "row_grad", outs, place, [sums],
        [matrix, high, w_weight, w_other] + list(pieces) + list(line_parts),
        [
            pltpu.VMEM((nodes, dim), BF16),
            pltpu.VMEM((total, dim), BF16),
            pltpu.VMEM((nodes, half), BF16),
            pltpu.VMEM((total, half), BF16),
            pltpu.VMEM((half, dim), BF16),
            pltpu.VMEM((total, nodes), BF16),
            pltpu.VMEM((total, half), BF16),
            pltpu.SemaphoreType.DMA((PIECES,)),
            pltpu.SemaphoreType.DMA((2 * lines - 1,)),
            pltpu.SemaphoreType.DMA(()),
            pltpu.SemaphoreType.DMA((2,)),
        ],
        flops=2 * nodes * dim * half + 2 * total * nodes * half + 2 * total * dim * half,
        limit=VMEM_BYTES if lines <= PLANE else ALL_VMEM,
    )


def fold(place, keep, came):
    height, width = keep.shape[0] - TILE, keep.shape[1]
    part = height // 2

    def kernel(place_ref, keep_ref, came_ref, stay_ref, go_ref):
        bias = keep_ref[height:, :].astype(F32) + came_ref[height:, :].astype(F32)
        bias = bias_rows(bias[0:1] + bias[1:2])
        for ref, at in ((stay_ref, 0), (go_ref, part)):
            span = slice(at, at + part)
            ref[:part, :] = (keep_ref[span, :].astype(F32) + came_ref[span, :].astype(F32)).astype(BF16)
            ref[part:, :] = bias

    return call(
        kernel, "fold", [array((part + TILE, width), BF16)] * 2, place, [keep, came]
    )


def merge(place, keep, came):
    height, width = keep.shape[0] - TILE, keep.shape[1]

    def kernel(place_ref, keep_ref, came_ref, out_ref):
        out_ref[...] = (keep_ref[...].astype(F32) + came_ref[...].astype(F32)).astype(BF16)
        bias = keep_ref[height:, :].astype(F32) + came_ref[height:, :].astype(F32)
        out_ref[height:, :] = bias_rows(bias[0:1] + bias[1:2])

    (out,) = call(kernel, "merge", [array(keep.shape, BF16)], place, [keep, came])
    return out


def unpack(place, sides, lines=0):
    parts = 2 if lines else 1
    height, width = sides[0][0].shape
    blocks = [block for side in sides for block in side]
    count = len(blocks)

    def kernel(place_ref, *refs):
        sources, (out_ref, block_ref, wide_ref, sem, out_sem) = refs[:count], refs[count:]
        spot = place_ref[0] % PLANE
        copies = [
            pltpu.make_async_copy(source, block_ref.at[index], sem.at[index])
            for index, source in enumerate(sources)
        ]
        start_all(copies)
        outs = []
        for index, copy in enumerate(copies):
            side, slot, at = index // (PLANE * parts), index // parts % PLANE, index % parts
            core = place_ref[1] ^ side
            row = (spot ^ away(core, slot, 2)) * parts
            if lines:
                row = row + (line_side(place_ref, lines) ^ at)
            cols = aligned(core * width, width) if len(sides) > 1 else pl.ds(0, width)
            copy.wait()
            wide_ref[index] = block_ref[index].astype(F32)
            outs.append(
                pltpu.make_async_copy(
                    wide_ref.at[index], out_ref.at[aligned(row * height, height), cols],
                    out_sem.at[index],
                )
            )
            outs[-1].start()
        wait_all(outs)

    (out,) = call(
        kernel, "unpack", [array((PLANE * parts * height, width * len(sides)), F32)], place, [],
        blocks,
        [
            pltpu.VMEM((count, height, width), BF16), pltpu.VMEM((count, height, width), F32),
            pltpu.SemaphoreType.DMA((count,)), pltpu.SemaphoreType.DMA((count,)),
        ],
        far_outs=1,
    )
    return out


def on_device(
    features, neighbours, present, importance, q_weight, q_bias, w_weight, w_bias, cotangent
):
    rows, dim = features.shape
    count = lax.axis_size("nodes")
    lines = count // PLANE
    line_bits = bits_of(lines)
    node = lax.axis_index("nodes")
    core = lax.axis_index("stream")
    place = jnp.stack([node, core]).astype(I32)
    half_rows = rows // 2
    fence = lax.optimization_barrier

    def swap(value, bit, other_bit=None):
        bits = (bit, bit if other_bit is None else other_bit)
        pairs = [
            (2 * at + side, 2 * (at ^ bits[side]) + side) for at in range(count) for side in (0, 1)
        ]
        return lax.ppermute(value, ("nodes", "stream"), pairs)

    def plane_swap(value, step):
        return swap(value, 1 << step, 2 >> step)

    def line_swap(value, step):
        return swap(value, PLANE << step, PLANE << (line_bits - 1 - step))

    def trade(value):
        return lax.ppermute(value, "stream", [(0, 1), (1, 0)])

    def own_half(value, axis):
        size = value.shape[axis] // 2
        return lax.dynamic_slice_in_dim(value, core * size, size, axis)

    def joined(mine, other, axis):
        return jnp.where(
            core == 0,
            jnp.concatenate([mine, other], axis),
            jnp.concatenate([other, mine], axis),
        )

    mine = own_half(features, 0)
    stages = [line_swap(mine, line_bits - 1)]
    lists = sort_slots(place, neighbours, present, importance, count)
    lists = [jnp.concatenate([lists, trade(lists)], 0)]
    lists.append(plane_swap(lists[0], 1))
    lists[1], stages[0] = fence((lists[1], stages[0]))
    for step in reversed(range(line_bits - 1)):
        stages.append(line_swap(jnp.concatenate([mine] + stages, 0), step))
    lists.append(plane_swap(jnp.concatenate(lists, 0), 0))
    traded = [trade(stage) for stage in stages[:-1]]
    matrix, weight_sums = slot_matrix(place, lists, count)
    matrix, stages[-1] = fence((matrix, stages[-1]))
    line_parts = [features] + stages + traded + [trade(stages[-1])]
    send, high, low = first_sums(place, line_parts, q_weight, q_bias[None], matrix)
    send, w_sent = fence((send, w_weight))
    w_other = trade(w_sent)

    came = plane_swap(send, 0)
    keep, middle, own_send = more_sums(place, [high], [low], matrix, 0, 3)
    came_own = plane_swap(own_send, 0)
    last = plane_swap(middle + came, 1)
    came_own, w_other = fence((came_own, w_other))
    self_part = self_product(place, features, w_weight, w_other, w_bias[None])
    last, self_part, keep = fence((last, self_part, keep))
    mean_half = ((keep + came_own + last) / weight_sums[:rows, 0:1]).astype(BF16)

    mean_other = trade(mean_half)
    own_slice, next_slice, send_slices = plane_slices(place, features, mean_half, mean_other)
    far_slices = plane_swap(send_slices, 0)
    embeddings, grad_linear, grad_half = node_step(
        place, mean_half, mean_other, self_part, cotangent, w_weight, w_other
    )

    one, two = plane_swap(grad_half, 1), plane_swap(grad_half, 0)
    last_slices = plane_swap(jnp.concatenate([next_slice, far_slices[rows:]], 0), 1)
    one, two = fence((one, two))
    three = plane_swap(one, 0)
    three, last_slices = fence((three, last_slices))
    pieces = [grad_linear, one, two, three, trade(one), trade(two), trade(three)]
    slices = [own_slice, far_slices, next_slice, last_slices]
    w_keep, w_send = self_weight(place, pieces, slices, lines)
    pieces, w_keep, w_send = fence((pieces, w_keep, w_send))

    stay, late, go, q_keep, q_send = row_grad(
        place, weight_sums, pieces, w_weight, w_other, matrix, high, line_parts, lines
    )
    w_came = line_swap(w_send, 0)
    stay, late, go, q_keep, q_send, w_keep, w_came = fence(
        (stay, late, go, q_keep, q_send, w_keep, w_came)
    )

    def last_sum(keep, came):
        height = keep.shape[0] - TILE
        total = keep.astype(F32) + came.astype(F32)
        return total[:height].astype(BF16), total[height] + total[height + 1]

    biases = {}

    rows_go, rows_late = line_swap(go, 0), line_swap(late, 0)
    q_came = plane_swap(q_send, 0)
    w_sum = merge(place, w_keep, w_came)
    w_came = line_swap(w_sum, 1)
    q_came = fence(q_came)
    q_keep, q_send = fold(place, q_keep, q_came)
    q_came, w_came, stay, rows_go, rows_late = fence(
        (plane_swap(q_send, 1), w_came, stay, rows_go, rows_late)
    )
    for step in range(2, line_bits):
        w_sum = merge(place, w_sum, w_came)
        w_came = line_swap(w_sum, step)
    q_sum = merge(place, q_keep, q_came)
    q_came = line_swap(q_sum, 0)
    w_near, biases["w"] = last_sum(w_sum, w_came)
    w_far = line_swap(w_near, 0)
    near_one, near_two = plane_swap(w_near, 1), plane_swap(w_near, 0)
    q_came, w_far, near_one, near_two, biases = fence((q_came, w_far, near_one, near_two, biases))
    for step in range(1, line_bits):
        q_sum = merge(place, q_sum, q_came)
        q_came = line_swap(q_sum, step)
    near_three = plane_swap(near_one, 0)
    far_one, far_two = plane_swap(w_far, 1), plane_swap(w_far, 0)
    q_came, near_three, far_one, far_two = fence((q_came, near_three, far_one, far_two))
    q_own, biases["q"] = last_sum(q_sum, q_came)
    half = stay.shape[0] // 2
    upper = (stay[half:].astype(F32) + rows_go.astype(F32)).astype(BF16)
    q_own, upper = fence((q_own, upper))
    rows_next = line_swap(upper, 1)
    q_one, q_two = plane_swap(q_own, 1), plane_swap(q_own, 0)
    far_three = plane_swap(far_one, 0)
    q_one, q_two, far_three, rows_next, biases = fence((q_one, q_two, far_three, rows_next, biases))
    q_three = plane_swap(q_one, 0)
    w_all = [w_near, w_far, near_one, far_one, near_two, far_two, near_three, far_three]
    w_grad = unpack(place, [w_all], lines)
    w_bias_grad, q_bias_half = biases["w"], biases["q"]
    q_bias_grad = joined(q_bias_half, trade(q_bias_half), 0)

    stay = stay[: stay.shape[0] // 2]
    for step in range(2, line_bits):
        half = rows_late.shape[0] // 2
        upper = stay[half:].astype(F32) + rows_late[half:] + rows_next[half:]
        rows_next = (rows_next[:half] + line_swap(upper.astype(BF16), step).astype(F32)).astype(BF16)
        stay, rows_late = stay[:half], rows_late[:half]
    row_half = row_sums(place, stay, rows_late, rows_next)
    row_other = trade(row_half)
    q_mine = [q_own, q_one, q_two]
    q_other = [trade(block) for block in q_mine]
    q_three, q_other, w_grad, q_bias_grad, row_other = fence(
        (q_three, q_other, w_grad, q_bias_grad, row_other)
    )
    feature_grad = feature_step(
        place, grad_linear, row_half, row_other, w_weight, w_other, q_weight
    )
    q_grad = unpack(place, [q_mine + [q_three], q_other + [trade(q_three)]])
    return (embeddings, feature_grad, q_grad, q_bias_grad, w_grad, w_bias_grad)


def solution(mesh):
    in_specs = (
        P("nodes", None),
        P("nodes", "stream"),
        P("nodes", "stream"),
        P("nodes", "stream"),
        P(),
        P(),
        P("stream", None),
        P(),
        P("nodes", None),
    )
    out_specs = (P("nodes", None), P("nodes", "stream"), P(), P(), P("stream", None), P())
    return jax.shard_map(
        on_device, mesh=mesh, in_specs=in_specs, out_specs=out_specs, check_vma=False
    )
```

```python
import jax
import jax.numpy as jnp
from jax import lax
from jax.experimental import pallas as pl
from jax.experimental.pallas import tpu as pltpu
from jax.sharding import PartitionSpec as P

PLANE = 4
TILE = 16
PIECES = 2 * PLANE - 1
VMEM_BYTES = 48 * 1024 * 1024
ALL_VMEM = 67_000_000
F32, BF16, I32 = jnp.float32, jnp.bfloat16, jnp.int32


def across(lhs, rhs):
    return lax.dot_general(lhs, rhs, (((0,), (0,)), ((), ())), preferred_element_type=F32)


def times_t(lhs, rhs):
    return lax.dot_general(lhs, rhs, (((1,), (1,)), ((), ())), preferred_element_type=F32)


def aligned(start, size):
    start = start if isinstance(start, int) else pl.multiple_of(start, size)
    return pl.ds(start, size)


def spaced(space, arrays):
    return [pl.BlockSpec(memory_space=space) for _ in arrays]


def array(shape, dtype):
    return jax.ShapeDtypeStruct(shape, dtype)


def call(kernel, name, outs, place, near, far=(), scratch=(), flops=0, far_outs=0,
         limit=VMEM_BYTES, light=False, aliases={}):
    operands = list(near) + list(far)
    moved = sum(a.size * a.dtype.itemsize for a in operands + list(outs))
    if light:
        flops, moved = 1, 1
    return pl.pallas_call(
        kernel,
        name=name,
        out_shape=list(outs),
        in_specs=spaced(pltpu.SMEM, [place]) + spaced(pltpu.VMEM, near) + spaced(pltpu.HBM, far),
        out_specs=spaced(pltpu.VMEM, outs[: len(outs) - far_outs])
        + spaced(pltpu.HBM, outs[len(outs) - far_outs :]),
        scratch_shapes=list(scratch),
        input_output_aliases=aliases,
        compiler_params=pltpu.CompilerParams(vmem_limit_bytes=limit),
        cost_estimate=pl.CostEstimate(
            flops=int(flops), bytes_accessed=int(moved), transcendentals=0
        ),
    )(place, *operands)


def reversed_bits(value, bits):
    out = 0
    for bit in range(bits):
        out = out | (((value >> bit) & 1) << (bits - 1 - bit))
    return out


def away(core, slot, bits):
    return jnp.where(core == 0, reversed_bits(slot, bits), slot)


def bits_of(size):
    return size.bit_length() - 1


def line_side(place_ref, lines):
    line = place_ref[0] // PLANE
    return jnp.where(place_ref[1] == 0, line & 1, line // (lines // 2))


def bias_rows(value):
    top = value.astype(BF16).astype(F32)
    row_at = lax.broadcasted_iota(I32, (TILE, value.shape[1]), 0)
    return jnp.where(row_at == 0, top, jnp.where(row_at == 1, value - top, 0.0)).astype(BF16)


def stacked(parts, target, sem, first=0):
    copies, at = [], 0
    for index, part in enumerate(parts):
        span = pl.ds(at, part.shape[0])
        copies.append(pltpu.make_async_copy(part, target.at[span, :], sem.at[first + index]))
        at += part.shape[0]
    return copies


def line_copies(parts, target, sem):
    own, parts = parts[0], parts[1:]
    mine, other = parts[: len(parts) // 2], parts[len(parts) // 2 :]
    rows, bits = own.shape[0], len(mine)
    half = rows // 2
    copies = [pltpu.make_async_copy(own, target.at[pl.ds(0, rows), :], sem.at[0])]
    for slot in range(1, 1 << bits):
        for index, (stages, at) in enumerate(((mine, slot), (other, reversed_bits(slot, bits)))):
            stage = at.bit_length() - 1
            view = stages[stage].at[pl.ds((at - (1 << stage)) * half, half), :]
            spot = target.at[pl.ds(slot * rows + index * half, half), :]
            copies.append(pltpu.make_async_copy(view, spot, sem.at[2 * slot - 1 + index]))
    return copies


def start_all(copies):
    for copy in copies:
        copy.start()


def wait_all(copies):
    for copy in copies:
        copy.wait()


def sort_slots(place, neighbours, present, importance, count):
    rows, slots = neighbours.shape
    turns = -(-slots // count)
    arrays = [neighbours.T, present.T, importance.T]

    def kernel(place_ref, *refs):
        out_ref, neighbours_ref, present_ref, importance_ref, sem = refs[3:]
        copies = [
            pltpu.make_async_copy(part, target, sem.at[index])
            for index, (part, target) in enumerate(zip(refs[:3], refs[4:7]))
        ]
        start_all(copies)
        wait_all(copies)
        slot_at = lax.broadcasted_iota(I32, (slots, rows), 0)
        node_at = lax.broadcasted_iota(I32, (slots, rows), 1)
        block = (node_at * slots + slot_at) & (count - 1)
        row = neighbours_ref[...] - rows * block
        packed = row * 128 + present_ref[...] * importance_ref[...]
        block_at = lax.broadcasted_iota(I32, (count, rows), 0)
        node_at = lax.broadcasted_iota(I32, (count, rows), 1)
        first = (block_at - slots * node_at) & (count - 1)
        for turn in range(turns):
            total = jnp.zeros((count, rows), I32)
            for slot in range(slots):
                at = slot - count * turn
                if 0 <= at < count:
                    total = jnp.where(first == at, packed[slot : slot + 1, :], total)
            out_ref[turn * count : (turn + 1) * count, :] = total

    (out,) = call(
        kernel, "sort_slots", [array((turns * count, rows), I32)], place, [], arrays,
        [pltpu.VMEM((slots, rows), I32)] * 3 + [pltpu.SemaphoreType.DMA((3,))], limit=ALL_VMEM,
    )
    return out


def slot_matrix(place, lists, count):
    tall, rows = lists[0].shape
    lines, width, turns = count // PLANE, PLANE * rows, tall // count

    def kernel(place_ref, own_ref, next_ref, rest_ref, sums_ref, far_ref, out_ref, sem):
        slot_refs = [(own_ref, 0), (next_ref, 0), (rest_ref, 0), (rest_ref, tall)]
        core, spot, line = place_ref[1], place_ref[0] % PLANE, place_ref[0] // PLANE
        sums = [
            jnp.sum((ref[at : at + tall, :] & 127).astype(F32), axis=0, keepdims=True)
            for ref, at in slot_refs
        ]
        sums = jnp.broadcast_to(jnp.concatenate(sums, axis=1), (8, width))
        sums_ref[...] = sums.T
        for at in range(lines):
            block = (line ^ away(core, at, bits_of(lines))) * PLANE + spot
            ids, weights = [], []
            for turn in range(turns):
                listed = jnp.concatenate(
                    [ref[pl.ds(at + turn * count + block, 1), :] for ref, at in slot_refs],
                    axis=1,
                )
                ids.append(((listed >> 7) - rows // 2).astype(F32).astype(BF16))
                weights.append((listed & 127).astype(F32).astype(BF16))
            shift = core * (rows // 2) if at else 0

            @pl.loop(0, rows // TILE)
            def _(step):
                base = step * TILE + shift
                base = jnp.where(base >= rows, base - rows, base)
                row_at = lax.broadcasted_iota(I32, (TILE, width), 0) + (base - rows // 2)
                row_at = row_at.astype(F32).astype(BF16)
                zero = jnp.zeros((TILE, width), BF16)
                total = zero
                for listed, weight in zip(ids, weights):
                    total = total + jnp.where(listed == row_at, weight, zero)
                out_ref[aligned(at * rows + step * TILE, TILE), :] = total

            span = pl.ds(at * rows, rows)
            pltpu.make_async_copy(out_ref.at[span, :], far_ref.at[span, :], sem.at[at]).start()
        for at in range(lines):
            span = pl.ds(at * rows, rows)
            pltpu.make_async_copy(out_ref.at[span, :], far_ref.at[span, :], sem.at[at]).wait()

    sums, matrix = call(
        kernel, "slot_matrix", [array((width, 8), F32), array((lines * rows, width), BF16)],
        place, lists,
        scratch=[pltpu.VMEM((lines * rows, width), BF16), pltpu.SemaphoreType.DMA((lines,))],
        flops=3 * turns * lines * rows * width, far_outs=1, limit=ALL_VMEM, light=True,
    )
    return matrix, sums


def half_copy(core, q_in, q_ref, sem):
    half = q_ref.shape[1]
    return pltpu.make_async_copy(q_in.at[:, aligned(core * half, half)], q_ref, sem)


def hidden_of(core, rows, q_ref, bias_ref):
    half = q_ref.shape[1]
    bias = bias_ref[:, aligned(core * half, half)]
    hidden = jnp.maximum(jnp.dot(rows, q_ref[...], preferred_element_type=F32) + bias, 0.0)
    top = hidden.astype(BF16)
    return top, (hidden - top.astype(F32)).astype(BF16)


def lane_span(start, size):
    low = start // 128 * 128
    high = -(-(start + size) // 128) * 128
    return low, high - low, start - low


def first_sums(place, line_parts, q_weight, q_bias, matrix):
    rows, dim = line_parts[0].shape
    total, width = matrix.shape
    half, part, count = dim // 2, width // PLANE, len(line_parts)
    lines = total // rows
    low, span_width, skip = lane_span(width - part, part)

    def kernel(place_ref, bias_ref, q_in, matrix_in, *refs):
        parts, refs = refs[:count], refs[count:]
        send_ref, high_out, low_out, rows_ref, high_ref, low_ref, matrix_ref, q_ref = refs[:8]
        row_sem, sem = refs[8:]
        core = place_ref[1]
        q_copy = half_copy(core, q_in, q_ref, sem.at[0])
        matrix_copy = pltpu.make_async_copy(
            matrix_in.at[:, pl.ds(low, span_width)], matrix_ref, sem.at[1]
        )
        copies = line_copies(parts, rows_ref, row_sem)
        start_all([q_copy] + copies + [matrix_copy])
        q_copy.wait()
        for at in range(lines):
            wait_all(copies[max(2 * at - 1, 0) : 2 * at + 1])
            span = slice(at * rows, (at + 1) * rows)
            high_ref[span, :], low_ref[span, :] = hidden_of(
                core, rows_ref[span, :], q_ref, bias_ref
            )
        outs = [
            pltpu.make_async_copy(high_ref, high_out, sem.at[2]),
            pltpu.make_async_copy(low_ref, low_out, sem.at[3]),
        ]
        start_all(outs)
        matrix_copy.wait()
        total_sum = across(matrix_ref[...], high_ref[...]) + across(matrix_ref[...], low_ref[...])
        send_ref[...] = total_sum[skip : skip + part, :]
        wait_all(outs)

    return call(
        kernel, "first_sums",
        [array((part, half), F32)] + [array((total, half), BF16)] * 2,
        place, [q_bias], [q_weight, matrix] + list(line_parts),
        [
            pltpu.VMEM((total, dim), BF16),
            pltpu.VMEM((total, half), BF16),
            pltpu.VMEM((total, half), BF16),
            pltpu.VMEM((total, span_width), BF16),
            pltpu.VMEM((dim, half), BF16),
            pltpu.SemaphoreType.DMA((2 * lines - 1,)),
            pltpu.SemaphoreType.DMA((4,)),
        ],
        flops=2 * total * dim * half + 4 * total * part * half, far_outs=2, limit=ALL_VMEM,
    )


def more_sums(place, highs, lows, matrix, first, slots):
    total = matrix.shape[0]
    part = matrix.shape[1] // PLANE
    width = slots * part
    start, span_width, skip = lane_span(first * part, width)
    half, count = highs[0].shape[1], len(highs)

    def kernel(place_ref, matrix_in, *refs):
        parts, refs = refs[: 2 * count], refs[2 * count :]
        sum_refs, refs = refs[:slots], refs[slots:]
        high_ref, low_ref, matrix_ref, sem = refs
        copies = [
            pltpu.make_async_copy(
                matrix_in.at[:, pl.ds(start, span_width)], matrix_ref, sem.at[2 * count]
            )
        ]
        copies += stacked(parts[:count], high_ref, sem)
        copies += stacked(parts[count:], low_ref, sem, count)
        start_all(copies)
        wait_all(copies)
        total_sum = across(matrix_ref[...], high_ref[...]) + across(matrix_ref[...], low_ref[...])
        for slot, sum_ref in enumerate(sum_refs):
            at = skip + slot * part
            sum_ref[...] = total_sum[at : at + part, :]

    return call(
        kernel, "more_sums", [array((part, half), F32)] * slots, place, [],
        [matrix] + list(highs) + list(lows),
        [
            pltpu.VMEM((total, half), BF16),
            pltpu.VMEM((total, half), BF16),
            pltpu.VMEM((total, span_width), BF16),
            pltpu.SemaphoreType.DMA((2 * count + 1,)),
        ],
        flops=4 * total * width * half, limit=ALL_VMEM,
    )


def pick_copy(core, first, second, target, sem, rows=None):
    views = [ref if rows is None else ref.at[rows, :] for ref in (first, second)]
    for side, view in enumerate(views):

        @pl.when(core == side)
        def _():
            pltpu.make_async_copy(view, target, sem).start()

    return pltpu.make_async_copy(views[0], target, sem)


def self_product(place, features, w_weight, w_other, w_bias):
    rows, dim = features.shape

    def kernel(place_ref, features_ref, bias_ref, w_in, w_other_in, out_ref, w_ref, sem):
        pick_copy(place_ref[1], w_in, w_other_in, w_ref, sem).wait()
        out_ref[...] = bias_ref[...] + jnp.dot(
            features_ref[...], w_ref[...], preferred_element_type=F32
        )

    (out,) = call(
        kernel, "self_product", [array((rows, dim), F32)], place, [features, w_bias],
        [w_weight, w_other], [pltpu.VMEM((dim, dim), BF16), pltpu.SemaphoreType.DMA(())],
        flops=2 * rows * dim * dim,
    )
    return out


def row_sums(place, stay, late, come):
    rows, half = late.shape

    def kernel(place_ref, stay_ref, late_ref, come_ref, out_ref):
        for part in range(2):
            span = slice(part * rows // 2, (part + 1) * rows // 2)
            came = late_ref[span, :].astype(F32) + come_ref[span, :].astype(F32)
            at = aligned((place_ref[1] ^ part) * (rows // 2), rows // 2)
            out_ref[at, :] = (stay_ref[at, :].astype(F32) + came).astype(BF16)

    (out,) = call(kernel, "row_sums", [array((rows, half), BF16)], place, [stay, late, come])
    return out


def self_feature(place, grad_linear, w_weight, w_other):
    rows, dim = grad_linear.shape
    half = dim // 2

    def kernel(place_ref, grad_ref, w_in, w_other_in, out_ref, w_ref, sem):
        core = place_ref[1]
        pick_copy(core, w_in, w_other_in, w_ref, sem, aligned(core * half, half)).wait()
        out_ref[...] = times_t(grad_ref[...], w_ref[...])

    (out,) = call(
        kernel, "self_feature", [array((rows, half), F32)], place, [grad_linear],
        [w_weight, w_other], [pltpu.VMEM((half, dim), BF16), pltpu.SemaphoreType.DMA(())],
        flops=2 * rows * dim * half,
    )
    return out


def feature_step(place, self_grad, mine, other, q_weight, bias_mine, bias_other):
    rows, half = mine.shape
    dim = 2 * half

    def kernel(
        place_ref, self_ref, mine_ref, other_ref, bias_mine_ref, bias_other_ref, q_in,
        out_ref, bias_ref, q_ref, sem,
    ):
        core = place_ref[1]
        spans = [aligned(core * half, half), aligned((1 - core) * half, half)]
        q_copy = pltpu.make_async_copy(q_in.at[spans[0], :], q_ref, sem)
        q_copy.start()
        bias_ref[:, spans[0]] = bias_mine_ref[...]
        bias_ref[:, spans[1]] = bias_other_ref[...]
        q_copy.wait()
        out_ref[...] = (
            self_ref[...]
            + times_t(mine_ref[...], q_ref[:, spans[0]])
            + times_t(other_ref[...], q_ref[:, spans[1]])
        )

    return call(
        kernel, "feature_step", [array((rows, half), F32), array((1, dim), F32)], place,
        [self_grad, mine, other, bias_mine, bias_other], [q_weight],
        [pltpu.VMEM((half, dim), BF16), pltpu.SemaphoreType.DMA(())],
        flops=2 * rows * dim * half,
    )


def plane_slices(place, features, mine, other):
    rows, dim = features.shape
    half, width = dim // 2, dim // PLANE

    def kernel(place_ref, features_ref, mine_ref, other_ref, own_ref, next_ref, send_ref):
        core, spot = place_ref[1], place_ref[0] % PLANE
        targets = [own_ref, next_ref, send_ref.at[pl.ds(0, rows), :], send_ref.at[pl.ds(rows, rows), :]]
        for slot, target in enumerate(targets):
            to = spot ^ away(core, slot, 2)

            @pl.when(core == 0)
            def _():
                target[...] = features_ref[:, aligned(to * width, width)]

            within = aligned(to % 2 * width, width)

            @pl.when((core == 1) & (to < 2))
            def _():
                target[...] = other_ref[:, within]

            @pl.when((core == 1) & (to >= 2))
            def _():
                target[...] = mine_ref[:, within]

    outs = [array((rows, width), BF16)] * 2 + [array((2 * rows, width), BF16)]
    return call(kernel, "plane_slices", outs, place, [features, mine, other])


def node_step(place, mine, other, self_part, cotangent, w_weight, w_other):
    rows, half = mine.shape
    dim = 2 * half

    def kernel(
        place_ref, mine_ref, other_ref, self_ref, cotangent_ref, w_in, w_other_in,
        embeddings_ref, grad_ref, half_ref, lhs_ref, linear_ref, near_ref, sem,
    ):
        core = place_ref[1]
        near_copy = pick_copy(core, w_other_in, w_in, near_ref, sem)
        lhs_ref[:, aligned(core * half, half)] = mine_ref[...]
        lhs_ref[:, aligned((1 - core) * half, half)] = other_ref[...]
        near_copy.wait()
        linear_ref[...] = self_ref[...] + jnp.dot(
            lhs_ref[...], near_ref[...], preferred_element_type=F32
        )

        @pl.loop(0, rows // TILE, unroll=4)
        def _(step):
            at = aligned(step * TILE, TILE)
            linear = linear_ref[at, :]
            relu_out = jnp.maximum(linear, 0.0)
            scale = lax.rsqrt(jnp.mean(relu_out * relu_out, axis=1, keepdims=True) + 1e-06)
            embeddings_ref[at, :] = relu_out * scale
            grad_out = cotangent_ref[at, :].astype(F32)
            inner = jnp.mean(relu_out * grad_out, axis=1, keepdims=True)
            grad_relu = scale * grad_out - relu_out * (scale * scale * scale) * inner
            grad_ref[at, :] = jnp.where(linear > 0, grad_relu, 0.0).astype(BF16)

        half_ref[...] = grad_ref[aligned(core * (rows // 2), rows // 2), :]

    outs = [
        array((rows, dim), F32), array((rows, dim), BF16), array((rows // 2, dim), BF16),
    ]
    return call(
        kernel, "node_step", outs, place, [mine, other, self_part, cotangent],
        [w_weight, w_other],
        [
            pltpu.VMEM((rows, dim), BF16), pltpu.VMEM((rows, dim), F32),
            pltpu.VMEM((dim, dim), BF16), pltpu.SemaphoreType.DMA(()),
        ],
        flops=2 * rows * dim * dim,
    )


def plane_copies(core, rows, pieces, target, sem):
    own = pieces[0]
    half = rows // 2
    copies = [pltpu.make_async_copy(own, target.at[pl.ds(0, rows), :], sem.at[0])]
    for slot in range(1, PLANE):
        mine = pieces[slot]
        other = pieces[PLANE - 1 + reversed_bits(slot, 2)]
        for index, (part, at) in enumerate(((mine, core), (other, 1 - core))):
            spot = pl.multiple_of(slot * rows + at * half, TILE)
            copies.append(
                pltpu.make_async_copy(
                    part, target.at[pl.ds(spot, half), :], sem.at[2 * slot - 1 + index]
                )
            )
    return copies


def self_weight(place, pieces, slices, lines):
    rows, dim = pieces[0].shape
    width = slices[0].shape[1]

    def kernel(place_ref, *refs):
        parts, refs = refs[:PIECES], refs[PIECES:]
        slots, outs = refs[:4], refs[4:6]
        grads_ref, lhs_ref, sum_ref, sem, slice_sem = refs[6:]
        copies = plane_copies(place_ref[1], rows, parts, grads_ref, sem)
        own, far, near, last = slots
        spans = [own, last.at[pl.ds(0, rows), :], far.at[pl.ds(0, rows), :], last.at[pl.ds(rows, rows), :]]
        for slot, part in enumerate(spans):
            copies.append(
                pltpu.make_async_copy(part, lhs_ref.at[pl.ds(slot * rows, rows), :], slice_sem.at[slot])
            )
        for copy in copies:
            copy.start()
        for copy in copies:
            copy.wait()
        sum_ref[...] = across(lhs_ref[...], grads_ref[...])
        bias = bias_rows(jnp.sum(grads_ref[...].astype(F32), axis=0, keepdims=True))
        first = line_side(place_ref, lines)
        for slot, out_ref in enumerate(outs):
            out_ref[: width // 2, :] = sum_ref[
                aligned((first ^ slot) * (width // 2), width // 2), :
            ].astype(BF16)
            out_ref[width // 2 :, :] = bias

    return call(
        kernel, "self_weight", [array((width // 2 + TILE, dim), BF16)] * 2, place, [],
        list(pieces) + list(slices),
        [
            pltpu.VMEM((PLANE * rows, dim), BF16),
            pltpu.VMEM((PLANE * rows, width), BF16),
            pltpu.VMEM((width, dim), F32),
            pltpu.SemaphoreType.DMA((PIECES,)),
            pltpu.SemaphoreType.DMA((PLANE,)),
        ],
        flops=2 * PLANE * rows * dim * width,
    )


def row_grad(place, sums, pieces, w_weight, w_other, matrix, high, line_parts, lines):
    rows, dim = pieces[0].shape
    half = dim // 2
    total, nodes, width = lines * rows, PLANE * rows, dim // PLANE

    def kernel(place_ref, sums_ref, matrix_in, high_in, w_in, w_other_in, *refs):
        parts, refs = refs[:PIECES], refs[PIECES:]
        row_parts, refs = refs[: len(line_parts)], refs[len(line_parts) :]
        stay_ref, late_ref, go_ref, keep_ref, send_ref, refs = *refs[:5], refs[5:]
        grads_ref, rows_ref, sum_ref, hidden_ref, near_ref, matrix_ref, high_ref = refs[:7]
        sem, row_sem, near_sem, line_sem = refs[7:]
        core, spot = place_ref[1], place_ref[0] % PLANE
        copies = plane_copies(core, rows, parts, grads_ref, sem)
        row_copies = line_copies(row_parts, rows_ref, row_sem)
        near_copy = pick_copy(
            core, w_other_in, w_in, near_ref, near_sem, aligned(core * half, half)
        )
        line_sums = [
            pltpu.make_async_copy(matrix_in, matrix_ref, line_sem.at[0]),
            pltpu.make_async_copy(high_in, high_ref, line_sem.at[1]),
        ]
        start_all(copies + line_sums + row_copies)
        near_copy.wait()
        for slot in range(PLANE):
            wait_all(copies[max(2 * slot - 1, 0) : 2 * slot + 1])
            span = slice(slot * rows, (slot + 1) * rows)
            grad = times_t(grads_ref[span, :], near_ref[...])
            sum_ref[span, :] = (grad / sums_ref[span, 0:1]).astype(BF16)
        wait_all(line_sums)
        bias = jnp.zeros((1, half), F32)
        for at in range(lines):
            span = slice(at * rows, (at + 1) * rows)
            grad = jnp.dot(matrix_ref[span, :], sum_ref[...], preferred_element_type=F32)
            grad = jnp.where(high_ref[span, :].astype(F32) > 0, grad, 0.0)
            bias = bias + jnp.sum(grad, axis=0, keepdims=True)
            hidden_ref[span, :] = grad.astype(BF16)
        for slot in range(lines):
            at = to = slot * rows
            for ref in (stay_ref, late_ref, go_ref):
                if 0 <= to < ref.shape[0]:
                    break
                to -= ref.shape[0]
            ref[to : to + rows, :] = hidden_ref[at : at + rows, :]
        wait_all(row_copies)
        for slot in range(PLANE):
            to = spot ^ away(core, slot, 2)
            ref, at = (keep_ref, send_ref)[slot // 2], slot % 2 * width
            ref[at : at + width, :] = across(
                rows_ref[:, aligned(to * width, width)], hidden_ref[...]
            ).astype(BF16)
        for ref in (keep_ref, send_ref):
            ref[2 * width :, :] = bias_rows(bias)

    outs = [array((total // 2, half), BF16)] + [array((total // 4, half), BF16)] * 2
    outs += [array((dim // 2 + TILE, half), BF16)] * 2
    return call(
        kernel, "row_grad", outs, place, [sums],
        [matrix, high, w_weight, w_other] + list(pieces) + list(line_parts),
        [
            pltpu.VMEM((nodes, dim), BF16),
            pltpu.VMEM((total, dim), BF16),
            pltpu.VMEM((nodes, half), BF16),
            pltpu.VMEM((total, half), BF16),
            pltpu.VMEM((half, dim), BF16),
            pltpu.VMEM((total, nodes), BF16),
            pltpu.VMEM((total, half), BF16),
            pltpu.SemaphoreType.DMA((PIECES,)),
            pltpu.SemaphoreType.DMA((2 * lines - 1,)),
            pltpu.SemaphoreType.DMA(()),
            pltpu.SemaphoreType.DMA((2,)),
        ],
        flops=2 * nodes * dim * half + 2 * total * nodes * half + 2 * total * dim * half,
        limit=VMEM_BYTES if lines <= PLANE else ALL_VMEM,
    )


def fold(place, keep, came):
    height, width = keep.shape[0] - TILE, keep.shape[1]
    part = height // 2

    def kernel(place_ref, keep_ref, came_ref, stay_ref, go_ref):
        bias = keep_ref[height:, :].astype(F32) + came_ref[height:, :].astype(F32)
        bias = bias_rows(bias[0:1] + bias[1:2])
        for ref, at in ((stay_ref, 0), (go_ref, part)):
            span = slice(at, at + part)
            ref[:part, :] = (keep_ref[span, :].astype(F32) + came_ref[span, :].astype(F32)).astype(BF16)
            ref[part:, :] = bias

    return call(
        kernel, "fold", [array((part + TILE, width), BF16)] * 2, place, [keep, came]
    )


def merge(place, keep, came):
    height, width = keep.shape[0] - TILE, keep.shape[1]

    def kernel(place_ref, keep_ref, came_ref, out_ref):
        out_ref[...] = (keep_ref[...].astype(F32) + came_ref[...].astype(F32)).astype(BF16)
        bias = keep_ref[height:, :].astype(F32) + came_ref[height:, :].astype(F32)
        out_ref[height:, :] = bias_rows(bias[0:1] + bias[1:2])

    (out,) = call(kernel, "merge", [array(keep.shape, BF16)], place, [keep, came])
    return out


def unpack(place, blocks, spots, lines=0, sides=1, onto=None):
    parts = 2 if lines else 1
    height, width = blocks[0].shape
    count = len(blocks)

    def kernel(place_ref, *refs):
        sources, refs = refs[:count], refs[count + (onto is not None) :]
        out_ref, block_ref, wide_ref, sem, out_sem = refs
        spot = place_ref[0] % PLANE
        copies = [
            pltpu.make_async_copy(source, block_ref.at[index], sem.at[index])
            for index, source in enumerate(sources)
        ]
        start_all(copies)
        outs = []
        for index, copy in enumerate(copies):
            side, slot, at = spots[index]
            core = place_ref[1] ^ side
            row = (spot ^ away(core, slot, 2)) * parts
            if lines:
                row = row + (line_side(place_ref, lines) ^ at)
            cols = aligned(core * width, width) if sides > 1 else pl.ds(0, width)
            copy.wait()
            wide_ref[index] = block_ref[index].astype(F32)
            outs.append(
                pltpu.make_async_copy(
                    wide_ref.at[index], out_ref.at[aligned(row * height, height), cols],
                    out_sem.at[index],
                )
            )
            outs[-1].start()
        wait_all(outs)

    (out,) = call(
        kernel, "unpack", [array((PLANE * parts * height, width * sides), F32)], place, [],
        list(blocks) + ([] if onto is None else [onto]),
        [
            pltpu.VMEM((count, height, width), BF16), pltpu.VMEM((count, height, width), F32),
            pltpu.SemaphoreType.DMA((count,)), pltpu.SemaphoreType.DMA((count,)),
        ],
        far_outs=1, aliases={} if onto is None else {count + 1: 0},
    )
    return out


def on_device(
    features, neighbours, present, importance, q_weight, q_bias, w_weight, w_bias, cotangent
):
    rows, dim = features.shape
    count = lax.axis_size("nodes")
    lines = count // PLANE
    line_bits = bits_of(lines)
    node = lax.axis_index("nodes")
    core = lax.axis_index("stream")
    place = jnp.stack([node, core]).astype(I32)
    half_rows = rows // 2
    fence = lax.optimization_barrier

    def swap(value, bit, other_bit=None):
        bits = (bit, bit if other_bit is None else other_bit)
        pairs = [
            (2 * at + side, 2 * (at ^ bits[side]) + side) for at in range(count) for side in (0, 1)
        ]
        return lax.ppermute(value, ("nodes", "stream"), pairs)

    def plane_swap(value, step):
        return swap(value, 1 << step, 2 >> step)

    def line_swap(value, step):
        return swap(value, PLANE << step, PLANE << (line_bits - 1 - step))

    def trade(value):
        return lax.ppermute(value, "stream", [(0, 1), (1, 0)])

    def own_half(value, axis):
        size = value.shape[axis] // 2
        return lax.dynamic_slice_in_dim(value, core * size, size, axis)

    def joined(mine, other, axis):
        return jnp.where(
            core == 0,
            jnp.concatenate([mine, other], axis),
            jnp.concatenate([other, mine], axis),
        )

    mine = own_half(features, 0)
    stages = [line_swap(mine, line_bits - 1)]
    lists = sort_slots(place, neighbours, present, importance, count)
    lists = [jnp.concatenate([lists, trade(lists)], 0)]
    lists.append(plane_swap(lists[0], 1))
    lists[1], stages[0] = fence((lists[1], stages[0]))
    for step in reversed(range(line_bits - 1)):
        stages.append(line_swap(jnp.concatenate([mine] + stages, 0), step))
    lists.append(plane_swap(jnp.concatenate(lists, 0), 0))
    traded = [trade(stage) for stage in stages[:-1]]
    matrix, weight_sums = slot_matrix(place, lists, count)
    matrix, stages[-1], traded = fence((matrix, stages[-1], traded))
    line_parts = [features] + stages + traded + [trade(stages[-1])]
    send, high, low = first_sums(place, line_parts, q_weight, q_bias[None], matrix)
    send, w_sent = fence((send, w_weight))
    w_other = trade(w_sent)

    came = plane_swap(send, 0)
    keep, middle, own_send = more_sums(place, [high], [low], matrix, 0, 3)
    came_own = plane_swap(own_send, 0)
    last = plane_swap(middle + came, 1)
    came_own, w_other = fence((came_own, w_other))
    self_part = self_product(place, features, w_weight, w_other, w_bias[None])
    last, self_part, keep = fence((last, self_part, keep))
    mean_half = ((keep + came_own + last) / weight_sums[:rows, 0:1]).astype(BF16)

    mean_other = trade(mean_half)
    own_slice, next_slice, send_slices = plane_slices(place, features, mean_half, mean_other)
    far_slices = plane_swap(send_slices, 0)
    embeddings, grad_linear, grad_half = node_step(
        place, mean_half, mean_other, self_part, cotangent, w_weight, w_other
    )

    one, two = plane_swap(grad_half, 1), plane_swap(grad_half, 0)
    last_slices = plane_swap(jnp.concatenate([next_slice, far_slices[rows:]], 0), 1)
    one, two = fence((one, two))
    three = plane_swap(one, 0)
    three, last_slices = fence((three, last_slices))
    pieces = [grad_linear, one, two, three, trade(one), trade(two), trade(three)]
    slices = [own_slice, far_slices, next_slice, last_slices]
    w_keep, w_send = self_weight(place, pieces, slices, lines)
    pieces, w_keep, w_send = fence((pieces, w_keep, w_send))

    stay, late, go, q_keep, q_send = row_grad(
        place, weight_sums, pieces, w_weight, w_other, matrix, high, line_parts, lines
    )
    w_came = line_swap(w_send, 0)
    stay, late, go, q_keep, q_send, w_keep, w_came = fence(
        (stay, late, go, q_keep, q_send, w_keep, w_came)
    )

    def last_sum(keep, came):
        height = keep.shape[0] - TILE
        total = keep.astype(F32) + came.astype(F32)
        return total[:height].astype(BF16), total[height] + total[height + 1]

    biases = {}

    rows_go, rows_late = line_swap(go, 0), line_swap(late, 0)
    q_came = plane_swap(q_send, 0)
    w_sum = merge(place, w_keep, w_came)
    w_came = line_swap(w_sum, 1)
    q_came = fence(q_came)
    q_keep, q_send = fold(place, q_keep, q_came)
    q_came, w_came, stay, rows_go, rows_late = fence(
        (plane_swap(q_send, 1), w_came, stay, rows_go, rows_late)
    )
    for step in range(2, line_bits):
        w_sum = merge(place, w_sum, w_came)
        w_came = line_swap(w_sum, step)
    q_sum = merge(place, q_keep, q_came)
    q_came = line_swap(q_sum, 0)
    w_near, biases["w"] = last_sum(w_sum, w_came)
    w_far = line_swap(w_near, 0)
    near_one, near_two = plane_swap(w_near, 1), plane_swap(w_near, 0)
    self_grad = self_feature(place, grad_linear, w_weight, w_other)
    q_came, w_far, near_one, near_two, biases, self_grad = fence(
        (q_came, w_far, near_one, near_two, biases, self_grad)
    )
    for step in range(1, line_bits):
        q_sum = merge(place, q_sum, q_came)
        q_came = line_swap(q_sum, step)
    near_three = plane_swap(near_one, 0)
    far_one, far_two = plane_swap(w_far, 1), plane_swap(w_far, 0)
    q_came, near_three, far_one, far_two = fence((q_came, near_three, far_one, far_two))
    q_own, biases["q"] = last_sum(q_sum, q_came)
    half = stay.shape[0] // 2
    upper = (stay[half:].astype(F32) + rows_go.astype(F32)).astype(BF16)
    q_own, upper = fence((q_own, upper))
    rows_next = line_swap(upper, 1)
    q_one, q_two = plane_swap(q_own, 1), plane_swap(q_own, 0)
    far_three = plane_swap(far_one, 0)
    w_all = [w_near, w_far, near_one, far_one, near_two, far_two, near_three]
    w_part = unpack(
        place, w_all, [(0, at // 2, at % 2) for at in range(2 * PLANE - 1)], lines
    )
    bias_other = trade(biases["q"][None])
    q_one, q_two, far_three, rows_next, biases, w_part, bias_other = fence(
        (q_one, q_two, far_three, rows_next, biases, w_part, bias_other)
    )
    q_three = plane_swap(q_one, 0)
    w_grad = unpack(place, [far_three], [(0, 3, 1)], lines, 1, w_part)
    w_bias_grad, q_bias_half = biases["w"], biases["q"][None]

    stay = stay[: stay.shape[0] // 2]
    for step in range(2, line_bits):
        half = rows_late.shape[0] // 2
        upper = stay[half:].astype(F32) + rows_late[half:] + rows_next[half:]
        rows_next = (rows_next[:half] + line_swap(upper.astype(BF16), step).astype(F32)).astype(BF16)
        stay, rows_late = stay[:half], rows_late[:half]
    row_half = row_sums(place, stay, rows_late, rows_next)
    row_other = trade(row_half)
    q_mine = [q_own, q_one, q_two]
    q_other = [trade(block) for block in q_mine]
    feature_grad, q_bias_grad = feature_step(
        place, self_grad, row_half, row_other, q_weight, q_bias_half, bias_other
    )
    q_three, q_other, w_grad, q_bias_grad, feature_grad = fence(
        (q_three, q_other, w_grad, q_bias_grad, feature_grad)
    )
    last_other = trade(q_three)
    q_part = unpack(place, q_mine + [q_three], [(0, at, 0) for at in range(PLANE)], 0, 2)
    q_part, last_other = fence((q_part, last_other))
    q_grad = unpack(
        place, q_other + [last_other], [(1, at, 0) for at in range(PLANE)], 0, 2, q_part
    )
    return (embeddings, feature_grad, q_grad, q_bias_grad[0], w_grad, w_bias_grad)


def solution(mesh):
    in_specs = (
        P("nodes", None),
        P("nodes", "stream"),
        P("nodes", "stream"),
        P("nodes", "stream"),
        P(),
        P(),
        P("stream", None),
        P(),
        P("nodes", None),
    )
    out_specs = (P("nodes", None), P("nodes", "stream"), P(), P(), P("stream", None), P())
    return jax.shard_map(
        on_device, mesh=mesh, in_specs=in_specs, out_specs=out_specs, check_vma=False
    )
```

```python
import jax
import jax.numpy as jnp
from jax import lax
from jax.experimental import pallas as pl
from jax.experimental.pallas import tpu as pltpu
from jax.sharding import PartitionSpec as P

PLANE = 4
TILE = 16
PIECES = 2 * PLANE - 1
VMEM_BYTES = 48 * 1024 * 1024
ALL_VMEM = 67_000_000
F32, BF16, I32 = jnp.float32, jnp.bfloat16, jnp.int32


def across(lhs, rhs):
    return lax.dot_general(lhs, rhs, (((0,), (0,)), ((), ())), preferred_element_type=F32)


def times_t(lhs, rhs):
    return lax.dot_general(lhs, rhs, (((1,), (1,)), ((), ())), preferred_element_type=F32)


def aligned(start, size):
    start = start if isinstance(start, int) else pl.multiple_of(start, size)
    return pl.ds(start, size)


def spaced(space, arrays):
    return [pl.BlockSpec(memory_space=space) for _ in arrays]


def array(shape, dtype):
    return jax.ShapeDtypeStruct(shape, dtype)


def call(kernel, name, outs, place, near, far=(), scratch=(), flops=0, far_outs=0,
         limit=VMEM_BYTES, light=False, aliases={}):
    operands = list(near) + list(far)
    moved = sum(a.size * a.dtype.itemsize for a in operands + list(outs))
    if light:
        flops, moved = 1, 1
    return pl.pallas_call(
        kernel,
        name=name,
        out_shape=list(outs),
        in_specs=spaced(pltpu.SMEM, [place]) + spaced(pltpu.VMEM, near) + spaced(pltpu.HBM, far),
        out_specs=spaced(pltpu.VMEM, outs[: len(outs) - far_outs])
        + spaced(pltpu.HBM, outs[len(outs) - far_outs :]),
        scratch_shapes=list(scratch),
        input_output_aliases=aliases,
        compiler_params=pltpu.CompilerParams(vmem_limit_bytes=limit),
        cost_estimate=pl.CostEstimate(
            flops=int(flops), bytes_accessed=int(moved), transcendentals=0
        ),
    )(place, *operands)


def reversed_bits(value, bits):
    out = 0
    for bit in range(bits):
        out = out | (((value >> bit) & 1) << (bits - 1 - bit))
    return out


def away(core, slot, bits):
    return jnp.where(core == 0, reversed_bits(slot, bits), slot)


def bits_of(size):
    return size.bit_length() - 1


def line_side(place_ref, lines):
    line = place_ref[0] // PLANE
    return jnp.where(place_ref[1] == 0, line & 1, line // (lines // 2))


def bias_rows(value):
    top = value.astype(BF16).astype(F32)
    row_at = lax.broadcasted_iota(I32, (TILE, value.shape[1]), 0)
    return jnp.where(row_at == 0, top, jnp.where(row_at == 1, value - top, 0.0)).astype(BF16)


def stacked(parts, target, sem, first=0):
    copies, at = [], 0
    for index, part in enumerate(parts):
        span = pl.ds(at, part.shape[0])
        copies.append(pltpu.make_async_copy(part, target.at[span, :], sem.at[first + index]))
        at += part.shape[0]
    return copies


def line_copies(parts, target, sem):
    own, parts = parts[0], parts[1:]
    mine, other = parts[: len(parts) // 2], parts[len(parts) // 2 :]
    rows, bits = own.shape[0], len(mine)
    half = rows // 2
    copies = [pltpu.make_async_copy(own, target.at[pl.ds(0, rows), :], sem.at[0])]
    for slot in range(1, 1 << bits):
        for index, (stages, at) in enumerate(((mine, slot), (other, reversed_bits(slot, bits)))):
            stage = at.bit_length() - 1
            view = stages[stage].at[pl.ds((at - (1 << stage)) * half, half), :]
            spot = target.at[pl.ds(slot * rows + index * half, half), :]
            copies.append(pltpu.make_async_copy(view, spot, sem.at[2 * slot - 1 + index]))
    return copies


def start_all(copies):
    for copy in copies:
        copy.start()


def wait_all(copies):
    for copy in copies:
        copy.wait()


def sort_slots(place, neighbours, present, importance, count):
    rows, slots = neighbours.shape
    turns = -(-slots // count)
    arrays = [neighbours.T, present.T, importance.T]

    def kernel(place_ref, *refs):
        out_ref, neighbours_ref, present_ref, importance_ref, sem = refs[3:]
        copies = [
            pltpu.make_async_copy(part, target, sem.at[index])
            for index, (part, target) in enumerate(zip(refs[:3], refs[4:7]))
        ]
        start_all(copies)
        wait_all(copies)
        slot_at = lax.broadcasted_iota(I32, (slots, rows), 0)
        node_at = lax.broadcasted_iota(I32, (slots, rows), 1)
        block = (node_at * slots + slot_at) & (count - 1)
        row = neighbours_ref[...] - rows * block
        packed = row * 128 + present_ref[...] * importance_ref[...]
        block_at = lax.broadcasted_iota(I32, (count, rows), 0)
        node_at = lax.broadcasted_iota(I32, (count, rows), 1)
        first = (block_at - slots * node_at) & (count - 1)
        for turn in range(turns):
            total = jnp.zeros((count, rows), I32)
            for slot in range(slots):
                at = slot - count * turn
                if 0 <= at < count:
                    total = jnp.where(first == at, packed[slot : slot + 1, :], total)
            out_ref[turn * count : (turn + 1) * count, :] = total

    (out,) = call(
        kernel, "sort_slots", [array((turns * count, rows), I32)], place, [], arrays,
        [pltpu.VMEM((slots, rows), I32)] * 3 + [pltpu.SemaphoreType.DMA((3,))], limit=ALL_VMEM,
    )
    return out


def slot_matrix(place, lists, count):
    tall, rows = lists[0].shape
    lines, width, turns = count // PLANE, PLANE * rows, tall // count

    def kernel(place_ref, own_ref, next_ref, rest_ref, sums_ref, far_ref, out_ref, sem):
        slot_refs = [(own_ref, 0), (next_ref, 0), (rest_ref, 0), (rest_ref, tall)]
        core, spot, line = place_ref[1], place_ref[0] % PLANE, place_ref[0] // PLANE
        sums = [
            jnp.sum((ref[at : at + tall, :] & 127).astype(F32), axis=0, keepdims=True)
            for ref, at in slot_refs
        ]
        sums = jnp.broadcast_to(jnp.concatenate(sums, axis=1), (8, width))
        sums_ref[...] = sums.T
        for at in range(lines):
            block = (line ^ away(core, at, bits_of(lines))) * PLANE + spot
            ids, weights = [], []
            for turn in range(turns):
                listed = jnp.concatenate(
                    [ref[pl.ds(at + turn * count + block, 1), :] for ref, at in slot_refs],
                    axis=1,
                )
                ids.append(((listed >> 7) - rows // 2).astype(F32).astype(BF16))
                weights.append((listed & 127).astype(F32).astype(BF16))
            shift = core * (rows // 2) if at else 0

            @pl.loop(0, rows // TILE)
            def _(step):
                base = step * TILE + shift
                base = jnp.where(base >= rows, base - rows, base)
                row_at = lax.broadcasted_iota(I32, (TILE, width), 0) + (base - rows // 2)
                row_at = row_at.astype(F32).astype(BF16)
                zero = jnp.zeros((TILE, width), BF16)
                total = zero
                for listed, weight in zip(ids, weights):
                    total = total + jnp.where(listed == row_at, weight, zero)
                out_ref[aligned(at * rows + step * TILE, TILE), :] = total

            span = pl.ds(at * rows, rows)
            pltpu.make_async_copy(out_ref.at[span, :], far_ref.at[span, :], sem.at[at]).start()
        for at in range(lines):
            span = pl.ds(at * rows, rows)
            pltpu.make_async_copy(out_ref.at[span, :], far_ref.at[span, :], sem.at[at]).wait()

    sums, matrix = call(
        kernel, "slot_matrix", [array((width, 8), F32), array((lines * rows, width), BF16)],
        place, lists,
        scratch=[pltpu.VMEM((lines * rows, width), BF16), pltpu.SemaphoreType.DMA((lines,))],
        flops=3 * turns * lines * rows * width, far_outs=1, limit=ALL_VMEM, light=True,
    )
    return matrix, sums


def half_copy(core, q_in, q_ref, sem):
    half = q_ref.shape[1]
    return pltpu.make_async_copy(q_in.at[:, aligned(core * half, half)], q_ref, sem)


def hidden_of(core, rows, q_ref, bias_ref):
    half = q_ref.shape[1]
    bias = bias_ref[:, aligned(core * half, half)]
    hidden = jnp.maximum(jnp.dot(rows, q_ref[...], preferred_element_type=F32) + bias, 0.0)
    top = hidden.astype(BF16)
    return top, (hidden - top.astype(F32)).astype(BF16)


def lane_span(start, size):
    low = start // 128 * 128
    high = -(-(start + size) // 128) * 128
    return low, high - low, start - low


def first_sums(place, line_parts, q_weight, q_bias, matrix):
    rows, dim = line_parts[0].shape
    total, width = matrix.shape
    half, part, count = dim // 2, width // PLANE, len(line_parts)
    lines = total // rows
    low, span_width, skip = lane_span(width - part, part)

    def kernel(place_ref, bias_ref, q_in, matrix_in, *refs):
        parts, refs = refs[:count], refs[count:]
        send_ref, high_out, low_out, rows_ref, high_ref, low_ref, matrix_ref, q_ref = refs[:8]
        row_sem, sem = refs[8:]
        core = place_ref[1]
        q_copy = half_copy(core, q_in, q_ref, sem.at[0])
        matrix_copy = pltpu.make_async_copy(
            matrix_in.at[:, pl.ds(low, span_width)], matrix_ref, sem.at[1]
        )
        copies = line_copies(parts, rows_ref, row_sem)
        start_all([q_copy] + copies + [matrix_copy])
        q_copy.wait()
        for at in range(lines):
            wait_all(copies[max(2 * at - 1, 0) : 2 * at + 1])
            span = slice(at * rows, (at + 1) * rows)
            high_ref[span, :], low_ref[span, :] = hidden_of(
                core, rows_ref[span, :], q_ref, bias_ref
            )
        outs = [
            pltpu.make_async_copy(high_ref, high_out, sem.at[2]),
            pltpu.make_async_copy(low_ref, low_out, sem.at[3]),
        ]
        start_all(outs)
        matrix_copy.wait()
        total_sum = across(matrix_ref[...], high_ref[...]) + across(matrix_ref[...], low_ref[...])
        send_ref[...] = total_sum[skip : skip + part, :]
        wait_all(outs)

    return call(
        kernel, "first_sums",
        [array((part, half), F32)] + [array((total, half), BF16)] * 2,
        place, [q_bias], [q_weight, matrix] + list(line_parts),
        [
            pltpu.VMEM((total, dim), BF16),
            pltpu.VMEM((total, half), BF16),
            pltpu.VMEM((total, half), BF16),
            pltpu.VMEM((total, span_width), BF16),
            pltpu.VMEM((dim, half), BF16),
            pltpu.SemaphoreType.DMA((2 * lines - 1,)),
            pltpu.SemaphoreType.DMA((4,)),
        ],
        flops=2 * total * dim * half + 4 * total * part * half, far_outs=2, limit=ALL_VMEM,
    )


def more_sums(place, highs, lows, matrix, first, slots):
    total = matrix.shape[0]
    part = matrix.shape[1] // PLANE
    width = slots * part
    start, span_width, skip = lane_span(first * part, width)
    half, count = highs[0].shape[1], len(highs)

    def kernel(place_ref, matrix_in, *refs):
        parts, refs = refs[: 2 * count], refs[2 * count :]
        sum_refs, refs = refs[:slots], refs[slots:]
        high_ref, low_ref, matrix_ref, sem = refs
        copies = [
            pltpu.make_async_copy(
                matrix_in.at[:, pl.ds(start, span_width)], matrix_ref, sem.at[2 * count]
            )
        ]
        copies += stacked(parts[:count], high_ref, sem)
        copies += stacked(parts[count:], low_ref, sem, count)
        start_all(copies)
        wait_all(copies)
        total_sum = across(matrix_ref[...], high_ref[...]) + across(matrix_ref[...], low_ref[...])
        for slot, sum_ref in enumerate(sum_refs):
            at = skip + slot * part
            sum_ref[...] = total_sum[at : at + part, :]

    return call(
        kernel, "more_sums", [array((part, half), F32)] * slots, place, [],
        [matrix] + list(highs) + list(lows),
        [
            pltpu.VMEM((total, half), BF16),
            pltpu.VMEM((total, half), BF16),
            pltpu.VMEM((total, span_width), BF16),
            pltpu.SemaphoreType.DMA((2 * count + 1,)),
        ],
        flops=4 * total * width * half, limit=ALL_VMEM,
    )


def pick_copy(core, first, second, target, sem, rows=None):
    views = [ref if rows is None else ref.at[rows, :] for ref in (first, second)]
    for side, view in enumerate(views):

        @pl.when(core == side)
        def _():
            pltpu.make_async_copy(view, target, sem).start()

    return pltpu.make_async_copy(views[0], target, sem)


def self_product(place, features, w_weight, w_other, w_bias):
    rows, dim = features.shape

    def kernel(place_ref, features_ref, bias_ref, w_in, w_other_in, out_ref, w_ref, sem):
        pick_copy(place_ref[1], w_in, w_other_in, w_ref, sem).wait()
        out_ref[...] = bias_ref[...] + jnp.dot(
            features_ref[...], w_ref[...], preferred_element_type=F32
        )

    (out,) = call(
        kernel, "self_product", [array((rows, dim), F32)], place, [features, w_bias],
        [w_weight, w_other], [pltpu.VMEM((dim, dim), BF16), pltpu.SemaphoreType.DMA(())],
        flops=2 * rows * dim * dim,
    )
    return out


def row_sums(place, stay, late, come):
    rows, half = late.shape

    def kernel(place_ref, stay_ref, late_ref, come_ref, out_ref):
        for part in range(2):
            span = slice(part * rows // 2, (part + 1) * rows // 2)
            came = late_ref[span, :].astype(F32) + come_ref[span, :].astype(F32)
            at = aligned((place_ref[1] ^ part) * (rows // 2), rows // 2)
            out_ref[at, :] = (stay_ref[at, :].astype(F32) + came).astype(BF16)

    (out,) = call(kernel, "row_sums", [array((rows, half), BF16)], place, [stay, late, come])
    return out


def self_feature(place, grad_linear, w_weight, w_other):
    rows, dim = grad_linear.shape
    half = dim // 2

    def kernel(place_ref, grad_ref, w_in, w_other_in, out_ref, w_ref, sem):
        core = place_ref[1]
        pick_copy(core, w_in, w_other_in, w_ref, sem, aligned(core * half, half)).wait()
        out_ref[...] = times_t(grad_ref[...], w_ref[...])

    (out,) = call(
        kernel, "self_feature", [array((rows, half), F32)], place, [grad_linear],
        [w_weight, w_other], [pltpu.VMEM((half, dim), BF16), pltpu.SemaphoreType.DMA(())],
        flops=2 * rows * dim * half,
    )
    return out


def feature_step(place, self_grad, mine, other, q_weight, bias_mine, bias_other):
    rows, half = mine.shape
    dim = 2 * half

    def kernel(
        place_ref, self_ref, mine_ref, other_ref, bias_mine_ref, bias_other_ref, q_in,
        out_ref, bias_ref, q_ref, sem,
    ):
        core = place_ref[1]
        spans = [aligned(core * half, half), aligned((1 - core) * half, half)]
        q_copy = pltpu.make_async_copy(q_in.at[spans[0], :], q_ref, sem)
        q_copy.start()
        bias_ref[:, spans[0]] = bias_mine_ref[...]
        bias_ref[:, spans[1]] = bias_other_ref[...]
        q_copy.wait()
        out_ref[...] = (
            self_ref[...]
            + times_t(mine_ref[...], q_ref[:, spans[0]])
            + times_t(other_ref[...], q_ref[:, spans[1]])
        )

    return call(
        kernel, "feature_step", [array((rows, half), F32), array((1, dim), F32)], place,
        [self_grad, mine, other, bias_mine, bias_other], [q_weight],
        [pltpu.VMEM((half, dim), BF16), pltpu.SemaphoreType.DMA(())],
        flops=2 * rows * dim * half,
    )


def plane_slices(place, features, mine, other):
    rows, dim = features.shape
    half, width = dim // 2, dim // PLANE

    def kernel(place_ref, features_ref, mine_ref, other_ref, own_ref, next_ref, send_ref):
        core, spot = place_ref[1], place_ref[0] % PLANE
        targets = [own_ref, next_ref, send_ref.at[pl.ds(0, rows), :], send_ref.at[pl.ds(rows, rows), :]]
        for slot, target in enumerate(targets):
            to = spot ^ away(core, slot, 2)

            @pl.when(core == 0)
            def _():
                target[...] = features_ref[:, aligned(to * width, width)]

            within = aligned(to % 2 * width, width)

            @pl.when((core == 1) & (to < 2))
            def _():
                target[...] = other_ref[:, within]

            @pl.when((core == 1) & (to >= 2))
            def _():
                target[...] = mine_ref[:, within]

    outs = [array((rows, width), BF16)] * 2 + [array((2 * rows, width), BF16)]
    return call(kernel, "plane_slices", outs, place, [features, mine, other])


def node_step(place, mine, other, self_part, cotangent, w_weight, w_other):
    rows, half = mine.shape
    dim = 2 * half

    def kernel(
        place_ref, mine_ref, other_ref, self_ref, cotangent_ref, w_in, w_other_in,
        embeddings_ref, grad_ref, half_ref, lhs_ref, linear_ref, near_ref, sem,
    ):
        core = place_ref[1]
        near_copy = pick_copy(core, w_other_in, w_in, near_ref, sem)
        lhs_ref[:, aligned(core * half, half)] = mine_ref[...]
        lhs_ref[:, aligned((1 - core) * half, half)] = other_ref[...]
        near_copy.wait()
        linear_ref[...] = self_ref[...] + jnp.dot(
            lhs_ref[...], near_ref[...], preferred_element_type=F32
        )

        @pl.loop(0, rows // TILE, unroll=4)
        def _(step):
            at = aligned(step * TILE, TILE)
            linear = linear_ref[at, :]
            relu_out = jnp.maximum(linear, 0.0)
            scale = lax.rsqrt(jnp.mean(relu_out * relu_out, axis=1, keepdims=True) + 1e-06)
            embeddings_ref[at, :] = relu_out * scale
            grad_out = cotangent_ref[at, :].astype(F32)
            inner = jnp.mean(relu_out * grad_out, axis=1, keepdims=True)
            grad_relu = scale * grad_out - relu_out * (scale * scale * scale) * inner
            grad_ref[at, :] = jnp.where(linear > 0, grad_relu, 0.0).astype(BF16)

        half_ref[...] = grad_ref[aligned(core * (rows // 2), rows // 2), :]

    outs = [
        array((rows, dim), F32), array((rows, dim), BF16), array((rows // 2, dim), BF16),
    ]
    return call(
        kernel, "node_step", outs, place, [mine, other, self_part, cotangent],
        [w_weight, w_other],
        [
            pltpu.VMEM((rows, dim), BF16), pltpu.VMEM((rows, dim), F32),
            pltpu.VMEM((dim, dim), BF16), pltpu.SemaphoreType.DMA(()),
        ],
        flops=2 * rows * dim * dim,
    )


def plane_copies(core, rows, pieces, target, sem):
    own = pieces[0]
    half = rows // 2
    copies = [pltpu.make_async_copy(own, target.at[pl.ds(0, rows), :], sem.at[0])]
    for slot in range(1, PLANE):
        mine = pieces[slot]
        other = pieces[PLANE - 1 + reversed_bits(slot, 2)]
        for index, (part, at) in enumerate(((mine, core), (other, 1 - core))):
            spot = pl.multiple_of(slot * rows + at * half, TILE)
            copies.append(
                pltpu.make_async_copy(
                    part, target.at[pl.ds(spot, half), :], sem.at[2 * slot - 1 + index]
                )
            )
    return copies


def self_weight(place, pieces, slices, lines):
    rows, dim = pieces[0].shape
    width = slices[0].shape[1]

    def kernel(place_ref, *refs):
        parts, refs = refs[:PIECES], refs[PIECES:]
        slots, outs = refs[:4], refs[4:6]
        grads_ref, lhs_ref, sum_ref, sem, slice_sem = refs[6:]
        copies = plane_copies(place_ref[1], rows, parts, grads_ref, sem)
        own, far, near, last = slots
        spans = [own, last.at[pl.ds(0, rows), :], far.at[pl.ds(0, rows), :], last.at[pl.ds(rows, rows), :]]
        for slot, part in enumerate(spans):
            copies.append(
                pltpu.make_async_copy(part, lhs_ref.at[pl.ds(slot * rows, rows), :], slice_sem.at[slot])
            )
        for copy in copies:
            copy.start()
        for copy in copies:
            copy.wait()
        sum_ref[...] = across(lhs_ref[...], grads_ref[...])
        bias = bias_rows(jnp.sum(grads_ref[...].astype(F32), axis=0, keepdims=True))
        first = line_side(place_ref, lines)
        for slot, out_ref in enumerate(outs):
            out_ref[: width // 2, :] = sum_ref[
                aligned((first ^ slot) * (width // 2), width // 2), :
            ].astype(BF16)
            out_ref[width // 2 :, :] = bias

    return call(
        kernel, "self_weight", [array((width // 2 + TILE, dim), BF16)] * 2, place, [],
        list(pieces) + list(slices),
        [
            pltpu.VMEM((PLANE * rows, dim), BF16),
            pltpu.VMEM((PLANE * rows, width), BF16),
            pltpu.VMEM((width, dim), F32),
            pltpu.SemaphoreType.DMA((PIECES,)),
            pltpu.SemaphoreType.DMA((PLANE,)),
        ],
        flops=2 * PLANE * rows * dim * width,
    )


def row_grad(place, sums, pieces, w_weight, w_other, matrix, high, line_parts, lines):
    rows, dim = pieces[0].shape
    half = dim // 2
    total, nodes, width = lines * rows, PLANE * rows, dim // PLANE

    def kernel(place_ref, sums_ref, matrix_in, high_in, w_in, w_other_in, *refs):
        parts, refs = refs[:PIECES], refs[PIECES:]
        row_parts, refs = refs[: len(line_parts)], refs[len(line_parts) :]
        stay_ref, late_ref, go_ref, keep_ref, send_ref, refs = *refs[:5], refs[5:]
        grads_ref, rows_ref, sum_ref, hidden_ref, near_ref, matrix_ref, high_ref = refs[:7]
        sem, row_sem, near_sem, line_sem = refs[7:]
        core, spot = place_ref[1], place_ref[0] % PLANE
        copies = plane_copies(core, rows, parts, grads_ref, sem)
        row_copies = line_copies(row_parts, rows_ref, row_sem)
        near_copy = pick_copy(
            core, w_other_in, w_in, near_ref, near_sem, aligned(core * half, half)
        )
        line_sums = [
            pltpu.make_async_copy(matrix_in, matrix_ref, line_sem.at[0]),
            pltpu.make_async_copy(high_in, high_ref, line_sem.at[1]),
        ]
        start_all(copies + line_sums + row_copies)
        near_copy.wait()
        for slot in range(PLANE):
            wait_all(copies[max(2 * slot - 1, 0) : 2 * slot + 1])
            span = slice(slot * rows, (slot + 1) * rows)
            grad = times_t(grads_ref[span, :], near_ref[...])
            sum_ref[span, :] = (grad / sums_ref[span, 0:1]).astype(BF16)
        wait_all(line_sums)
        bias = jnp.zeros((1, half), F32)
        for at in range(lines):
            span = slice(at * rows, (at + 1) * rows)
            grad = jnp.dot(matrix_ref[span, :], sum_ref[...], preferred_element_type=F32)
            grad = jnp.where(high_ref[span, :].astype(F32) > 0, grad, 0.0)
            bias = bias + jnp.sum(grad, axis=0, keepdims=True)
            hidden_ref[span, :] = grad.astype(BF16)
        for slot in range(lines):
            at = to = slot * rows
            for ref in (stay_ref, late_ref, go_ref):
                if 0 <= to < ref.shape[0]:
                    break
                to -= ref.shape[0]
            ref[to : to + rows, :] = hidden_ref[at : at + rows, :]
        wait_all(row_copies)
        for slot in range(PLANE):
            to = spot ^ away(core, slot, 2)
            ref, at = (keep_ref, send_ref)[slot // 2], slot % 2 * width
            ref[at : at + width, :] = across(
                rows_ref[:, aligned(to * width, width)], hidden_ref[...]
            ).astype(BF16)
        for ref in (keep_ref, send_ref):
            ref[2 * width :, :] = bias_rows(bias)

    outs = [array((total // 2, half), BF16)] + [array((total // 4, half), BF16)] * 2
    outs += [array((dim // 2 + TILE, half), BF16)] * 2
    return call(
        kernel, "row_grad", outs, place, [sums],
        [matrix, high, w_weight, w_other] + list(pieces) + list(line_parts),
        [
            pltpu.VMEM((nodes, dim), BF16),
            pltpu.VMEM((total, dim), BF16),
            pltpu.VMEM((nodes, half), BF16),
            pltpu.VMEM((total, half), BF16),
            pltpu.VMEM((half, dim), BF16),
            pltpu.VMEM((total, nodes), BF16),
            pltpu.VMEM((total, half), BF16),
            pltpu.SemaphoreType.DMA((PIECES,)),
            pltpu.SemaphoreType.DMA((2 * lines - 1,)),
            pltpu.SemaphoreType.DMA(()),
            pltpu.SemaphoreType.DMA((2,)),
        ],
        flops=2 * nodes * dim * half + 2 * total * nodes * half + 2 * total * dim * half,
        limit=VMEM_BYTES if lines <= PLANE else ALL_VMEM,
    )


def fold(place, keep, came):
    height, width = keep.shape[0] - TILE, keep.shape[1]
    part = height // 2

    def kernel(place_ref, keep_ref, came_ref, stay_ref, go_ref):
        bias = keep_ref[height:, :].astype(F32) + came_ref[height:, :].astype(F32)
        bias = bias_rows(bias[0:1] + bias[1:2])
        for ref, at in ((stay_ref, 0), (go_ref, part)):
            span = slice(at, at + part)
            ref[:part, :] = (keep_ref[span, :].astype(F32) + came_ref[span, :].astype(F32)).astype(BF16)
            ref[part:, :] = bias

    return call(
        kernel, "fold", [array((part + TILE, width), BF16)] * 2, place, [keep, came]
    )


def merge(place, keep, came):
    height, width = keep.shape[0] - TILE, keep.shape[1]

    def kernel(place_ref, keep_ref, came_ref, out_ref):
        out_ref[...] = (keep_ref[...].astype(F32) + came_ref[...].astype(F32)).astype(BF16)
        bias = keep_ref[height:, :].astype(F32) + came_ref[height:, :].astype(F32)
        out_ref[height:, :] = bias_rows(bias[0:1] + bias[1:2])

    (out,) = call(kernel, "merge", [array(keep.shape, BF16)], place, [keep, came])
    return out


def unpack(place, blocks, spots, lines=0, sides=1, onto=None):
    parts = 2 if lines else 1
    height, width = blocks[0].shape
    count = len(blocks)

    def kernel(place_ref, *refs):
        sources, refs = refs[:count], refs[count + (onto is not None) :]
        out_ref, block_ref, wide_ref, sem, out_sem = refs
        spot = place_ref[0] % PLANE
        copies = [
            pltpu.make_async_copy(source, block_ref.at[index], sem.at[index])
            for index, source in enumerate(sources)
        ]
        start_all(copies)
        outs = []
        for index, copy in enumerate(copies):
            side, slot, at = spots[index]
            core = place_ref[1] ^ side
            row = (spot ^ away(core, slot, 2)) * parts
            if lines:
                row = row + (line_side(place_ref, lines) ^ at)
            cols = aligned(core * width, width) if sides > 1 else pl.ds(0, width)
            copy.wait()
            wide_ref[index] = block_ref[index].astype(F32)
            outs.append(
                pltpu.make_async_copy(
                    wide_ref.at[index], out_ref.at[aligned(row * height, height), cols],
                    out_sem.at[index],
                )
            )
            outs[-1].start()
        wait_all(outs)

    (out,) = call(
        kernel, "unpack", [array((PLANE * parts * height, width * sides), F32)], place, [],
        list(blocks) + ([] if onto is None else [onto]),
        [
            pltpu.VMEM((count, height, width), BF16), pltpu.VMEM((count, height, width), F32),
            pltpu.SemaphoreType.DMA((count,)), pltpu.SemaphoreType.DMA((count,)),
        ],
        far_outs=1, aliases={} if onto is None else {count + 1: 0},
    )
    return out


def on_device(
    features, neighbours, present, importance, q_weight, q_bias, w_weight, w_bias, cotangent
):
    rows, dim = features.shape
    count = lax.axis_size("nodes")
    lines = count // PLANE
    line_bits = bits_of(lines)
    node = lax.axis_index("nodes")
    core = lax.axis_index("stream")
    place = jnp.stack([node, core]).astype(I32)
    half_rows = rows // 2
    fence = lax.optimization_barrier

    def swap(value, bit, other_bit=None):
        bits = (bit, bit if other_bit is None else other_bit)
        pairs = [
            (2 * at + side, 2 * (at ^ bits[side]) + side) for at in range(count) for side in (0, 1)
        ]
        return lax.ppermute(value, ("nodes", "stream"), pairs)

    def plane_swap(value, step):
        return swap(value, 1 << step, 2 >> step)

    def line_swap(value, step):
        return swap(value, PLANE << step, PLANE << (line_bits - 1 - step))

    def trade(value):
        return lax.ppermute(value, "stream", [(0, 1), (1, 0)])

    def own_half(value, axis):
        size = value.shape[axis] // 2
        return lax.dynamic_slice_in_dim(value, core * size, size, axis)

    def joined(mine, other, axis):
        return jnp.where(
            core == 0,
            jnp.concatenate([mine, other], axis),
            jnp.concatenate([other, mine], axis),
        )

    mine = own_half(features, 0)
    stages = [line_swap(mine, line_bits - 1)]
    lists = sort_slots(place, neighbours, present, importance, count)
    lists = [jnp.concatenate([lists, trade(lists)], 0)]
    lists.append(plane_swap(lists[0], 1))
    lists[1], stages[0] = fence((lists[1], stages[0]))
    for step in reversed(range(line_bits - 1)):
        stages.append(line_swap(jnp.concatenate([mine] + stages, 0), step))
    lists.append(plane_swap(jnp.concatenate(lists, 0), 0))
    traded = [trade(stage) for stage in stages[:-1]]
    matrix, weight_sums = slot_matrix(place, lists, count)
    matrix, stages[-1], traded = fence((matrix, stages[-1], traded))
    line_parts = [features] + stages + traded + [trade(stages[-1])]
    send, high, low = first_sums(place, line_parts, q_weight, q_bias[None], matrix)
    send, w_sent = fence((send, w_weight))
    w_other = trade(w_sent)

    came = plane_swap(send, 0)
    keep, middle, own_send = more_sums(place, [high], [low], matrix, 0, 3)
    came_own = plane_swap(own_send, 0)
    last = plane_swap(middle + came, 1)
    self_part = self_product(place, features, w_weight, w_other, w_bias[None])
    came_own, self_part, keep, weight_sum = fence((came_own, self_part, keep, weight_sums[:rows, 0]))
    mean_half = ((keep + came_own + last) / weight_sum[:, None]).astype(BF16)

    mean_other = trade(mean_half)
    own_slice, next_slice, send_slices = plane_slices(place, features, mean_half, mean_other)
    far_slices = plane_swap(send_slices, 0)
    embeddings, grad_linear, grad_half = node_step(
        place, mean_half, mean_other, self_part, cotangent, w_weight, w_other
    )

    one, two = plane_swap(grad_half, 1), plane_swap(grad_half, 0)
    last_slices = plane_swap(jnp.concatenate([next_slice, far_slices[rows:]], 0), 1)
    one, two = fence((one, two))
    three = plane_swap(one, 0)
    three, last_slices = fence((three, last_slices))
    pieces = [grad_linear, one, two, three, trade(one), trade(two), trade(three)]
    slices = [own_slice, far_slices, next_slice, last_slices]
    w_keep, w_send = self_weight(place, pieces, slices, lines)
    pieces, w_keep, w_send = fence((pieces, w_keep, w_send))

    stay, late, go, q_keep, q_send = row_grad(
        place, weight_sums, pieces, w_weight, w_other, matrix, high, line_parts, lines
    )
    w_came = line_swap(w_send, 0)
    stay, late, go, q_keep, q_send, w_keep, w_came = fence(
        (stay, late, go, q_keep, q_send, w_keep, w_came)
    )

    def last_sum(keep, came):
        height = keep.shape[0] - TILE
        total = keep.astype(F32) + came.astype(F32)
        return total[:height].astype(BF16), total[height] + total[height + 1]

    biases = {}

    rows_go, rows_late = line_swap(go, 0), line_swap(late, 0)
    q_came = plane_swap(q_send, 0)
    w_sum = merge(place, w_keep, w_came)
    w_came = line_swap(w_sum, 1)
    q_came = fence(q_came)
    q_keep, q_send = fold(place, q_keep, q_came)
    q_came, w_came, stay, rows_go, rows_late = fence(
        (plane_swap(q_send, 1), w_came, stay, rows_go, rows_late)
    )
    for step in range(2, line_bits):
        w_sum = merge(place, w_sum, w_came)
        w_came = line_swap(w_sum, step)
    q_sum = merge(place, q_keep, q_came)
    q_came = line_swap(q_sum, 0)
    w_near, biases["w"] = last_sum(w_sum, w_came)
    w_far = line_swap(w_near, 0)
    near_one, near_two = plane_swap(w_near, 1), plane_swap(w_near, 0)
    self_grad = self_feature(place, grad_linear, w_weight, w_other)
    q_came, w_far, near_one, near_two, biases, self_grad = fence(
        (q_came, w_far, near_one, near_two, biases, self_grad)
    )
    for step in range(1, line_bits):
        q_sum = merge(place, q_sum, q_came)
        q_came = line_swap(q_sum, step)
    near_three = plane_swap(near_one, 0)
    far_one, far_two = plane_swap(w_far, 1), plane_swap(w_far, 0)
    q_came, near_three, far_one, far_two = fence((q_came, near_three, far_one, far_two))
    q_own, biases["q"] = last_sum(q_sum, q_came)
    half = stay.shape[0] // 2
    upper = (stay[half:].astype(F32) + rows_go.astype(F32)).astype(BF16)
    q_own, upper = fence((q_own, upper))
    rows_next = line_swap(upper, 1)
    q_one, q_two = plane_swap(q_own, 1), plane_swap(q_own, 0)
    far_three = plane_swap(far_one, 0)
    w_all = [w_near, w_far, near_one, far_one, near_two, far_two, near_three]
    w_part = unpack(
        place, w_all, [(0, at // 2, at % 2) for at in range(2 * PLANE - 1)], lines
    )
    bias_other = trade(biases["q"][None])
    q_one, q_two, far_three, rows_next, biases, w_part, bias_other = fence(
        (q_one, q_two, far_three, rows_next, biases, w_part, bias_other)
    )
    q_three = plane_swap(q_one, 0)
    w_grad = unpack(place, [far_three], [(0, 3, 1)], lines, 1, w_part)
    w_bias_grad, q_bias_half = biases["w"], biases["q"][None]

    stay = stay[: stay.shape[0] // 2]
    for step in range(2, line_bits):
        half = rows_late.shape[0] // 2
        upper = stay[half:].astype(F32) + rows_late[half:] + rows_next[half:]
        rows_next = (rows_next[:half] + line_swap(upper.astype(BF16), step).astype(F32)).astype(BF16)
        stay, rows_late = stay[:half], rows_late[:half]
    row_half = row_sums(place, stay, rows_late, rows_next)
    row_other = trade(row_half)
    q_mine = [q_own, q_one, q_two]
    q_other = [trade(block) for block in q_mine]
    feature_grad, q_bias_grad = feature_step(
        place, self_grad, row_half, row_other, q_weight, q_bias_half, bias_other
    )
    q_three, q_other, w_grad, q_bias_grad, feature_grad = fence(
        (q_three, q_other, w_grad, q_bias_grad, feature_grad)
    )
    last_other = trade(q_three)
    q_part = unpack(place, q_mine + [q_three], [(0, at, 0) for at in range(PLANE)], 0, 2)
    q_part, last_other = fence((q_part, last_other))
    q_grad = unpack(
        place, q_other + [last_other], [(1, at, 0) for at in range(PLANE)], 0, 2, q_part
    )
    return (embeddings, feature_grad, q_grad, q_bias_grad[0], w_grad, w_bias_grad)


def solution(mesh):
    in_specs = (
        P("nodes", None),
        P("nodes", "stream"),
        P("nodes", "stream"),
        P("nodes", "stream"),
        P(),
        P(),
        P("stream", None),
        P(),
        P("nodes", None),
    )
    out_specs = (P("nodes", None), P("nodes", "stream"), P(), P(), P("stream", None), P())
    return jax.shard_map(
        on_device, mesh=mesh, in_specs=in_specs, out_specs=out_specs, check_vma=False
    )
```

```python
import jax
import jax.numpy as jnp
from jax import lax
from jax.experimental import pallas as pl
from jax.experimental.pallas import tpu as pltpu
from jax.sharding import PartitionSpec as P

PLANE = 4
TILE = 16
PIECES = 2 * PLANE - 1
VMEM_BYTES = 48 * 1024 * 1024
ALL_VMEM = 67_000_000
F32, BF16, I32 = jnp.float32, jnp.bfloat16, jnp.int32


def across(lhs, rhs):
    return lax.dot_general(lhs, rhs, (((0,), (0,)), ((), ())), preferred_element_type=F32)


def times_t(lhs, rhs):
    return lax.dot_general(lhs, rhs, (((1,), (1,)), ((), ())), preferred_element_type=F32)


def aligned(start, size):
    start = start if isinstance(start, int) else pl.multiple_of(start, size)
    return pl.ds(start, size)


def spaced(space, arrays):
    return [pl.BlockSpec(memory_space=space) for _ in arrays]


def array(shape, dtype):
    return jax.ShapeDtypeStruct(shape, dtype)


def call(kernel, name, outs, place, near, far=(), scratch=(), flops=0, far_outs=0,
         limit=VMEM_BYTES, light=False, aliases={}):
    operands = list(near) + list(far)
    moved = sum(a.size * a.dtype.itemsize for a in operands + list(outs))
    if light:
        flops, moved = 1, 1
    return pl.pallas_call(
        kernel,
        name=name,
        out_shape=list(outs),
        in_specs=spaced(pltpu.SMEM, [place]) + spaced(pltpu.VMEM, near) + spaced(pltpu.HBM, far),
        out_specs=spaced(pltpu.VMEM, outs[: len(outs) - far_outs])
        + spaced(pltpu.HBM, outs[len(outs) - far_outs :]),
        scratch_shapes=list(scratch),
        input_output_aliases=aliases,
        compiler_params=pltpu.CompilerParams(vmem_limit_bytes=limit),
        cost_estimate=pl.CostEstimate(
            flops=int(flops), bytes_accessed=int(moved), transcendentals=0
        ),
    )(place, *operands)


def reversed_bits(value, bits):
    out = 0
    for bit in range(bits):
        out = out | (((value >> bit) & 1) << (bits - 1 - bit))
    return out


def away(core, slot, bits):
    return jnp.where(core == 0, reversed_bits(slot, bits), slot)


def bits_of(size):
    return size.bit_length() - 1


def line_side(place_ref, lines):
    line = place_ref[0] // PLANE
    return jnp.where(place_ref[1] == 0, line & 1, line // (lines // 2))


def bias_rows(value):
    top = value.astype(BF16).astype(F32)
    row_at = lax.broadcasted_iota(I32, (TILE, value.shape[1]), 0)
    return jnp.where(row_at == 0, top, jnp.where(row_at == 1, value - top, 0.0)).astype(BF16)


def stacked(parts, target, sem, first=0):
    copies, at = [], 0
    for index, part in enumerate(parts):
        span = pl.ds(at, part.shape[0])
        copies.append(pltpu.make_async_copy(part, target.at[span, :], sem.at[first + index]))
        at += part.shape[0]
    return copies


def line_copies(parts, target, sem):
    own, parts = parts[0], parts[1:]
    mine, other = parts[: len(parts) // 2], parts[len(parts) // 2 :]
    rows, bits = own.shape[0], len(mine)
    half = rows // 2
    copies = [pltpu.make_async_copy(own, target.at[pl.ds(0, rows), :], sem.at[0])]
    for slot in range(1, 1 << bits):
        for index, (stages, at) in enumerate(((mine, slot), (other, reversed_bits(slot, bits)))):
            stage = at.bit_length() - 1
            view = stages[stage].at[pl.ds((at - (1 << stage)) * half, half), :]
            spot = target.at[pl.ds(slot * rows + index * half, half), :]
            copies.append(pltpu.make_async_copy(view, spot, sem.at[2 * slot - 1 + index]))
    return copies


def start_all(copies):
    for copy in copies:
        copy.start()


def wait_all(copies):
    for copy in copies:
        copy.wait()


def sort_slots(place, neighbours, present, importance, count):
    rows, slots = neighbours.shape
    turns = -(-slots // count)
    arrays = [neighbours.T, present.T, importance.T]

    def kernel(place_ref, *refs):
        out_ref, neighbours_ref, present_ref, importance_ref, sem = refs[3:]
        copies = [
            pltpu.make_async_copy(part, target, sem.at[index])
            for index, (part, target) in enumerate(zip(refs[:3], refs[4:7]))
        ]
        start_all(copies)
        wait_all(copies)
        slot_at = lax.broadcasted_iota(I32, (slots, rows), 0)
        node_at = lax.broadcasted_iota(I32, (slots, rows), 1)
        block = (node_at * slots + slot_at) & (count - 1)
        row = neighbours_ref[...] - rows * block
        packed = row * 128 + present_ref[...] * importance_ref[...]
        block_at = lax.broadcasted_iota(I32, (count, rows), 0)
        node_at = lax.broadcasted_iota(I32, (count, rows), 1)
        first = (block_at - slots * node_at) & (count - 1)
        for turn in range(turns):
            total = jnp.zeros((count, rows), I32)
            for slot in range(slots):
                at = slot - count * turn
                if 0 <= at < count:
                    total = jnp.where(first == at, packed[slot : slot + 1, :], total)
            out_ref[turn * count : (turn + 1) * count, :] = total

    (out,) = call(
        kernel, "sort_slots", [array((turns * count, rows), I32)], place, [], arrays,
        [pltpu.VMEM((slots, rows), I32)] * 3 + [pltpu.SemaphoreType.DMA((3,))], limit=ALL_VMEM,
    )
    return out


def slot_matrix(place, lists, count):
    tall, rows = lists[0].shape
    lines, width, turns = count // PLANE, PLANE * rows, tall // count

    def kernel(place_ref, own_ref, next_ref, rest_ref, sums_ref, far_ref, out_ref, sem):
        slot_refs = [(own_ref, 0), (next_ref, 0), (rest_ref, 0), (rest_ref, tall)]
        core, spot, line = place_ref[1], place_ref[0] % PLANE, place_ref[0] // PLANE
        sums = [
            jnp.sum((ref[at : at + tall, :] & 127).astype(F32), axis=0, keepdims=True)
            for ref, at in slot_refs
        ]
        sums = jnp.broadcast_to(jnp.concatenate(sums, axis=1), (8, width))
        sums_ref[...] = sums.T
        for at in range(lines):
            block = (line ^ away(core, at, bits_of(lines))) * PLANE + spot
            ids, weights = [], []
            for turn in range(turns):
                listed = jnp.concatenate(
                    [ref[pl.ds(at + turn * count + block, 1), :] for ref, at in slot_refs],
                    axis=1,
                )
                ids.append(((listed >> 7) - rows // 2).astype(F32).astype(BF16))
                weights.append((listed & 127).astype(F32).astype(BF16))
            shift = core * (rows // 2) if at else 0

            @pl.loop(0, rows // TILE)
            def _(step):
                base = step * TILE + shift
                base = jnp.where(base >= rows, base - rows, base)
                row_at = lax.broadcasted_iota(I32, (TILE, width), 0) + (base - rows // 2)
                row_at = row_at.astype(F32).astype(BF16)
                zero = jnp.zeros((TILE, width), BF16)
                total = zero
                for listed, weight in zip(ids, weights):
                    total = total + jnp.where(listed == row_at, weight, zero)
                out_ref[aligned(at * rows + step * TILE, TILE), :] = total

            span = pl.ds(at * rows, rows)
            pltpu.make_async_copy(out_ref.at[span, :], far_ref.at[span, :], sem.at[at]).start()
        for at in range(lines):
            span = pl.ds(at * rows, rows)
            pltpu.make_async_copy(out_ref.at[span, :], far_ref.at[span, :], sem.at[at]).wait()

    sums, matrix = call(
        kernel, "slot_matrix", [array((width, 8), F32), array((lines * rows, width), BF16)],
        place, lists,
        scratch=[pltpu.VMEM((lines * rows, width), BF16), pltpu.SemaphoreType.DMA((lines,))],
        flops=3 * turns * lines * rows * width, far_outs=1, limit=ALL_VMEM, light=True,
    )
    return matrix, sums


def half_copy(core, q_in, q_ref, sem):
    half = q_ref.shape[1]
    return pltpu.make_async_copy(q_in.at[:, aligned(core * half, half)], q_ref, sem)


def hidden_of(core, rows, q_ref, bias_ref):
    half = q_ref.shape[1]
    bias = bias_ref[:, aligned(core * half, half)]
    hidden = jnp.maximum(jnp.dot(rows, q_ref[...], preferred_element_type=F32) + bias, 0.0)
    top = hidden.astype(BF16)
    return top, (hidden - top.astype(F32)).astype(BF16)


def lane_span(start, size):
    low = start // 128 * 128
    high = -(-(start + size) // 128) * 128
    return low, high - low, start - low


def first_sums(place, line_parts, q_weight, q_bias, matrix):
    rows, dim = line_parts[0].shape
    total, width = matrix.shape
    half, part, count = dim // 2, width // PLANE, len(line_parts)
    lines = total // rows
    low, span_width, skip = lane_span(width - part, part)

    def kernel(place_ref, bias_ref, q_in, matrix_in, *refs):
        parts, refs = refs[:count], refs[count:]
        send_ref, high_out, low_out, rows_ref, high_ref, low_ref, matrix_ref, q_ref = refs[:8]
        row_sem, sem = refs[8:]
        core = place_ref[1]
        q_copy = half_copy(core, q_in, q_ref, sem.at[0])
        matrix_copy = pltpu.make_async_copy(
            matrix_in.at[:, pl.ds(low, span_width)], matrix_ref, sem.at[1]
        )
        copies = line_copies(parts, rows_ref, row_sem)
        start_all([q_copy] + copies + [matrix_copy])
        q_copy.wait()
        for at in range(lines):
            wait_all(copies[max(2 * at - 1, 0) : 2 * at + 1])
            span = slice(at * rows, (at + 1) * rows)
            high_ref[span, :], low_ref[span, :] = hidden_of(
                core, rows_ref[span, :], q_ref, bias_ref
            )
        outs = [
            pltpu.make_async_copy(high_ref, high_out, sem.at[2]),
            pltpu.make_async_copy(low_ref, low_out, sem.at[3]),
        ]
        start_all(outs)
        matrix_copy.wait()
        total_sum = across(matrix_ref[...], high_ref[...]) + across(matrix_ref[...], low_ref[...])
        send_ref[...] = total_sum[skip : skip + part, :]
        wait_all(outs)

    return call(
        kernel, "first_sums",
        [array((part, half), F32)] + [array((total, half), BF16)] * 2,
        place, [q_bias], [q_weight, matrix] + list(line_parts),
        [
            pltpu.VMEM((total, dim), BF16),
            pltpu.VMEM((total, half), BF16),
            pltpu.VMEM((total, half), BF16),
            pltpu.VMEM((total, span_width), BF16),
            pltpu.VMEM((dim, half), BF16),
            pltpu.SemaphoreType.DMA((2 * lines - 1,)),
            pltpu.SemaphoreType.DMA((4,)),
        ],
        flops=2 * total * dim * half + 4 * total * part * half, far_outs=2, limit=ALL_VMEM,
    )


def more_sums(place, highs, lows, matrix, first, slots):
    total = matrix.shape[0]
    part = matrix.shape[1] // PLANE
    width = slots * part
    start, span_width, skip = lane_span(first * part, width)
    half, count = highs[0].shape[1], len(highs)

    def kernel(place_ref, matrix_in, *refs):
        parts, refs = refs[: 2 * count], refs[2 * count :]
        sum_refs, refs = refs[:slots], refs[slots:]
        high_ref, low_ref, matrix_ref, sem = refs
        copies = [
            pltpu.make_async_copy(
                matrix_in.at[:, pl.ds(start, span_width)], matrix_ref, sem.at[2 * count]
            )
        ]
        copies += stacked(parts[:count], high_ref, sem)
        copies += stacked(parts[count:], low_ref, sem, count)
        start_all(copies)
        wait_all(copies)
        total_sum = across(matrix_ref[...], high_ref[...]) + across(matrix_ref[...], low_ref[...])
        for slot, sum_ref in enumerate(sum_refs):
            at = skip + slot * part
            sum_ref[...] = total_sum[at : at + part, :]

    return call(
        kernel, "more_sums", [array((part, half), F32)] * slots, place, [],
        [matrix] + list(highs) + list(lows),
        [
            pltpu.VMEM((total, half), BF16),
            pltpu.VMEM((total, half), BF16),
            pltpu.VMEM((total, span_width), BF16),
            pltpu.SemaphoreType.DMA((2 * count + 1,)),
        ],
        flops=4 * total * width * half, limit=ALL_VMEM,
    )


def pick_copy(core, first, second, target, sem, rows=None):
    views = [ref if rows is None else ref.at[rows, :] for ref in (first, second)]
    for side, view in enumerate(views):

        @pl.when(core == side)
        def _():
            pltpu.make_async_copy(view, target, sem).start()

    return pltpu.make_async_copy(views[0], target, sem)


def self_product(place, features, w_weight, w_other, w_bias):
    rows, dim = features.shape

    def kernel(place_ref, features_ref, bias_ref, w_in, w_other_in, out_ref, w_ref, sem):
        pick_copy(place_ref[1], w_in, w_other_in, w_ref, sem).wait()
        out_ref[...] = bias_ref[...] + jnp.dot(
            features_ref[...], w_ref[...], preferred_element_type=F32
        )

    (out,) = call(
        kernel, "self_product", [array((rows, dim), F32)], place, [features, w_bias],
        [w_weight, w_other], [pltpu.VMEM((dim, dim), BF16), pltpu.SemaphoreType.DMA(())],
        flops=2 * rows * dim * dim,
    )
    return out


def row_sums(place, stay, late, come):
    rows, half = late.shape

    def kernel(place_ref, stay_ref, late_ref, come_ref, out_ref):
        for part in range(2):
            span = slice(part * rows // 2, (part + 1) * rows // 2)
            came = late_ref[span, :].astype(F32) + come_ref[span, :].astype(F32)
            at = aligned((place_ref[1] ^ part) * (rows // 2), rows // 2)
            out_ref[at, :] = (stay_ref[at, :].astype(F32) + came).astype(BF16)

    (out,) = call(kernel, "row_sums", [array((rows, half), BF16)], place, [stay, late, come])
    return out


def self_feature(place, grad_linear, w_weight, w_other):
    rows, dim = grad_linear.shape
    half = dim // 2

    def kernel(place_ref, grad_ref, w_in, w_other_in, out_ref, w_ref, sem):
        core = place_ref[1]
        pick_copy(core, w_in, w_other_in, w_ref, sem, aligned(core * half, half)).wait()
        out_ref[...] = times_t(grad_ref[...], w_ref[...])

    (out,) = call(
        kernel, "self_feature", [array((rows, half), F32)], place, [grad_linear],
        [w_weight, w_other], [pltpu.VMEM((half, dim), BF16), pltpu.SemaphoreType.DMA(())],
        flops=2 * rows * dim * half,
    )
    return out


def feature_step(place, self_grad, mine, other, q_weight, bias_mine, bias_other):
    rows, half = mine.shape
    dim = 2 * half

    def kernel(
        place_ref, self_ref, mine_ref, other_ref, bias_mine_ref, bias_other_ref, q_in,
        out_ref, bias_ref, q_ref, sem,
    ):
        core = place_ref[1]
        spans = [aligned(core * half, half), aligned((1 - core) * half, half)]
        q_copy = pltpu.make_async_copy(q_in.at[spans[0], :], q_ref, sem)
        q_copy.start()
        bias_ref[:, spans[0]] = bias_mine_ref[...]
        bias_ref[:, spans[1]] = bias_other_ref[...]
        q_copy.wait()
        out_ref[...] = (
            self_ref[...]
            + times_t(mine_ref[...], q_ref[:, spans[0]])
            + times_t(other_ref[...], q_ref[:, spans[1]])
        )

    return call(
        kernel, "feature_step", [array((rows, half), F32), array((1, dim), F32)], place,
        [self_grad, mine, other, bias_mine, bias_other], [q_weight],
        [pltpu.VMEM((half, dim), BF16), pltpu.SemaphoreType.DMA(())],
        flops=2 * rows * dim * half,
    )


def plane_slices(place, features, mine, other):
    rows, dim = features.shape
    half, width = dim // 2, dim // PLANE

    def kernel(place_ref, features_ref, mine_ref, other_ref, own_ref, next_ref, send_ref):
        core, spot = place_ref[1], place_ref[0] % PLANE
        targets = [own_ref, next_ref, send_ref.at[pl.ds(0, rows), :], send_ref.at[pl.ds(rows, rows), :]]
        for slot, target in enumerate(targets):
            to = spot ^ away(core, slot, 2)

            @pl.when(core == 0)
            def _():
                target[...] = features_ref[:, aligned(to * width, width)]

            within = aligned(to % 2 * width, width)

            @pl.when((core == 1) & (to < 2))
            def _():
                target[...] = other_ref[:, within]

            @pl.when((core == 1) & (to >= 2))
            def _():
                target[...] = mine_ref[:, within]

    outs = [array((rows, width), BF16)] * 2 + [array((2 * rows, width), BF16)]
    return call(kernel, "plane_slices", outs, place, [features, mine, other])


def node_step(place, mine, other, self_part, cotangent, w_weight, w_other):
    rows, half = mine.shape
    dim = 2 * half

    def kernel(
        place_ref, mine_ref, other_ref, self_ref, cotangent_ref, w_in, w_other_in,
        embeddings_ref, grad_ref, half_ref, lhs_ref, linear_ref, near_ref, sem,
    ):
        core = place_ref[1]
        near_copy = pick_copy(core, w_other_in, w_in, near_ref, sem)
        lhs_ref[:, aligned(core * half, half)] = mine_ref[...]
        lhs_ref[:, aligned((1 - core) * half, half)] = other_ref[...]
        near_copy.wait()
        linear_ref[...] = self_ref[...] + jnp.dot(
            lhs_ref[...], near_ref[...], preferred_element_type=F32
        )

        @pl.loop(0, rows // TILE, unroll=4)
        def _(step):
            at = aligned(step * TILE, TILE)
            linear = linear_ref[at, :]
            relu_out = jnp.maximum(linear, 0.0)
            scale = lax.rsqrt(jnp.mean(relu_out * relu_out, axis=1, keepdims=True) + 1e-06)
            embeddings_ref[at, :] = relu_out * scale
            grad_out = cotangent_ref[at, :].astype(F32)
            inner = jnp.mean(relu_out * grad_out, axis=1, keepdims=True)
            grad_relu = scale * grad_out - relu_out * (scale * scale * scale) * inner
            grad_ref[at, :] = jnp.where(linear > 0, grad_relu, 0.0).astype(BF16)

        half_ref[...] = grad_ref[aligned(core * (rows // 2), rows // 2), :]

    outs = [
        array((rows, dim), F32), array((rows, dim), BF16), array((rows // 2, dim), BF16),
    ]
    return call(
        kernel, "node_step", outs, place, [mine, other, self_part, cotangent],
        [w_weight, w_other],
        [
            pltpu.VMEM((rows, dim), BF16), pltpu.VMEM((rows, dim), F32),
            pltpu.VMEM((dim, dim), BF16), pltpu.SemaphoreType.DMA(()),
        ],
        flops=2 * rows * dim * dim,
    )


def plane_copies(core, rows, pieces, target, sem):
    own = pieces[0]
    half = rows // 2
    copies = [pltpu.make_async_copy(own, target.at[pl.ds(0, rows), :], sem.at[0])]
    for slot in range(1, PLANE):
        mine = pieces[slot]
        other = pieces[PLANE - 1 + reversed_bits(slot, 2)]
        for index, (part, at) in enumerate(((mine, core), (other, 1 - core))):
            spot = pl.multiple_of(slot * rows + at * half, TILE)
            copies.append(
                pltpu.make_async_copy(
                    part, target.at[pl.ds(spot, half), :], sem.at[2 * slot - 1 + index]
                )
            )
    return copies


def self_weight(place, pieces, slices, lines):
    rows, dim = pieces[0].shape
    width = slices[0].shape[1]

    def kernel(place_ref, *refs):
        parts, refs = refs[:PIECES], refs[PIECES:]
        slots, outs = refs[:4], refs[4:6]
        grads_ref, lhs_ref, sum_ref, sem, slice_sem = refs[6:]
        copies = plane_copies(place_ref[1], rows, parts, grads_ref, sem)
        own, far, near, last = slots
        spans = [own, last.at[pl.ds(0, rows), :], far.at[pl.ds(0, rows), :], last.at[pl.ds(rows, rows), :]]
        for slot, part in enumerate(spans):
            copies.append(
                pltpu.make_async_copy(part, lhs_ref.at[pl.ds(slot * rows, rows), :], slice_sem.at[slot])
            )
        for copy in copies:
            copy.start()
        for copy in copies:
            copy.wait()
        sum_ref[...] = across(lhs_ref[...], grads_ref[...])
        bias = bias_rows(jnp.sum(grads_ref[...].astype(F32), axis=0, keepdims=True))
        first = line_side(place_ref, lines)
        for slot, out_ref in enumerate(outs):
            out_ref[: width // 2, :] = sum_ref[
                aligned((first ^ slot) * (width // 2), width // 2), :
            ].astype(BF16)
            out_ref[width // 2 :, :] = bias

    return call(
        kernel, "self_weight", [array((width // 2 + TILE, dim), BF16)] * 2, place, [],
        list(pieces) + list(slices),
        [
            pltpu.VMEM((PLANE * rows, dim), BF16),
            pltpu.VMEM((PLANE * rows, width), BF16),
            pltpu.VMEM((width, dim), F32),
            pltpu.SemaphoreType.DMA((PIECES,)),
            pltpu.SemaphoreType.DMA((PLANE,)),
        ],
        flops=2 * PLANE * rows * dim * width,
    )


def row_grad(place, sums, pieces, w_weight, w_other, matrix, high, line_parts, lines):
    rows, dim = pieces[0].shape
    half = dim // 2
    total, nodes, width = lines * rows, PLANE * rows, dim // PLANE

    def kernel(place_ref, sums_ref, matrix_in, high_in, w_in, w_other_in, *refs):
        parts, refs = refs[:PIECES], refs[PIECES:]
        row_parts, refs = refs[: len(line_parts)], refs[len(line_parts) :]
        stay_ref, late_ref, go_ref, keep_ref, send_ref, refs = *refs[:5], refs[5:]
        grads_ref, rows_ref, sum_ref, hidden_ref, near_ref, matrix_ref, high_ref = refs[:7]
        sem, row_sem, near_sem, line_sem = refs[7:]
        core, spot = place_ref[1], place_ref[0] % PLANE
        copies = plane_copies(core, rows, parts, grads_ref, sem)
        row_copies = line_copies(row_parts, rows_ref, row_sem)
        near_copy = pick_copy(
            core, w_other_in, w_in, near_ref, near_sem, aligned(core * half, half)
        )
        line_sums = [
            pltpu.make_async_copy(matrix_in, matrix_ref, line_sem.at[0]),
            pltpu.make_async_copy(high_in, high_ref, line_sem.at[1]),
        ]
        start_all(copies + line_sums + row_copies)
        near_copy.wait()
        for slot in range(PLANE):
            wait_all(copies[max(2 * slot - 1, 0) : 2 * slot + 1])
            span = slice(slot * rows, (slot + 1) * rows)
            grad = times_t(grads_ref[span, :], near_ref[...])
            sum_ref[span, :] = (grad / sums_ref[span, 0:1]).astype(BF16)
        wait_all(line_sums)
        bias = jnp.zeros((1, half), F32)
        for at in range(lines):
            span = slice(at * rows, (at + 1) * rows)
            grad = jnp.dot(matrix_ref[span, :], sum_ref[...], preferred_element_type=F32)
            grad = jnp.where(high_ref[span, :].astype(F32) > 0, grad, 0.0)
            bias = bias + jnp.sum(grad, axis=0, keepdims=True)
            hidden_ref[span, :] = grad.astype(BF16)
        for slot in range(lines):
            at = to = slot * rows
            for ref in (stay_ref, late_ref, go_ref):
                if 0 <= to < ref.shape[0]:
                    break
                to -= ref.shape[0]
            ref[to : to + rows, :] = hidden_ref[at : at + rows, :]
        wait_all(row_copies)
        for slot in range(PLANE):
            to = spot ^ away(core, slot, 2)
            ref, at = (keep_ref, send_ref)[slot // 2], slot % 2 * width
            ref[at : at + width, :] = across(
                rows_ref[:, aligned(to * width, width)], hidden_ref[...]
            ).astype(BF16)
        for ref in (keep_ref, send_ref):
            ref[2 * width :, :] = bias_rows(bias)

    outs = [array((total // 2, half), BF16)] + [array((total // 4, half), BF16)] * 2
    outs += [array((dim // 2 + TILE, half), BF16)] * 2
    return call(
        kernel, "row_grad", outs, place, [sums],
        [matrix, high, w_weight, w_other] + list(pieces) + list(line_parts),
        [
            pltpu.VMEM((nodes, dim), BF16),
            pltpu.VMEM((total, dim), BF16),
            pltpu.VMEM((nodes, half), BF16),
            pltpu.VMEM((total, half), BF16),
            pltpu.VMEM((half, dim), BF16),
            pltpu.VMEM((total, nodes), BF16),
            pltpu.VMEM((total, half), BF16),
            pltpu.SemaphoreType.DMA((PIECES,)),
            pltpu.SemaphoreType.DMA((2 * lines - 1,)),
            pltpu.SemaphoreType.DMA(()),
            pltpu.SemaphoreType.DMA((2,)),
        ],
        flops=2 * nodes * dim * half + 2 * total * nodes * half + 2 * total * dim * half,
        limit=VMEM_BYTES if lines <= PLANE else ALL_VMEM,
    )


def fold(place, keep, came):
    height, width = keep.shape[0] - TILE, keep.shape[1]
    part = height // 2

    def kernel(place_ref, keep_ref, came_ref, stay_ref, go_ref):
        bias = keep_ref[height:, :].astype(F32) + came_ref[height:, :].astype(F32)
        bias = bias_rows(bias[0:1] + bias[1:2])
        for ref, at in ((stay_ref, 0), (go_ref, part)):
            span = slice(at, at + part)
            ref[:part, :] = (keep_ref[span, :].astype(F32) + came_ref[span, :].astype(F32)).astype(BF16)
            ref[part:, :] = bias

    return call(
        kernel, "fold", [array((part + TILE, width), BF16)] * 2, place, [keep, came]
    )


def merge(place, keep, came):
    height, width = keep.shape[0] - TILE, keep.shape[1]

    def kernel(place_ref, keep_ref, came_ref, out_ref):
        out_ref[...] = (keep_ref[...].astype(F32) + came_ref[...].astype(F32)).astype(BF16)
        bias = keep_ref[height:, :].astype(F32) + came_ref[height:, :].astype(F32)
        out_ref[height:, :] = bias_rows(bias[0:1] + bias[1:2])

    (out,) = call(kernel, "merge", [array(keep.shape, BF16)], place, [keep, came])
    return out


def unpack(place, blocks, spots, lines=0, sides=1, onto=None):
    parts = 2 if lines else 1
    height, width = blocks[0].shape
    count = len(blocks)

    def kernel(place_ref, *refs):
        sources, refs = refs[:count], refs[count + (onto is not None) :]
        out_ref, block_ref, wide_ref, sem, out_sem = refs
        spot = place_ref[0] % PLANE
        copies = [
            pltpu.make_async_copy(source, block_ref.at[index], sem.at[index])
            for index, source in enumerate(sources)
        ]
        start_all(copies)
        outs = []
        for index, copy in enumerate(copies):
            side, slot, at = spots[index]
            core = place_ref[1] ^ side
            row = (spot ^ away(core, slot, 2)) * parts
            if lines:
                row = row + (line_side(place_ref, lines) ^ at)
            cols = aligned(core * width, width) if sides > 1 else pl.ds(0, width)
            copy.wait()
            wide_ref[index] = block_ref[index].astype(F32)
            outs.append(
                pltpu.make_async_copy(
                    wide_ref.at[index], out_ref.at[aligned(row * height, height), cols],
                    out_sem.at[index],
                )
            )
            outs[-1].start()
        wait_all(outs)

    (out,) = call(
        kernel, "unpack", [array((PLANE * parts * height, width * sides), F32)], place, [],
        list(blocks) + ([] if onto is None else [onto]),
        [
            pltpu.VMEM((count, height, width), BF16), pltpu.VMEM((count, height, width), F32),
            pltpu.SemaphoreType.DMA((count,)), pltpu.SemaphoreType.DMA((count,)),
        ],
        far_outs=1, aliases={} if onto is None else {count + 1: 0},
    )
    return out


def on_device(
    features, neighbours, present, importance, q_weight, q_bias, w_weight, w_bias, cotangent
):
    rows, dim = features.shape
    count = lax.axis_size("nodes")
    lines = count // PLANE
    line_bits = bits_of(lines)
    node = lax.axis_index("nodes")
    core = lax.axis_index("stream")
    place = jnp.stack([node, core]).astype(I32)
    half_rows = rows // 2
    fence = lax.optimization_barrier

    def swap(value, bit, other_bit=None):
        bits = (bit, bit if other_bit is None else other_bit)
        pairs = [
            (2 * at + side, 2 * (at ^ bits[side]) + side) for at in range(count) for side in (0, 1)
        ]
        return lax.ppermute(value, ("nodes", "stream"), pairs)

    def plane_swap(value, step):
        return swap(value, 1 << step, 2 >> step)

    def line_swap(value, step):
        return swap(value, PLANE << step, PLANE << (line_bits - 1 - step))

    def trade(value):
        return lax.ppermute(value, "stream", [(0, 1), (1, 0)])

    def own_half(value, axis):
        size = value.shape[axis] // 2
        return lax.dynamic_slice_in_dim(value, core * size, size, axis)

    def joined(mine, other, axis):
        return jnp.where(
            core == 0,
            jnp.concatenate([mine, other], axis),
            jnp.concatenate([other, mine], axis),
        )

    mine = own_half(features, 0)
    stages = [line_swap(mine, line_bits - 1)]
    lists = sort_slots(place, neighbours, present, importance, count)
    lists = [jnp.concatenate([lists, trade(lists)], 0)]
    lists.append(plane_swap(lists[0], 1))
    lists[1], stages[0] = fence((lists[1], stages[0]))
    for step in reversed(range(line_bits - 1)):
        stages.append(line_swap(jnp.concatenate([mine] + stages, 0), step))
    lists.append(plane_swap(jnp.concatenate(lists, 0), 0))
    traded = [trade(stage) for stage in stages[:-1]]
    matrix, weight_sums = slot_matrix(place, lists, count)
    matrix, stages[-1], traded = fence((matrix, stages[-1], traded))
    line_parts = [features] + stages + traded + [trade(stages[-1])]
    send, high, low = first_sums(place, line_parts, q_weight, q_bias[None], matrix)
    send, w_sent = fence((send, w_weight))
    w_other = trade(w_sent)

    came = plane_swap(send, 0)
    keep, middle, own_send = more_sums(place, [high], [low], matrix, 0, 3)
    came_own = plane_swap(own_send, 0)
    last = plane_swap(middle + came, 1)
    self_part = self_product(place, features, w_weight, w_other, w_bias[None])
    came_own, self_part, keep, weight_sum = fence((came_own, self_part, keep, weight_sums[:rows, 0]))
    mean_half = ((keep + came_own + last) / weight_sum[:, None]).astype(BF16)

    mean_other = trade(mean_half)
    own_slice, next_slice, send_slices = plane_slices(place, features, mean_half, mean_other)
    far_slices = plane_swap(send_slices, 0)
    embeddings, grad_linear, grad_half = node_step(
        place, mean_half, mean_other, self_part, cotangent, w_weight, w_other
    )

    one, two = plane_swap(grad_half, 1), plane_swap(grad_half, 0)
    last_slices = plane_swap(jnp.concatenate([next_slice, far_slices[rows:]], 0), 1)
    one = fence(one)
    three = plane_swap(one, 0)
    three, last_slices = fence((three, last_slices))
    pieces = [grad_linear, one, two, three, trade(one), trade(two), trade(three)]
    slices = [own_slice, far_slices, next_slice, last_slices]
    w_keep, w_send = self_weight(place, pieces, slices, lines)
    pieces, w_keep, w_send = fence((pieces, w_keep, w_send))

    stay, late, go, q_keep, q_send = row_grad(
        place, weight_sums, pieces, w_weight, w_other, matrix, high, line_parts, lines
    )
    w_came = line_swap(w_send, 0)
    stay, late, go, q_keep, q_send, w_keep, w_came = fence(
        (stay, late, go, q_keep, q_send, w_keep, w_came)
    )

    def last_sum(keep, came):
        height = keep.shape[0] - TILE
        total = keep.astype(F32) + came.astype(F32)
        return total[:height].astype(BF16), total[height] + total[height + 1]

    biases = {}

    rows_go, rows_late = line_swap(go, 0), line_swap(late, 0)
    q_came = plane_swap(q_send, 0)
    w_sum = merge(place, w_keep, w_came)
    w_came = line_swap(w_sum, 1)
    q_came = fence(q_came)
    q_keep, q_send = fold(place, q_keep, q_came)
    q_came, w_came, stay, rows_go, rows_late = fence(
        (plane_swap(q_send, 1), w_came, stay, rows_go, rows_late)
    )
    for step in range(2, line_bits):
        w_sum = merge(place, w_sum, w_came)
        w_came = line_swap(w_sum, step)
    q_sum = merge(place, q_keep, q_came)
    q_came = line_swap(q_sum, 0)
    w_near, biases["w"] = last_sum(w_sum, w_came)
    w_far = line_swap(w_near, 0)
    near_one, near_two = plane_swap(w_near, 1), plane_swap(w_near, 0)
    self_grad = self_feature(place, grad_linear, w_weight, w_other)
    q_came, w_far, near_one, near_two, biases, self_grad = fence(
        (q_came, w_far, near_one, near_two, biases, self_grad)
    )
    for step in range(1, line_bits):
        q_sum = merge(place, q_sum, q_came)
        q_came = line_swap(q_sum, step)
    near_three = plane_swap(near_one, 0)
    far_one, far_two = plane_swap(w_far, 1), plane_swap(w_far, 0)
    q_came, near_three, far_one, far_two = fence((q_came, near_three, far_one, far_two))
    q_own, biases["q"] = last_sum(q_sum, q_came)
    half = stay.shape[0] // 2
    upper = (stay[half:].astype(F32) + rows_go.astype(F32)).astype(BF16)
    q_own, upper = fence((q_own, upper))
    rows_next = line_swap(upper, 1)
    q_one, q_two = plane_swap(q_own, 1), plane_swap(q_own, 0)
    far_three = plane_swap(far_one, 0)
    w_all = [w_near, w_far, near_one, far_one, near_two, far_two, near_three]
    w_part = unpack(
        place, w_all, [(0, at // 2, at % 2) for at in range(2 * PLANE - 1)], lines
    )
    bias_other = trade(biases["q"][None])
    q_one, far_three, rows_next, biases, w_part, bias_other = fence(
        (q_one, far_three, rows_next, biases, w_part, bias_other)
    )
    q_three = plane_swap(q_one, 0)
    w_grad = unpack(place, [far_three], [(0, 3, 1)], lines, 1, w_part)
    w_bias_grad, q_bias_half = biases["w"], biases["q"][None]

    stay = stay[: stay.shape[0] // 2]
    for step in range(2, line_bits):
        half = rows_late.shape[0] // 2
        upper = stay[half:].astype(F32) + rows_late[half:] + rows_next[half:]
        rows_next = (rows_next[:half] + line_swap(upper.astype(BF16), step).astype(F32)).astype(BF16)
        stay, rows_late = stay[:half], rows_late[:half]
    row_half = row_sums(place, stay, rows_late, rows_next)
    row_other = trade(row_half)
    q_mine = [q_own, q_one, q_two]
    q_other = [trade(block) for block in q_mine]
    feature_grad, q_bias_grad = feature_step(
        place, self_grad, row_half, row_other, q_weight, q_bias_half, bias_other
    )
    q_three, q_other, w_grad, q_bias_grad, feature_grad = fence(
        (q_three, q_other, w_grad, q_bias_grad, feature_grad)
    )
    last_other = trade(q_three)
    q_part = unpack(place, q_mine + [q_three], [(0, at, 0) for at in range(PLANE)], 0, 2)
    q_part, last_other = fence((q_part, last_other))
    q_grad = unpack(
        place, q_other + [last_other], [(1, at, 0) for at in range(PLANE)], 0, 2, q_part
    )
    return (embeddings, feature_grad, q_grad, q_bias_grad[0], w_grad, w_bias_grad)


def solution(mesh):
    in_specs = (
        P("nodes", None),
        P("nodes", "stream"),
        P("nodes", "stream"),
        P("nodes", "stream"),
        P(),
        P(),
        P("stream", None),
        P(),
        P("nodes", None),
    )
    out_specs = (P("nodes", None), P("nodes", "stream"), P(), P(), P("stream", None), P())
    return jax.shard_map(
        on_device, mesh=mesh, in_specs=in_specs, out_specs=out_specs, check_vma=False
    )
```

```python
import jax
import jax.numpy as jnp
from jax import lax
from jax.experimental import pallas as pl
from jax.experimental.pallas import tpu as pltpu
from jax.sharding import PartitionSpec as P

PLANE = 4
TILE = 16
PIECES = 2 * PLANE - 1
VMEM_BYTES = 48 * 1024 * 1024
ALL_VMEM = 67_000_000
F32, BF16, I32 = jnp.float32, jnp.bfloat16, jnp.int32


def across(lhs, rhs):
    return lax.dot_general(lhs, rhs, (((0,), (0,)), ((), ())), preferred_element_type=F32)


def times_t(lhs, rhs):
    return lax.dot_general(lhs, rhs, (((1,), (1,)), ((), ())), preferred_element_type=F32)


def aligned(start, size):
    start = start if isinstance(start, int) else pl.multiple_of(start, size)
    return pl.ds(start, size)


def spaced(space, arrays):
    return [pl.BlockSpec(memory_space=space) for _ in arrays]


def array(shape, dtype):
    return jax.ShapeDtypeStruct(shape, dtype)


def call(kernel, name, outs, place, near, far=(), scratch=(), flops=0, far_outs=0,
         limit=VMEM_BYTES, light=False, aliases={}):
    operands = list(near) + list(far)
    moved = sum(a.size * a.dtype.itemsize for a in operands + list(outs))
    if light:
        flops, moved = 1, 1
    return pl.pallas_call(
        kernel,
        name=name,
        out_shape=list(outs),
        in_specs=spaced(pltpu.SMEM, [place]) + spaced(pltpu.VMEM, near) + spaced(pltpu.HBM, far),
        out_specs=spaced(pltpu.VMEM, outs[: len(outs) - far_outs])
        + spaced(pltpu.HBM, outs[len(outs) - far_outs :]),
        scratch_shapes=list(scratch),
        input_output_aliases=aliases,
        compiler_params=pltpu.CompilerParams(vmem_limit_bytes=limit),
        cost_estimate=pl.CostEstimate(
            flops=int(flops), bytes_accessed=int(moved), transcendentals=0
        ),
    )(place, *operands)


def reversed_bits(value, bits):
    out = 0
    for bit in range(bits):
        out = out | (((value >> bit) & 1) << (bits - 1 - bit))
    return out


def away(core, slot, bits):
    return jnp.where(core == 0, reversed_bits(slot, bits), slot)


def bits_of(size):
    return size.bit_length() - 1


def line_side(place_ref, lines):
    line = place_ref[0] // PLANE
    return jnp.where(place_ref[1] == 0, line & 1, line // (lines // 2))


def bias_rows(value):
    top = value.astype(BF16).astype(F32)
    row_at = lax.broadcasted_iota(I32, (TILE, value.shape[1]), 0)
    return jnp.where(row_at == 0, top, jnp.where(row_at == 1, value - top, 0.0)).astype(BF16)


def stacked(parts, target, sem, first=0):
    copies, at = [], 0
    for index, part in enumerate(parts):
        span = pl.ds(at, part.shape[0])
        copies.append(pltpu.make_async_copy(part, target.at[span, :], sem.at[first + index]))
        at += part.shape[0]
    return copies


def line_copies(parts, target, sem):
    own, parts = parts[0], parts[1:]
    mine, other = parts[: len(parts) // 2], parts[len(parts) // 2 :]
    rows, bits = own.shape[0], len(mine)
    half = rows // 2
    copies = [pltpu.make_async_copy(own, target.at[pl.ds(0, rows), :], sem.at[0])]
    for slot in range(1, 1 << bits):
        for index, (stages, at) in enumerate(((mine, slot), (other, reversed_bits(slot, bits)))):
            stage = at.bit_length() - 1
            view = stages[stage].at[pl.ds((at - (1 << stage)) * half, half), :]
            spot = target.at[pl.ds(slot * rows + index * half, half), :]
            copies.append(pltpu.make_async_copy(view, spot, sem.at[2 * slot - 1 + index]))
    return copies


def start_all(copies):
    for copy in copies:
        copy.start()


def wait_all(copies):
    for copy in copies:
        copy.wait()


def sort_slots(place, neighbours, present, importance, count):
    rows, slots = neighbours.shape
    turns = -(-slots // count)
    arrays = [neighbours.T, present.T, importance.T]

    def kernel(place_ref, *refs):
        out_ref, neighbours_ref, present_ref, importance_ref, sem = refs[3:]
        copies = [
            pltpu.make_async_copy(part, target, sem.at[index])
            for index, (part, target) in enumerate(zip(refs[:3], refs[4:7]))
        ]
        start_all(copies)
        wait_all(copies)
        slot_at = lax.broadcasted_iota(I32, (slots, rows), 0)
        node_at = lax.broadcasted_iota(I32, (slots, rows), 1)
        block = (node_at * slots + slot_at) & (count - 1)
        row = neighbours_ref[...] - rows * block
        packed = row * 128 + present_ref[...] * importance_ref[...]
        block_at = lax.broadcasted_iota(I32, (count, rows), 0)
        node_at = lax.broadcasted_iota(I32, (count, rows), 1)
        first = (block_at - slots * node_at) & (count - 1)
        for turn in range(turns):
            total = jnp.zeros((count, rows), I32)
            for slot in range(slots):
                at = slot - count * turn
                if 0 <= at < count:
                    total = jnp.where(first == at, packed[slot : slot + 1, :], total)
            out_ref[turn * count : (turn + 1) * count, :] = total

    (out,) = call(
        kernel, "sort_slots", [array((turns * count, rows), I32)], place, [], arrays,
        [pltpu.VMEM((slots, rows), I32)] * 3 + [pltpu.SemaphoreType.DMA((3,))], limit=ALL_VMEM,
    )
    return out


def slot_matrix(place, lists, count):
    tall, rows = lists[0].shape
    lines, width, turns = count // PLANE, PLANE * rows, tall // count

    def kernel(place_ref, own_ref, next_ref, rest_ref, sums_ref, far_ref, out_ref, sem):
        slot_refs = [(own_ref, 0), (next_ref, 0), (rest_ref, 0), (rest_ref, tall)]
        core, spot, line = place_ref[1], place_ref[0] % PLANE, place_ref[0] // PLANE
        sums = [
            jnp.sum((ref[at : at + tall, :] & 127).astype(F32), axis=0, keepdims=True)
            for ref, at in slot_refs
        ]
        sums = jnp.broadcast_to(jnp.concatenate(sums, axis=1), (8, width))
        sums_ref[...] = sums.T
        for at in range(lines):
            block = (line ^ away(core, at, bits_of(lines))) * PLANE + spot
            ids, weights = [], []
            for turn in range(turns):
                listed = jnp.concatenate(
                    [ref[pl.ds(at + turn * count + block, 1), :] for ref, at in slot_refs],
                    axis=1,
                )
                ids.append(((listed >> 7) - rows // 2).astype(F32).astype(BF16))
                weights.append((listed & 127).astype(F32).astype(BF16))
            shift = core * (rows // 2) if at else 0

            @pl.loop(0, rows // TILE)
            def _(step):
                base = step * TILE + shift
                base = jnp.where(base >= rows, base - rows, base)
                row_at = lax.broadcasted_iota(I32, (TILE, width), 0) + (base - rows // 2)
                row_at = row_at.astype(F32).astype(BF16)
                zero = jnp.zeros((TILE, width), BF16)
                total = zero
                for listed, weight in zip(ids, weights):
                    total = total + jnp.where(listed == row_at, weight, zero)
                out_ref[aligned(at * rows + step * TILE, TILE), :] = total

            span = pl.ds(at * rows, rows)
            pltpu.make_async_copy(out_ref.at[span, :], far_ref.at[span, :], sem.at[at]).start()
        for at in range(lines):
            span = pl.ds(at * rows, rows)
            pltpu.make_async_copy(out_ref.at[span, :], far_ref.at[span, :], sem.at[at]).wait()

    sums, matrix = call(
        kernel, "slot_matrix", [array((width, 8), F32), array((lines * rows, width), BF16)],
        place, lists,
        scratch=[pltpu.VMEM((lines * rows, width), BF16), pltpu.SemaphoreType.DMA((lines,))],
        flops=3 * turns * lines * rows * width, far_outs=1, limit=ALL_VMEM, light=True,
    )
    return matrix, sums


def half_copy(core, q_in, q_ref, sem):
    half = q_ref.shape[1]
    return pltpu.make_async_copy(q_in.at[:, aligned(core * half, half)], q_ref, sem)


def hidden_of(core, rows, q_ref, bias_ref):
    half = q_ref.shape[1]
    bias = bias_ref[:, aligned(core * half, half)]
    hidden = jnp.maximum(jnp.dot(rows, q_ref[...], preferred_element_type=F32) + bias, 0.0)
    top = hidden.astype(BF16)
    return top, (hidden - top.astype(F32)).astype(BF16)


def lane_span(start, size):
    low = start // 128 * 128
    high = -(-(start + size) // 128) * 128
    return low, high - low, start - low


def first_sums(place, line_parts, q_weight, q_bias, matrix):
    rows, dim = line_parts[0].shape
    total, width = matrix.shape
    half, part, count = dim // 2, width // PLANE, len(line_parts)
    lines = total // rows
    low, span_width, skip = lane_span(width - part, part)

    def kernel(place_ref, bias_ref, q_in, matrix_in, *refs):
        parts, refs = refs[:count], refs[count:]
        send_ref, high_out, low_out, rows_ref, high_ref, low_ref, matrix_ref, q_ref = refs[:8]
        row_sem, sem = refs[8:]
        core = place_ref[1]
        q_copy = half_copy(core, q_in, q_ref, sem.at[0])
        matrix_copy = pltpu.make_async_copy(
            matrix_in.at[:, pl.ds(low, span_width)], matrix_ref, sem.at[1]
        )
        copies = line_copies(parts, rows_ref, row_sem)
        start_all([q_copy] + copies + [matrix_copy])
        q_copy.wait()
        for at in range(lines):
            wait_all(copies[max(2 * at - 1, 0) : 2 * at + 1])
            span = slice(at * rows, (at + 1) * rows)
            high_ref[span, :], low_ref[span, :] = hidden_of(
                core, rows_ref[span, :], q_ref, bias_ref
            )
        outs = [
            pltpu.make_async_copy(high_ref, high_out, sem.at[2]),
            pltpu.make_async_copy(low_ref, low_out, sem.at[3]),
        ]
        start_all(outs)
        matrix_copy.wait()
        total_sum = across(matrix_ref[...], high_ref[...]) + across(matrix_ref[...], low_ref[...])
        send_ref[...] = total_sum[skip : skip + part, :]
        wait_all(outs)

    return call(
        kernel, "first_sums",
        [array((part, half), F32)] + [array((total, half), BF16)] * 2,
        place, [q_bias], [q_weight, matrix] + list(line_parts),
        [
            pltpu.VMEM((total, dim), BF16),
            pltpu.VMEM((total, half), BF16),
            pltpu.VMEM((total, half), BF16),
            pltpu.VMEM((total, span_width), BF16),
            pltpu.VMEM((dim, half), BF16),
            pltpu.SemaphoreType.DMA((2 * lines - 1,)),
            pltpu.SemaphoreType.DMA((4,)),
        ],
        flops=2 * total * dim * half + 4 * total * part * half, far_outs=2, limit=ALL_VMEM,
    )


def more_sums(place, highs, lows, matrix, first, slots):
    total = matrix.shape[0]
    part = matrix.shape[1] // PLANE
    width = slots * part
    start, span_width, skip = lane_span(first * part, width)
    half, count = highs[0].shape[1], len(highs)

    def kernel(place_ref, matrix_in, *refs):
        parts, refs = refs[: 2 * count], refs[2 * count :]
        sum_refs, refs = refs[:slots], refs[slots:]
        high_ref, low_ref, matrix_ref, sem = refs
        copies = [
            pltpu.make_async_copy(
                matrix_in.at[:, pl.ds(start, span_width)], matrix_ref, sem.at[2 * count]
            )
        ]
        copies += stacked(parts[:count], high_ref, sem)
        copies += stacked(parts[count:], low_ref, sem, count)
        start_all(copies)
        wait_all(copies)
        total_sum = across(matrix_ref[...], high_ref[...]) + across(matrix_ref[...], low_ref[...])
        for slot, sum_ref in enumerate(sum_refs):
            at = skip + slot * part
            sum_ref[...] = total_sum[at : at + part, :]

    return call(
        kernel, "more_sums", [array((part, half), F32)] * slots, place, [],
        [matrix] + list(highs) + list(lows),
        [
            pltpu.VMEM((total, half), BF16),
            pltpu.VMEM((total, half), BF16),
            pltpu.VMEM((total, span_width), BF16),
            pltpu.SemaphoreType.DMA((2 * count + 1,)),
        ],
        flops=4 * total * width * half, limit=ALL_VMEM,
    )


def pick_copy(core, first, second, target, sem, rows=None):
    views = [ref if rows is None else ref.at[rows, :] for ref in (first, second)]
    for side, view in enumerate(views):

        @pl.when(core == side)
        def _():
            pltpu.make_async_copy(view, target, sem).start()

    return pltpu.make_async_copy(views[0], target, sem)


def self_product(place, features, w_weight, w_other, w_bias):
    rows, dim = features.shape

    def kernel(place_ref, features_ref, bias_ref, w_in, w_other_in, out_ref, w_ref, sem):
        pick_copy(place_ref[1], w_in, w_other_in, w_ref, sem).wait()
        out_ref[...] = bias_ref[...] + jnp.dot(
            features_ref[...], w_ref[...], preferred_element_type=F32
        )

    (out,) = call(
        kernel, "self_product", [array((rows, dim), F32)], place, [features, w_bias],
        [w_weight, w_other], [pltpu.VMEM((dim, dim), BF16), pltpu.SemaphoreType.DMA(())],
        flops=2 * rows * dim * dim,
    )
    return out


def row_sums(place, stay, late, come):
    rows, half = late.shape

    def kernel(place_ref, stay_ref, late_ref, come_ref, out_ref):
        for part in range(2):
            span = slice(part * rows // 2, (part + 1) * rows // 2)
            came = late_ref[span, :].astype(F32) + come_ref[span, :].astype(F32)
            at = aligned((place_ref[1] ^ part) * (rows // 2), rows // 2)
            out_ref[at, :] = (stay_ref[at, :].astype(F32) + came).astype(BF16)

    (out,) = call(kernel, "row_sums", [array((rows, half), BF16)], place, [stay, late, come])
    return out


def self_feature(place, grad_linear, w_weight, w_other):
    rows, dim = grad_linear.shape
    half = dim // 2

    def kernel(place_ref, grad_ref, w_in, w_other_in, out_ref, w_ref, sem):
        core = place_ref[1]
        pick_copy(core, w_in, w_other_in, w_ref, sem, aligned(core * half, half)).wait()
        out_ref[...] = times_t(grad_ref[...], w_ref[...])

    (out,) = call(
        kernel, "self_feature", [array((rows, half), F32)], place, [grad_linear],
        [w_weight, w_other], [pltpu.VMEM((half, dim), BF16), pltpu.SemaphoreType.DMA(())],
        flops=2 * rows * dim * half,
    )
    return out


def feature_step(place, self_grad, mine, other, q_weight, bias_mine, bias_other):
    rows, half = mine.shape
    dim = 2 * half

    def kernel(
        place_ref, self_ref, mine_ref, other_ref, bias_mine_ref, bias_other_ref, q_in,
        out_ref, bias_ref, q_ref, sem,
    ):
        core = place_ref[1]
        spans = [aligned(core * half, half), aligned((1 - core) * half, half)]
        q_copy = pltpu.make_async_copy(q_in.at[spans[0], :], q_ref, sem)
        q_copy.start()
        bias_ref[:, spans[0]] = bias_mine_ref[...]
        bias_ref[:, spans[1]] = bias_other_ref[...]
        q_copy.wait()
        out_ref[...] = (
            self_ref[...]
            + times_t(mine_ref[...], q_ref[:, spans[0]])
            + times_t(other_ref[...], q_ref[:, spans[1]])
        )

    return call(
        kernel, "feature_step", [array((rows, half), F32), array((1, dim), F32)], place,
        [self_grad, mine, other, bias_mine, bias_other], [q_weight],
        [pltpu.VMEM((half, dim), BF16), pltpu.SemaphoreType.DMA(())],
        flops=2 * rows * dim * half,
    )


def plane_slices(place, features, mine, other):
    rows, dim = features.shape
    half, width = dim // 2, dim // PLANE

    def kernel(place_ref, features_ref, mine_ref, other_ref, own_ref, next_ref, send_ref):
        core, spot = place_ref[1], place_ref[0] % PLANE
        targets = [own_ref, next_ref, send_ref.at[pl.ds(0, rows), :], send_ref.at[pl.ds(rows, rows), :]]
        for slot, target in enumerate(targets):
            to = spot ^ away(core, slot, 2)

            @pl.when(core == 0)
            def _():
                target[...] = features_ref[:, aligned(to * width, width)]

            within = aligned(to % 2 * width, width)

            @pl.when((core == 1) & (to < 2))
            def _():
                target[...] = other_ref[:, within]

            @pl.when((core == 1) & (to >= 2))
            def _():
                target[...] = mine_ref[:, within]

    outs = [array((rows, width), BF16)] * 2 + [array((2 * rows, width), BF16)]
    return call(kernel, "plane_slices", outs, place, [features, mine, other])


def node_step(place, mine, other, self_part, cotangent, w_weight, w_other):
    rows, half = mine.shape
    dim = 2 * half

    def kernel(
        place_ref, mine_ref, other_ref, self_ref, cotangent_ref, w_in, w_other_in,
        embeddings_ref, grad_ref, half_ref, lhs_ref, linear_ref, near_ref, sem,
    ):
        core = place_ref[1]
        near_copy = pick_copy(core, w_other_in, w_in, near_ref, sem)
        lhs_ref[:, aligned(core * half, half)] = mine_ref[...]
        lhs_ref[:, aligned((1 - core) * half, half)] = other_ref[...]
        near_copy.wait()
        linear_ref[...] = self_ref[...] + jnp.dot(
            lhs_ref[...], near_ref[...], preferred_element_type=F32
        )

        @pl.loop(0, rows // TILE, unroll=4)
        def _(step):
            at = aligned(step * TILE, TILE)
            linear = linear_ref[at, :]
            relu_out = jnp.maximum(linear, 0.0)
            scale = lax.rsqrt(jnp.mean(relu_out * relu_out, axis=1, keepdims=True) + 1e-06)
            embeddings_ref[at, :] = relu_out * scale
            grad_out = cotangent_ref[at, :].astype(F32)
            inner = jnp.mean(relu_out * grad_out, axis=1, keepdims=True)
            grad_relu = scale * grad_out - relu_out * (scale * scale * scale) * inner
            grad_ref[at, :] = jnp.where(linear > 0, grad_relu, 0.0).astype(BF16)

        half_ref[...] = grad_ref[aligned(core * (rows // 2), rows // 2), :]

    outs = [
        array((rows, dim), F32), array((rows, dim), BF16), array((rows // 2, dim), BF16),
    ]
    return call(
        kernel, "node_step", outs, place, [mine, other, self_part, cotangent],
        [w_weight, w_other],
        [
            pltpu.VMEM((rows, dim), BF16), pltpu.VMEM((rows, dim), F32),
            pltpu.VMEM((dim, dim), BF16), pltpu.SemaphoreType.DMA(()),
        ],
        flops=2 * rows * dim * dim,
    )


def plane_copies(core, rows, pieces, target, sem):
    own = pieces[0]
    half = rows // 2
    copies = [pltpu.make_async_copy(own, target.at[pl.ds(0, rows), :], sem.at[0])]
    for slot in range(1, PLANE):
        mine = pieces[slot]
        other = pieces[PLANE - 1 + reversed_bits(slot, 2)]
        for index, (part, at) in enumerate(((mine, core), (other, 1 - core))):
            spot = pl.multiple_of(slot * rows + at * half, TILE)
            copies.append(
                pltpu.make_async_copy(
                    part, target.at[pl.ds(spot, half), :], sem.at[2 * slot - 1 + index]
                )
            )
    return copies


def self_weight(place, pieces, slices, lines):
    rows, dim = pieces[0].shape
    width = slices[0].shape[1]

    def kernel(place_ref, *refs):
        parts, refs = refs[:PIECES], refs[PIECES:]
        slots, outs = refs[:4], refs[4:6]
        grads_ref, lhs_ref, sum_ref, sem, slice_sem = refs[6:]
        copies = plane_copies(place_ref[1], rows, parts, grads_ref, sem)
        own, far, near, last = slots
        spans = [own, last.at[pl.ds(0, rows), :], far.at[pl.ds(0, rows), :], last.at[pl.ds(rows, rows), :]]
        for slot, part in enumerate(spans):
            copies.append(
                pltpu.make_async_copy(part, lhs_ref.at[pl.ds(slot * rows, rows), :], slice_sem.at[slot])
            )
        for copy in copies:
            copy.start()
        for copy in copies:
            copy.wait()
        sum_ref[...] = across(lhs_ref[...], grads_ref[...])
        bias = bias_rows(jnp.sum(grads_ref[...].astype(F32), axis=0, keepdims=True))
        first = line_side(place_ref, lines)
        for slot, out_ref in enumerate(outs):
            out_ref[: width // 2, :] = sum_ref[
                aligned((first ^ slot) * (width // 2), width // 2), :
            ].astype(BF16)
            out_ref[width // 2 :, :] = bias

    return call(
        kernel, "self_weight", [array((width // 2 + TILE, dim), BF16)] * 2, place, [],
        list(pieces) + list(slices),
        [
            pltpu.VMEM((PLANE * rows, dim), BF16),
            pltpu.VMEM((PLANE * rows, width), BF16),
            pltpu.VMEM((width, dim), F32),
            pltpu.SemaphoreType.DMA((PIECES,)),
            pltpu.SemaphoreType.DMA((PLANE,)),
        ],
        flops=2 * PLANE * rows * dim * width,
    )


def row_grad(place, sums, pieces, w_weight, w_other, matrix, high, line_parts, lines):
    rows, dim = pieces[0].shape
    half = dim // 2
    total, nodes, width = lines * rows, PLANE * rows, dim // PLANE

    def kernel(place_ref, sums_ref, matrix_in, high_in, w_in, w_other_in, *refs):
        parts, refs = refs[:PIECES], refs[PIECES:]
        row_parts, refs = refs[: len(line_parts)], refs[len(line_parts) :]
        stay_ref, late_ref, go_ref, keep_ref, send_ref, refs = *refs[:5], refs[5:]
        grads_ref, rows_ref, sum_ref, hidden_ref, near_ref, matrix_ref, high_ref = refs[:7]
        sem, row_sem, near_sem, line_sem = refs[7:]
        core, spot = place_ref[1], place_ref[0] % PLANE
        copies = plane_copies(core, rows, parts, grads_ref, sem)
        row_copies = line_copies(row_parts, rows_ref, row_sem)
        near_copy = pick_copy(
            core, w_other_in, w_in, near_ref, near_sem, aligned(core * half, half)
        )
        line_sums = [
            pltpu.make_async_copy(matrix_in, matrix_ref, line_sem.at[0]),
            pltpu.make_async_copy(high_in, high_ref, line_sem.at[1]),
        ]
        start_all(copies + line_sums + row_copies)
        near_copy.wait()
        for slot in range(PLANE):
            wait_all(copies[max(2 * slot - 1, 0) : 2 * slot + 1])
            span = slice(slot * rows, (slot + 1) * rows)
            grad = times_t(grads_ref[span, :], near_ref[...])
            sum_ref[span, :] = (grad / sums_ref[span, 0:1]).astype(BF16)
        wait_all(line_sums)
        bias = jnp.zeros((1, half), F32)
        for at in range(lines):
            span = slice(at * rows, (at + 1) * rows)
            grad = jnp.dot(matrix_ref[span, :], sum_ref[...], preferred_element_type=F32)
            grad = jnp.where(high_ref[span, :].astype(F32) > 0, grad, 0.0)
            bias = bias + jnp.sum(grad, axis=0, keepdims=True)
            hidden_ref[span, :] = grad.astype(BF16)
        for slot in range(lines):
            at = to = slot * rows
            for ref in (stay_ref, late_ref, go_ref):
                if 0 <= to < ref.shape[0]:
                    break
                to -= ref.shape[0]
            ref[to : to + rows, :] = hidden_ref[at : at + rows, :]
        wait_all(row_copies)
        for slot in range(PLANE):
            to = spot ^ away(core, slot, 2)
            ref, at = (keep_ref, send_ref)[slot // 2], slot % 2 * width
            ref[at : at + width, :] = across(
                rows_ref[:, aligned(to * width, width)], hidden_ref[...]
            ).astype(BF16)
        for ref in (keep_ref, send_ref):
            ref[2 * width :, :] = bias_rows(bias)

    outs = [array((total // 2, half), BF16)] + [array((total // 4, half), BF16)] * 2
    outs += [array((dim // 2 + TILE, half), BF16)] * 2
    return call(
        kernel, "row_grad", outs, place, [sums],
        [matrix, high, w_weight, w_other] + list(pieces) + list(line_parts),
        [
            pltpu.VMEM((nodes, dim), BF16),
            pltpu.VMEM((total, dim), BF16),
            pltpu.VMEM((nodes, half), BF16),
            pltpu.VMEM((total, half), BF16),
            pltpu.VMEM((half, dim), BF16),
            pltpu.VMEM((total, nodes), BF16),
            pltpu.VMEM((total, half), BF16),
            pltpu.SemaphoreType.DMA((PIECES,)),
            pltpu.SemaphoreType.DMA((2 * lines - 1,)),
            pltpu.SemaphoreType.DMA(()),
            pltpu.SemaphoreType.DMA((2,)),
        ],
        flops=2 * nodes * dim * half + 2 * total * nodes * half + 2 * total * dim * half,
        limit=VMEM_BYTES if lines <= PLANE else ALL_VMEM,
    )


def fold(place, keep, came):
    height, width = keep.shape[0] - TILE, keep.shape[1]
    part = height // 2

    def kernel(place_ref, keep_ref, came_ref, stay_ref, go_ref):
        bias = keep_ref[height:, :].astype(F32) + came_ref[height:, :].astype(F32)
        bias = bias_rows(bias[0:1] + bias[1:2])
        for ref, at in ((stay_ref, 0), (go_ref, part)):
            span = slice(at, at + part)
            ref[:part, :] = (keep_ref[span, :].astype(F32) + came_ref[span, :].astype(F32)).astype(BF16)
            ref[part:, :] = bias

    return call(
        kernel, "fold", [array((part + TILE, width), BF16)] * 2, place, [keep, came]
    )


def merge(place, keep, came):
    height, width = keep.shape[0] - TILE, keep.shape[1]

    def kernel(place_ref, keep_ref, came_ref, out_ref):
        out_ref[...] = (keep_ref[...].astype(F32) + came_ref[...].astype(F32)).astype(BF16)
        bias = keep_ref[height:, :].astype(F32) + came_ref[height:, :].astype(F32)
        out_ref[height:, :] = bias_rows(bias[0:1] + bias[1:2])

    (out,) = call(kernel, "merge", [array(keep.shape, BF16)], place, [keep, came])
    return out


def unpack(place, blocks, spots, lines=0, sides=1, onto=None):
    parts = 2 if lines else 1
    height, width = blocks[0].shape
    count = len(blocks)

    def kernel(place_ref, *refs):
        sources, refs = refs[:count], refs[count + (onto is not None) :]
        out_ref, block_ref, wide_ref, sem, out_sem = refs
        spot = place_ref[0] % PLANE
        copies = [
            pltpu.make_async_copy(source, block_ref.at[index], sem.at[index])
            for index, source in enumerate(sources)
        ]
        start_all(copies)
        outs = []
        for index, copy in enumerate(copies):
            side, slot, at = spots[index]
            core = place_ref[1] ^ side
            row = (spot ^ away(core, slot, 2)) * parts
            if lines:
                row = row + (line_side(place_ref, lines) ^ at)
            cols = aligned(core * width, width) if sides > 1 else pl.ds(0, width)
            copy.wait()
            wide_ref[index] = block_ref[index].astype(F32)
            outs.append(
                pltpu.make_async_copy(
                    wide_ref.at[index], out_ref.at[aligned(row * height, height), cols],
                    out_sem.at[index],
                )
            )
            outs[-1].start()
        wait_all(outs)

    (out,) = call(
        kernel, "unpack", [array((PLANE * parts * height, width * sides), F32)], place, [],
        list(blocks) + ([] if onto is None else [onto]),
        [
            pltpu.VMEM((count, height, width), BF16), pltpu.VMEM((count, height, width), F32),
            pltpu.SemaphoreType.DMA((count,)), pltpu.SemaphoreType.DMA((count,)),
        ],
        far_outs=1, aliases={} if onto is None else {count + 1: 0},
    )
    return out


def on_device(
    features, neighbours, present, importance, q_weight, q_bias, w_weight, w_bias, cotangent
):
    rows, dim = features.shape
    count = lax.axis_size("nodes")
    lines = count // PLANE
    line_bits = bits_of(lines)
    node = lax.axis_index("nodes")
    core = lax.axis_index("stream")
    place = jnp.stack([node, core]).astype(I32)
    half_rows = rows // 2
    fence = lax.optimization_barrier

    def swap(value, bit, other_bit=None):
        bits = (bit, bit if other_bit is None else other_bit)
        pairs = [
            (2 * at + side, 2 * (at ^ bits[side]) + side) for at in range(count) for side in (0, 1)
        ]
        return lax.ppermute(value, ("nodes", "stream"), pairs)

    def plane_swap(value, step):
        return swap(value, 1 << step, 2 >> step)

    def line_swap(value, step):
        return swap(value, PLANE << step, PLANE << (line_bits - 1 - step))

    def trade(value):
        return lax.ppermute(value, "stream", [(0, 1), (1, 0)])

    def own_half(value, axis):
        size = value.shape[axis] // 2
        return lax.dynamic_slice_in_dim(value, core * size, size, axis)

    def joined(mine, other, axis):
        return jnp.where(
            core == 0,
            jnp.concatenate([mine, other], axis),
            jnp.concatenate([other, mine], axis),
        )

    mine = own_half(features, 0)
    stages = [line_swap(mine, line_bits - 1)]
    lists = sort_slots(place, neighbours, present, importance, count)
    lists = [jnp.concatenate([lists, trade(lists)], 0)]
    lists.append(plane_swap(lists[0], 1))
    lists[1], stages[0] = fence((lists[1], stages[0]))
    for step in reversed(range(line_bits - 1)):
        stages.append(line_swap(jnp.concatenate([mine] + stages, 0), step))
    lists.append(plane_swap(jnp.concatenate(lists, 0), 0))
    traded = [trade(stage) for stage in stages[:-1]]
    matrix, weight_sums = slot_matrix(place, lists, count)
    matrix, stages[-1], traded = fence((matrix, stages[-1], traded))
    line_parts = [features] + stages + traded + [trade(stages[-1])]
    send, high, low = first_sums(place, line_parts, q_weight, q_bias[None], matrix)
    send, w_sent = fence((send, w_weight))
    w_other = trade(w_sent)

    came = plane_swap(send, 0)
    keep, middle, own_send = more_sums(place, [high], [low], matrix, 0, 3)
    came_own = plane_swap(own_send, 0)
    last = plane_swap(middle + came, 1)
    self_part = self_product(place, features, w_weight, w_other, w_bias[None])
    came_own, self_part, keep, weight_sum = fence((came_own, self_part, keep, weight_sums[:rows, 0]))
    mean_half = ((keep + came_own + last) / weight_sum[:, None]).astype(BF16)

    mean_other = trade(mean_half)
    own_slice, next_slice, send_slices = plane_slices(place, features, mean_half, mean_other)
    far_slices = plane_swap(send_slices, 0)
    embeddings, grad_linear, grad_half = node_step(
        place, mean_half, mean_other, self_part, cotangent, w_weight, w_other
    )

    one, two = plane_swap(grad_half, 1), plane_swap(grad_half, 0)
    last_slices = plane_swap(jnp.concatenate([next_slice, far_slices[rows:]], 0), 1)
    one = fence(one)
    three = plane_swap(one, 0)
    three, last_slices = fence((three, last_slices))
    pieces = [grad_linear, one, two, three, trade(one), trade(two), trade(three)]
    slices = [own_slice, far_slices, next_slice, last_slices]
    w_keep, w_send = self_weight(place, pieces, slices, lines)
    pieces, w_keep, w_send = fence((pieces, w_keep, w_send))

    stay, late, go, q_keep, q_send = row_grad(
        place, weight_sums, pieces, w_weight, w_other, matrix, high, line_parts, lines
    )
    w_came = line_swap(w_send, 0)
    stay, late, go, q_keep, q_send, w_keep, w_came = fence(
        (stay, late, go, q_keep, q_send, w_keep, w_came)
    )

    def last_sum(keep, came):
        height = keep.shape[0] - TILE
        total = keep.astype(F32) + came.astype(F32)
        return total[:height].astype(BF16), total[height] + total[height + 1]

    biases = {}

    rows_go, rows_late = line_swap(go, 0), line_swap(late, 0)
    q_came = plane_swap(q_send, 0)
    w_sum = merge(place, w_keep, w_came)
    w_came = line_swap(w_sum, 1)
    q_came = fence(q_came)
    q_keep, q_send = fold(place, q_keep, q_came)
    q_came, w_came, stay, rows_go = fence((plane_swap(q_send, 1), w_came, stay, rows_go))
    for step in range(2, line_bits):
        w_sum = merge(place, w_sum, w_came)
        w_came = line_swap(w_sum, step)
    q_sum = merge(place, q_keep, q_came)
    q_came = line_swap(q_sum, 0)
    w_near, biases["w"] = last_sum(w_sum, w_came)
    w_far = line_swap(w_near, 0)
    near_one, near_two = plane_swap(w_near, 1), plane_swap(w_near, 0)
    self_grad = self_feature(place, grad_linear, w_weight, w_other)
    q_came, w_far, near_one, near_two, biases, self_grad, rows_late = fence(
        (q_came, w_far, near_one, near_two, biases, self_grad, rows_late)
    )
    for step in range(1, line_bits):
        q_sum = merge(place, q_sum, q_came)
        q_came = line_swap(q_sum, step)
    near_three = plane_swap(near_one, 0)
    far_one, far_two = plane_swap(w_far, 1), plane_swap(w_far, 0)
    q_came, near_three, far_one, far_two = fence((q_came, near_three, far_one, far_two))
    q_own, biases["q"] = last_sum(q_sum, q_came)
    half = stay.shape[0] // 2
    upper = (stay[half:].astype(F32) + rows_go.astype(F32)).astype(BF16)
    q_own, upper = fence((q_own, upper))
    rows_next = line_swap(upper, 1)
    q_one, q_two = plane_swap(q_own, 1), plane_swap(q_own, 0)
    far_three = plane_swap(far_one, 0)
    w_all = [w_near, w_far, near_one, far_one, near_two, far_two, near_three]
    w_part = unpack(
        place, w_all, [(0, at // 2, at % 2) for at in range(2 * PLANE - 1)], lines
    )
    bias_other = trade(biases["q"][None])
    q_one, far_three, rows_next, biases, w_part, bias_other = fence(
        (q_one, far_three, rows_next, biases, w_part, bias_other)
    )
    q_three = plane_swap(q_one, 0)
    w_grad = unpack(place, [far_three], [(0, 3, 1)], lines, 1, w_part)
    w_bias_grad, q_bias_half = biases["w"], biases["q"][None]

    stay = stay[: stay.shape[0] // 2]
    for step in range(2, line_bits):
        half = rows_late.shape[0] // 2
        upper = stay[half:].astype(F32) + rows_late[half:] + rows_next[half:]
        rows_next = (rows_next[:half] + line_swap(upper.astype(BF16), step).astype(F32)).astype(BF16)
        stay, rows_late = stay[:half], rows_late[:half]
    row_half = row_sums(place, stay, rows_late, rows_next)
    row_other = trade(row_half)
    q_mine = [q_own, q_one, q_two]
    q_other = [trade(block) for block in q_mine]
    feature_grad, q_bias_grad = feature_step(
        place, self_grad, row_half, row_other, q_weight, q_bias_half, bias_other
    )
    q_three, q_other, w_grad, q_bias_grad, feature_grad = fence(
        (q_three, q_other, w_grad, q_bias_grad, feature_grad)
    )
    last_other = trade(q_three)
    q_part = unpack(place, q_mine + [q_three], [(0, at, 0) for at in range(PLANE)], 0, 2)
    q_part, last_other = fence((q_part, last_other))
    q_grad = unpack(
        place, q_other + [last_other], [(1, at, 0) for at in range(PLANE)], 0, 2, q_part
    )
    return (embeddings, feature_grad, q_grad, q_bias_grad[0], w_grad, w_bias_grad)


def solution(mesh):
    in_specs = (
        P("nodes", None),
        P("nodes", "stream"),
        P("nodes", "stream"),
        P("nodes", "stream"),
        P(),
        P(),
        P("stream", None),
        P(),
        P("nodes", None),
    )
    out_specs = (P("nodes", None), P("nodes", "stream"), P(), P(), P("stream", None), P())
    return jax.shard_map(
        on_device, mesh=mesh, in_specs=in_specs, out_specs=out_specs, check_vma=False
    )
```

```python
import jax
import jax.numpy as jnp
from jax import lax
from jax.experimental import pallas as pl
from jax.experimental.pallas import tpu as pltpu
from jax.sharding import PartitionSpec as P

PLANE = 4
TILE = 16
PIECES = 2 * PLANE - 1
VMEM_BYTES = 48 * 1024 * 1024
ALL_VMEM = 67_000_000
F32, BF16, I32 = jnp.float32, jnp.bfloat16, jnp.int32


def across(lhs, rhs):
    return lax.dot_general(lhs, rhs, (((0,), (0,)), ((), ())), preferred_element_type=F32)


def times_t(lhs, rhs):
    return lax.dot_general(lhs, rhs, (((1,), (1,)), ((), ())), preferred_element_type=F32)


def aligned(start, size):
    start = start if isinstance(start, int) else pl.multiple_of(start, size)
    return pl.ds(start, size)


def spaced(space, arrays):
    return [pl.BlockSpec(memory_space=space) for _ in arrays]


def array(shape, dtype):
    return jax.ShapeDtypeStruct(shape, dtype)


def call(kernel, name, outs, place, near, far=(), scratch=(), flops=0, far_outs=0,
         limit=VMEM_BYTES, light=False, aliases={}):
    operands = list(near) + list(far)
    moved = sum(a.size * a.dtype.itemsize for a in operands + list(outs))
    if light:
        flops, moved = 1, 1
    return pl.pallas_call(
        kernel,
        name=name,
        out_shape=list(outs),
        in_specs=spaced(pltpu.SMEM, [place]) + spaced(pltpu.VMEM, near) + spaced(pltpu.HBM, far),
        out_specs=spaced(pltpu.VMEM, outs[: len(outs) - far_outs])
        + spaced(pltpu.HBM, outs[len(outs) - far_outs :]),
        scratch_shapes=list(scratch),
        input_output_aliases=aliases,
        compiler_params=pltpu.CompilerParams(vmem_limit_bytes=limit),
        cost_estimate=pl.CostEstimate(
            flops=int(flops), bytes_accessed=int(moved), transcendentals=0
        ),
    )(place, *operands)


def reversed_bits(value, bits):
    out = 0
    for bit in range(bits):
        out = out | (((value >> bit) & 1) << (bits - 1 - bit))
    return out


def away(core, slot, bits):
    return jnp.where(core == 0, reversed_bits(slot, bits), slot)


def bits_of(size):
    return size.bit_length() - 1


def line_side(place_ref, lines):
    line = place_ref[0] // PLANE
    return jnp.where(place_ref[1] == 0, line & 1, line // (lines // 2))


def bias_rows(value):
    top = value.astype(BF16).astype(F32)
    row_at = lax.broadcasted_iota(I32, (TILE, value.shape[1]), 0)
    return jnp.where(row_at == 0, top, jnp.where(row_at == 1, value - top, 0.0)).astype(BF16)


def stacked(parts, target, sem, first=0):
    copies, at = [], 0
    for index, part in enumerate(parts):
        span = pl.ds(at, part.shape[0])
        copies.append(pltpu.make_async_copy(part, target.at[span, :], sem.at[first + index]))
        at += part.shape[0]
    return copies


def line_copies(parts, target, sem):
    own, parts = parts[0], parts[1:]
    mine, other = parts[: len(parts) // 2], parts[len(parts) // 2 :]
    rows, bits = own.shape[0], len(mine)
    half = rows // 2
    copies = [pltpu.make_async_copy(own, target.at[pl.ds(0, rows), :], sem.at[0])]
    for slot in range(1, 1 << bits):
        for index, (stages, at) in enumerate(((mine, slot), (other, reversed_bits(slot, bits)))):
            stage = at.bit_length() - 1
            view = stages[stage].at[pl.ds((at - (1 << stage)) * half, half), :]
            spot = target.at[pl.ds(slot * rows + index * half, half), :]
            copies.append(pltpu.make_async_copy(view, spot, sem.at[2 * slot - 1 + index]))
    return copies


def start_all(copies):
    for copy in copies:
        copy.start()


def wait_all(copies):
    for copy in copies:
        copy.wait()


def sort_slots(place, neighbours, present, importance, count):
    rows, slots = neighbours.shape
    turns = -(-slots // count)
    arrays = [neighbours.T, present.T, importance.T]

    def kernel(place_ref, *refs):
        out_ref, neighbours_ref, present_ref, importance_ref, sem = refs[3:]
        copies = [
            pltpu.make_async_copy(part, target, sem.at[index])
            for index, (part, target) in enumerate(zip(refs[:3], refs[4:7]))
        ]
        start_all(copies)
        wait_all(copies)
        slot_at = lax.broadcasted_iota(I32, (slots, rows), 0)
        node_at = lax.broadcasted_iota(I32, (slots, rows), 1)
        block = (node_at * slots + slot_at) & (count - 1)
        row = neighbours_ref[...] - rows * block
        packed = row * 128 + present_ref[...] * importance_ref[...]
        block_at = lax.broadcasted_iota(I32, (count, rows), 0)
        node_at = lax.broadcasted_iota(I32, (count, rows), 1)
        first = (block_at - slots * node_at) & (count - 1)
        for turn in range(turns):
            total = jnp.zeros((count, rows), I32)
            for slot in range(slots):
                at = slot - count * turn
                if 0 <= at < count:
                    total = jnp.where(first == at, packed[slot : slot + 1, :], total)
            out_ref[turn * count : (turn + 1) * count, :] = total

    (out,) = call(
        kernel, "sort_slots", [array((turns * count, rows), I32)], place, [], arrays,
        [pltpu.VMEM((slots, rows), I32)] * 3 + [pltpu.SemaphoreType.DMA((3,))], limit=ALL_VMEM,
    )
    return out


def slot_matrix(place, lists, count):
    tall, rows = lists[0].shape
    lines, width, turns = count // PLANE, PLANE * rows, tall // count

    def kernel(place_ref, own_ref, next_ref, rest_ref, sums_ref, far_ref, out_ref, sem):
        slot_refs = [(own_ref, 0), (next_ref, 0), (rest_ref, 0), (rest_ref, tall)]
        core, spot, line = place_ref[1], place_ref[0] % PLANE, place_ref[0] // PLANE
        sums = [
            jnp.sum((ref[at : at + tall, :] & 127).astype(F32), axis=0, keepdims=True)
            for ref, at in slot_refs
        ]
        sums = jnp.broadcast_to(jnp.concatenate(sums, axis=1), (8, width))
        sums_ref[...] = sums.T
        for at in range(lines):
            block = (line ^ away(core, at, bits_of(lines))) * PLANE + spot
            ids, weights = [], []
            for turn in range(turns):
                listed = jnp.concatenate(
                    [ref[pl.ds(at + turn * count + block, 1), :] for ref, at in slot_refs],
                    axis=1,
                )
                ids.append(((listed >> 7) - rows // 2).astype(F32).astype(BF16))
                weights.append((listed & 127).astype(F32).astype(BF16))
            shift = core * (rows // 2) if at else 0

            @pl.loop(0, rows // TILE)
            def _(step):
                base = step * TILE + shift
                base = jnp.where(base >= rows, base - rows, base)
                row_at = lax.broadcasted_iota(I32, (TILE, width), 0) + (base - rows // 2)
                row_at = row_at.astype(F32).astype(BF16)
                zero = jnp.zeros((TILE, width), BF16)
                total = zero
                for listed, weight in zip(ids, weights):
                    total = total + jnp.where(listed == row_at, weight, zero)
                out_ref[aligned(at * rows + step * TILE, TILE), :] = total

            span = pl.ds(at * rows, rows)
            pltpu.make_async_copy(out_ref.at[span, :], far_ref.at[span, :], sem.at[at]).start()
        for at in range(lines):
            span = pl.ds(at * rows, rows)
            pltpu.make_async_copy(out_ref.at[span, :], far_ref.at[span, :], sem.at[at]).wait()

    sums, matrix = call(
        kernel, "slot_matrix", [array((width, 8), F32), array((lines * rows, width), BF16)],
        place, lists,
        scratch=[pltpu.VMEM((lines * rows, width), BF16), pltpu.SemaphoreType.DMA((lines,))],
        flops=3 * turns * lines * rows * width, far_outs=1, limit=ALL_VMEM, light=True,
    )
    return matrix, sums


def half_copy(core, q_in, q_ref, sem):
    half = q_ref.shape[1]
    return pltpu.make_async_copy(q_in.at[:, aligned(core * half, half)], q_ref, sem)


def hidden_of(core, rows, q_ref, bias_ref):
    half = q_ref.shape[1]
    bias = bias_ref[:, aligned(core * half, half)]
    hidden = jnp.maximum(jnp.dot(rows, q_ref[...], preferred_element_type=F32) + bias, 0.0)
    top = hidden.astype(BF16)
    return top, (hidden - top.astype(F32)).astype(BF16)


def lane_span(start, size):
    low = start // 128 * 128
    high = -(-(start + size) // 128) * 128
    return low, high - low, start - low


def first_sums(place, line_parts, q_weight, q_bias, matrix):
    rows, dim = line_parts[0].shape
    total, width = matrix.shape
    half, part, count = dim // 2, width // PLANE, len(line_parts)
    lines = total // rows
    low, span_width, skip = lane_span(width - part, part)

    def kernel(place_ref, bias_ref, q_in, matrix_in, *refs):
        parts, refs = refs[:count], refs[count:]
        send_ref, high_out, low_out, rows_ref, high_ref, low_ref, matrix_ref, q_ref = refs[:8]
        row_sem, sem = refs[8:]
        core = place_ref[1]
        q_copy = half_copy(core, q_in, q_ref, sem.at[0])
        matrix_copy = pltpu.make_async_copy(
            matrix_in.at[:, pl.ds(low, span_width)], matrix_ref, sem.at[1]
        )
        copies = line_copies(parts, rows_ref, row_sem)
        start_all([q_copy] + copies + [matrix_copy])
        q_copy.wait()
        for at in range(lines):
            wait_all(copies[max(2 * at - 1, 0) : 2 * at + 1])
            span = slice(at * rows, (at + 1) * rows)
            high_ref[span, :], low_ref[span, :] = hidden_of(
                core, rows_ref[span, :], q_ref, bias_ref
            )
        outs = [
            pltpu.make_async_copy(high_ref, high_out, sem.at[2]),
            pltpu.make_async_copy(low_ref, low_out, sem.at[3]),
        ]
        start_all(outs)
        matrix_copy.wait()
        total_sum = across(matrix_ref[...], high_ref[...]) + across(matrix_ref[...], low_ref[...])
        send_ref[...] = total_sum[skip : skip + part, :]
        wait_all(outs)

    return call(
        kernel, "first_sums",
        [array((part, half), F32)] + [array((total, half), BF16)] * 2,
        place, [q_bias], [q_weight, matrix] + list(line_parts),
        [
            pltpu.VMEM((total, dim), BF16),
            pltpu.VMEM((total, half), BF16),
            pltpu.VMEM((total, half), BF16),
            pltpu.VMEM((total, span_width), BF16),
            pltpu.VMEM((dim, half), BF16),
            pltpu.SemaphoreType.DMA((2 * lines - 1,)),
            pltpu.SemaphoreType.DMA((4,)),
        ],
        flops=2 * total * dim * half + 4 * total * part * half, far_outs=2, limit=ALL_VMEM,
    )


def more_sums(place, highs, lows, matrix, first, slots):
    total = matrix.shape[0]
    part = matrix.shape[1] // PLANE
    width = slots * part
    start, span_width, skip = lane_span(first * part, width)
    half, count = highs[0].shape[1], len(highs)

    def kernel(place_ref, matrix_in, *refs):
        parts, refs = refs[: 2 * count], refs[2 * count :]
        sum_refs, refs = refs[:slots], refs[slots:]
        high_ref, low_ref, matrix_ref, sem = refs
        copies = [
            pltpu.make_async_copy(
                matrix_in.at[:, pl.ds(start, span_width)], matrix_ref, sem.at[2 * count]
            )
        ]
        copies += stacked(parts[:count], high_ref, sem)
        copies += stacked(parts[count:], low_ref, sem, count)
        start_all(copies)
        wait_all(copies)
        total_sum = across(matrix_ref[...], high_ref[...]) + across(matrix_ref[...], low_ref[...])
        for slot, sum_ref in enumerate(sum_refs):
            at = skip + slot * part
            sum_ref[...] = total_sum[at : at + part, :]

    return call(
        kernel, "more_sums", [array((part, half), F32)] * slots, place, [],
        [matrix] + list(highs) + list(lows),
        [
            pltpu.VMEM((total, half), BF16),
            pltpu.VMEM((total, half), BF16),
            pltpu.VMEM((total, span_width), BF16),
            pltpu.SemaphoreType.DMA((2 * count + 1,)),
        ],
        flops=4 * total * width * half, limit=ALL_VMEM,
    )


def pick_copy(core, first, second, target, sem, rows=None):
    views = [ref if rows is None else ref.at[rows, :] for ref in (first, second)]
    for side, view in enumerate(views):

        @pl.when(core == side)
        def _():
            pltpu.make_async_copy(view, target, sem).start()

    return pltpu.make_async_copy(views[0], target, sem)


def self_product(place, features, w_weight, w_other, w_bias):
    rows, dim = features.shape

    def kernel(place_ref, features_ref, bias_ref, w_in, w_other_in, out_ref, w_ref, sem):
        pick_copy(place_ref[1], w_in, w_other_in, w_ref, sem).wait()
        out_ref[...] = bias_ref[...] + jnp.dot(
            features_ref[...], w_ref[...], preferred_element_type=F32
        )

    (out,) = call(
        kernel, "self_product", [array((rows, dim), F32)], place, [features, w_bias],
        [w_weight, w_other], [pltpu.VMEM((dim, dim), BF16), pltpu.SemaphoreType.DMA(())],
        flops=2 * rows * dim * dim,
    )
    return out


def row_sums(place, stay, late, come):
    rows, half = late.shape

    def kernel(place_ref, stay_ref, late_ref, come_ref, out_ref):
        for part in range(2):
            span = slice(part * rows // 2, (part + 1) * rows // 2)
            came = late_ref[span, :].astype(F32) + come_ref[span, :].astype(F32)
            at = aligned((place_ref[1] ^ part) * (rows // 2), rows // 2)
            out_ref[at, :] = (stay_ref[at, :].astype(F32) + came).astype(BF16)

    (out,) = call(kernel, "row_sums", [array((rows, half), BF16)], place, [stay, late, come])
    return out


def self_feature(place, grad_linear, w_weight, w_other):
    rows, dim = grad_linear.shape
    half = dim // 2

    def kernel(place_ref, grad_ref, w_in, w_other_in, out_ref, w_ref, sem):
        core = place_ref[1]
        pick_copy(core, w_in, w_other_in, w_ref, sem, aligned(core * half, half)).wait()
        out_ref[...] = times_t(grad_ref[...], w_ref[...])

    (out,) = call(
        kernel, "self_feature", [array((rows, half), F32)], place, [grad_linear],
        [w_weight, w_other], [pltpu.VMEM((half, dim), BF16), pltpu.SemaphoreType.DMA(())],
        flops=2 * rows * dim * half,
    )
    return out


def feature_step(place, self_grad, mine, other, q_weight, bias_mine, bias_other):
    rows, half = mine.shape
    dim = 2 * half

    def kernel(
        place_ref, self_ref, mine_ref, other_ref, bias_mine_ref, bias_other_ref, q_in,
        out_ref, bias_ref, q_ref, sem,
    ):
        core = place_ref[1]
        spans = [aligned(core * half, half), aligned((1 - core) * half, half)]
        q_copy = pltpu.make_async_copy(q_in.at[spans[0], :], q_ref, sem)
        q_copy.start()
        bias_ref[:, spans[0]] = bias_mine_ref[...]
        bias_ref[:, spans[1]] = bias_other_ref[...]
        q_copy.wait()
        out_ref[...] = (
            self_ref[...]
            + times_t(mine_ref[...], q_ref[:, spans[0]])
            + times_t(other_ref[...], q_ref[:, spans[1]])
        )

    return call(
        kernel, "feature_step", [array((rows, half), F32), array((1, dim), F32)], place,
        [self_grad, mine, other, bias_mine, bias_other], [q_weight],
        [pltpu.VMEM((half, dim), BF16), pltpu.SemaphoreType.DMA(())],
        flops=2 * rows * dim * half,
    )


def plane_slices(place, features, mine, other):
    rows, dim = features.shape
    half, width = dim // 2, dim // PLANE

    def kernel(place_ref, features_ref, mine_ref, other_ref, own_ref, next_ref, send_ref):
        core, spot = place_ref[1], place_ref[0] % PLANE
        targets = [own_ref, next_ref, send_ref.at[pl.ds(0, rows), :], send_ref.at[pl.ds(rows, rows), :]]
        for slot, target in enumerate(targets):
            to = spot ^ away(core, slot, 2)

            @pl.when(core == 0)
            def _():
                target[...] = features_ref[:, aligned(to * width, width)]

            within = aligned(to % 2 * width, width)

            @pl.when((core == 1) & (to < 2))
            def _():
                target[...] = other_ref[:, within]

            @pl.when((core == 1) & (to >= 2))
            def _():
                target[...] = mine_ref[:, within]

    outs = [array((rows, width), BF16)] * 2 + [array((2 * rows, width), BF16)]
    return call(kernel, "plane_slices", outs, place, [features, mine, other])


def node_step(place, mine, other, self_part, cotangent, w_weight, w_other):
    rows, half = mine.shape
    dim = 2 * half

    def kernel(
        place_ref, mine_ref, other_ref, self_ref, cotangent_ref, w_in, w_other_in,
        embeddings_ref, grad_ref, half_ref, lhs_ref, linear_ref, near_ref, sem,
    ):
        core = place_ref[1]
        near_copy = pick_copy(core, w_other_in, w_in, near_ref, sem)
        lhs_ref[:, aligned(core * half, half)] = mine_ref[...]
        lhs_ref[:, aligned((1 - core) * half, half)] = other_ref[...]
        near_copy.wait()
        linear_ref[...] = self_ref[...] + jnp.dot(
            lhs_ref[...], near_ref[...], preferred_element_type=F32
        )

        @pl.loop(0, rows // TILE, unroll=4)
        def _(step):
            at = aligned(step * TILE, TILE)
            linear = linear_ref[at, :]
            relu_out = jnp.maximum(linear, 0.0)
            scale = lax.rsqrt(jnp.mean(relu_out * relu_out, axis=1, keepdims=True) + 1e-06)
            embeddings_ref[at, :] = relu_out * scale
            grad_out = cotangent_ref[at, :].astype(F32)
            inner = jnp.mean(relu_out * grad_out, axis=1, keepdims=True)
            grad_relu = scale * grad_out - relu_out * (scale * scale * scale) * inner
            grad_ref[at, :] = jnp.where(linear > 0, grad_relu, 0.0).astype(BF16)

        half_ref[...] = grad_ref[aligned(core * (rows // 2), rows // 2), :]

    outs = [
        array((rows, dim), F32), array((rows, dim), BF16), array((rows // 2, dim), BF16),
    ]
    return call(
        kernel, "node_step", outs, place, [mine, other, self_part, cotangent],
        [w_weight, w_other],
        [
            pltpu.VMEM((rows, dim), BF16), pltpu.VMEM((rows, dim), F32),
            pltpu.VMEM((dim, dim), BF16), pltpu.SemaphoreType.DMA(()),
        ],
        flops=2 * rows * dim * dim,
    )


def plane_copies(core, rows, pieces, target, sem):
    own = pieces[0]
    half = rows // 2
    copies = [pltpu.make_async_copy(own, target.at[pl.ds(0, rows), :], sem.at[0])]
    for slot in range(1, PLANE):
        mine = pieces[slot]
        other = pieces[PLANE - 1 + reversed_bits(slot, 2)]
        for index, (part, at) in enumerate(((mine, core), (other, 1 - core))):
            spot = pl.multiple_of(slot * rows + at * half, TILE)
            copies.append(
                pltpu.make_async_copy(
                    part, target.at[pl.ds(spot, half), :], sem.at[2 * slot - 1 + index]
                )
            )
    return copies


def self_weight(place, pieces, slices, lines):
    rows, dim = pieces[0].shape
    width = slices[0].shape[1]

    def kernel(place_ref, *refs):
        parts, refs = refs[:PIECES], refs[PIECES:]
        slots, outs = refs[:4], refs[4:6]
        grads_ref, lhs_ref, sum_ref, sem, slice_sem = refs[6:]
        copies = plane_copies(place_ref[1], rows, parts, grads_ref, sem)
        own, far, near, last = slots
        spans = [own, last.at[pl.ds(0, rows), :], far.at[pl.ds(0, rows), :], last.at[pl.ds(rows, rows), :]]
        for slot, part in enumerate(spans):
            copies.append(
                pltpu.make_async_copy(part, lhs_ref.at[pl.ds(slot * rows, rows), :], slice_sem.at[slot])
            )
        for copy in copies:
            copy.start()
        for copy in copies:
            copy.wait()
        sum_ref[...] = across(lhs_ref[...], grads_ref[...])
        bias = bias_rows(jnp.sum(grads_ref[...].astype(F32), axis=0, keepdims=True))
        first = line_side(place_ref, lines)
        for slot, out_ref in enumerate(outs):
            out_ref[: width // 2, :] = sum_ref[
                aligned((first ^ slot) * (width // 2), width // 2), :
            ].astype(BF16)
            out_ref[width // 2 :, :] = bias

    return call(
        kernel, "self_weight", [array((width // 2 + TILE, dim), BF16)] * 2, place, [],
        list(pieces) + list(slices),
        [
            pltpu.VMEM((PLANE * rows, dim), BF16),
            pltpu.VMEM((PLANE * rows, width), BF16),
            pltpu.VMEM((width, dim), F32),
            pltpu.SemaphoreType.DMA((PIECES,)),
            pltpu.SemaphoreType.DMA((PLANE,)),
        ],
        flops=2 * PLANE * rows * dim * width,
    )


def row_grad(place, sums, pieces, w_weight, w_other, matrix, high, line_parts, lines):
    rows, dim = pieces[0].shape
    half = dim // 2
    total, nodes, width = lines * rows, PLANE * rows, dim // PLANE

    def kernel(place_ref, sums_ref, matrix_in, high_in, w_in, w_other_in, *refs):
        parts, refs = refs[:PIECES], refs[PIECES:]
        row_parts, refs = refs[: len(line_parts)], refs[len(line_parts) :]
        stay_ref, late_ref, go_ref, keep_ref, send_ref, refs = *refs[:5], refs[5:]
        grads_ref, rows_ref, sum_ref, hidden_ref, near_ref, matrix_ref, high_ref = refs[:7]
        sem, row_sem, near_sem, line_sem = refs[7:]
        core, spot = place_ref[1], place_ref[0] % PLANE
        copies = plane_copies(core, rows, parts, grads_ref, sem)
        row_copies = line_copies(row_parts, rows_ref, row_sem)
        near_copy = pick_copy(
            core, w_other_in, w_in, near_ref, near_sem, aligned(core * half, half)
        )
        line_sums = [
            pltpu.make_async_copy(matrix_in, matrix_ref, line_sem.at[0]),
            pltpu.make_async_copy(high_in, high_ref, line_sem.at[1]),
        ]
        start_all(copies + line_sums + row_copies)
        near_copy.wait()
        for slot in range(PLANE):
            wait_all(copies[max(2 * slot - 1, 0) : 2 * slot + 1])
            span = slice(slot * rows, (slot + 1) * rows)
            grad = times_t(grads_ref[span, :], near_ref[...])
            sum_ref[span, :] = (grad / sums_ref[span, 0:1]).astype(BF16)
        wait_all(line_sums)
        bias = jnp.zeros((1, half), F32)
        for at in range(lines):
            span = slice(at * rows, (at + 1) * rows)
            grad = jnp.dot(matrix_ref[span, :], sum_ref[...], preferred_element_type=F32)
            grad = jnp.where(high_ref[span, :].astype(F32) > 0, grad, 0.0)
            bias = bias + jnp.sum(grad, axis=0, keepdims=True)
            hidden_ref[span, :] = grad.astype(BF16)
        for slot in range(lines):
            at = to = slot * rows
            for ref in (stay_ref, late_ref, go_ref):
                if 0 <= to < ref.shape[0]:
                    break
                to -= ref.shape[0]
            ref[to : to + rows, :] = hidden_ref[at : at + rows, :]
        wait_all(row_copies)
        for slot in range(PLANE):
            to = spot ^ away(core, slot, 2)
            ref, at = (keep_ref, send_ref)[slot // 2], slot % 2 * width
            ref[at : at + width, :] = across(
                rows_ref[:, aligned(to * width, width)], hidden_ref[...]
            ).astype(BF16)
        for ref in (keep_ref, send_ref):
            ref[2 * width :, :] = bias_rows(bias)

    outs = [array((total // 2, half), BF16)] + [array((total // 4, half), BF16)] * 2
    outs += [array((dim // 2 + TILE, half), BF16)] * 2
    return call(
        kernel, "row_grad", outs, place, [sums],
        [matrix, high, w_weight, w_other] + list(pieces) + list(line_parts),
        [
            pltpu.VMEM((nodes, dim), BF16),
            pltpu.VMEM((total, dim), BF16),
            pltpu.VMEM((nodes, half), BF16),
            pltpu.VMEM((total, half), BF16),
            pltpu.VMEM((half, dim), BF16),
            pltpu.VMEM((total, nodes), BF16),
            pltpu.VMEM((total, half), BF16),
            pltpu.SemaphoreType.DMA((PIECES,)),
            pltpu.SemaphoreType.DMA((2 * lines - 1,)),
            pltpu.SemaphoreType.DMA(()),
            pltpu.SemaphoreType.DMA((2,)),
        ],
        flops=2 * nodes * dim * half + 2 * total * nodes * half + 2 * total * dim * half,
        limit=VMEM_BYTES if lines <= PLANE else ALL_VMEM,
    )


def fold(place, keep, came):
    height, width = keep.shape[0] - TILE, keep.shape[1]
    part = height // 2

    def kernel(place_ref, keep_ref, came_ref, stay_ref, go_ref):
        bias = keep_ref[height:, :].astype(F32) + came_ref[height:, :].astype(F32)
        bias = bias_rows(bias[0:1] + bias[1:2])
        for ref, at in ((stay_ref, 0), (go_ref, part)):
            span = slice(at, at + part)
            ref[:part, :] = (keep_ref[span, :].astype(F32) + came_ref[span, :].astype(F32)).astype(BF16)
            ref[part:, :] = bias

    return call(
        kernel, "fold", [array((part + TILE, width), BF16)] * 2, place, [keep, came]
    )


def merge(place, keep, came):
    height, width = keep.shape[0] - TILE, keep.shape[1]

    def kernel(place_ref, keep_ref, came_ref, out_ref):
        out_ref[...] = (keep_ref[...].astype(F32) + came_ref[...].astype(F32)).astype(BF16)
        bias = keep_ref[height:, :].astype(F32) + came_ref[height:, :].astype(F32)
        out_ref[height:, :] = bias_rows(bias[0:1] + bias[1:2])

    (out,) = call(kernel, "merge", [array(keep.shape, BF16)], place, [keep, came])
    return out


def unpack(place, blocks, spots, lines=0, sides=1, onto=None):
    parts = 2 if lines else 1
    height, width = blocks[0].shape
    count = len(blocks)

    def kernel(place_ref, *refs):
        sources, refs = refs[:count], refs[count + (onto is not None) :]
        out_ref, block_ref, wide_ref, sem, out_sem = refs
        spot = place_ref[0] % PLANE
        copies = [
            pltpu.make_async_copy(source, block_ref.at[index], sem.at[index])
            for index, source in enumerate(sources)
        ]
        start_all(copies)
        outs = []
        for index, copy in enumerate(copies):
            side, slot, at = spots[index]
            core = place_ref[1] ^ side
            row = (spot ^ away(core, slot, 2)) * parts
            if lines:
                row = row + (line_side(place_ref, lines) ^ at)
            cols = aligned(core * width, width) if sides > 1 else pl.ds(0, width)
            copy.wait()
            wide_ref[index] = block_ref[index].astype(F32)
            outs.append(
                pltpu.make_async_copy(
                    wide_ref.at[index], out_ref.at[aligned(row * height, height), cols],
                    out_sem.at[index],
                )
            )
            outs[-1].start()
        wait_all(outs)

    (out,) = call(
        kernel, "unpack", [array((PLANE * parts * height, width * sides), F32)], place, [],
        list(blocks) + ([] if onto is None else [onto]),
        [
            pltpu.VMEM((count, height, width), BF16), pltpu.VMEM((count, height, width), F32),
            pltpu.SemaphoreType.DMA((count,)), pltpu.SemaphoreType.DMA((count,)),
        ],
        far_outs=1, aliases={} if onto is None else {count + 1: 0},
    )
    return out


def on_device(
    features, neighbours, present, importance, q_weight, q_bias, w_weight, w_bias, cotangent
):
    rows, dim = features.shape
    count = lax.axis_size("nodes")
    lines = count // PLANE
    line_bits = bits_of(lines)
    node = lax.axis_index("nodes")
    core = lax.axis_index("stream")
    place = jnp.stack([node, core]).astype(I32)
    half_rows = rows // 2
    fence = lax.optimization_barrier

    def swap(value, bit, other_bit=None):
        bits = (bit, bit if other_bit is None else other_bit)
        pairs = [
            (2 * at + side, 2 * (at ^ bits[side]) + side) for at in range(count) for side in (0, 1)
        ]
        return lax.ppermute(value, ("nodes", "stream"), pairs)

    def plane_swap(value, step):
        return swap(value, 1 << step, 2 >> step)

    def line_swap(value, step):
        return swap(value, PLANE << step, PLANE << (line_bits - 1 - step))

    def trade(value):
        return lax.ppermute(value, "stream", [(0, 1), (1, 0)])

    def own_half(value, axis):
        size = value.shape[axis] // 2
        return lax.dynamic_slice_in_dim(value, core * size, size, axis)

    def joined(mine, other, axis):
        return jnp.where(
            core == 0,
            jnp.concatenate([mine, other], axis),
            jnp.concatenate([other, mine], axis),
        )

    mine = own_half(features, 0)
    stages = [line_swap(mine, line_bits - 1)]
    lists = sort_slots(place, neighbours, present, importance, count)
    lists = [jnp.concatenate([lists, trade(lists)], 0)]
    lists.append(plane_swap(lists[0], 1))
    lists[1], stages[0] = fence((lists[1], stages[0]))
    for step in reversed(range(line_bits - 1)):
        stages.append(line_swap(jnp.concatenate([mine] + stages, 0), step))
    lists.append(plane_swap(jnp.concatenate(lists, 0), 0))
    traded = [trade(stage) for stage in stages[:-1]]
    matrix, weight_sums = slot_matrix(place, lists, count)
    matrix, stages[-1], traded = fence((matrix, stages[-1], traded))
    line_parts = [features] + stages + traded + [trade(stages[-1])]
    send, high, low = first_sums(place, line_parts, q_weight, q_bias[None], matrix)
    send, w_sent = fence((send, w_weight))
    w_other = trade(w_sent)

    came = plane_swap(send, 0)
    keep, middle, own_send = more_sums(place, [high], [low], matrix, 0, 3)
    came_own = plane_swap(own_send, 0)
    last = plane_swap(middle + came, 1)
    self_part = self_product(place, features, w_weight, w_other, w_bias[None])
    came_own, self_part, keep, weight_sum = fence((came_own, self_part, keep, weight_sums[:rows, 0]))
    mean_half = ((keep + came_own + last) / weight_sum[:, None]).astype(BF16)

    mean_other = trade(mean_half)
    own_slice, next_slice, send_slices = plane_slices(place, features, mean_half, mean_other)
    far_slices = plane_swap(send_slices, 0)
    embeddings, grad_linear, grad_half = node_step(
        place, mean_half, mean_other, self_part, cotangent, w_weight, w_other
    )

    one, two = plane_swap(grad_half, 1), plane_swap(grad_half, 0)
    last_slices = plane_swap(jnp.concatenate([next_slice, far_slices[rows:]], 0), 1)
    one = fence(one)
    three = plane_swap(one, 0)
    three, last_slices = fence((three, last_slices))
    pieces = [grad_linear, one, two, three, trade(one), trade(two), trade(three)]
    slices = [own_slice, far_slices, next_slice, last_slices]
    w_keep, w_send = self_weight(place, pieces, slices, lines)
    pieces, w_keep, w_send = fence((pieces, w_keep, w_send))

    stay, late, go, q_keep, q_send = row_grad(
        place, weight_sums, pieces, w_weight, w_other, matrix, high, line_parts, lines
    )
    w_came = line_swap(w_send, 0)
    stay, late, go, q_keep, q_send, w_keep, w_came = fence(
        (stay, late, go, q_keep, q_send, w_keep, w_came)
    )

    def last_sum(keep, came):
        height = keep.shape[0] - TILE
        total = keep.astype(F32) + came.astype(F32)
        return total[:height].astype(BF16), total[height] + total[height + 1]

    biases = {}

    rows_go, rows_late = line_swap(go, 0), line_swap(late, 0)
    q_came = plane_swap(q_send, 0)
    w_sum = merge(place, w_keep, w_came)
    w_came = line_swap(w_sum, 1)
    q_came = fence(q_came)
    q_keep, q_send = fold(place, q_keep, q_came)
    q_came, w_came, stay, rows_go = fence((plane_swap(q_send, 1), w_came, stay, rows_go))
    for step in range(2, line_bits):
        w_sum = merge(place, w_sum, w_came)
        w_came = line_swap(w_sum, step)
    q_sum = merge(place, q_keep, q_came)
    q_came = line_swap(q_sum, 0)
    w_near, biases["w"] = last_sum(w_sum, w_came)
    w_far = line_swap(w_near, 0)
    near_one, near_two = plane_swap(w_near, 1), plane_swap(w_near, 0)
    self_grad = self_feature(place, grad_linear, w_weight, w_other)
    q_came, w_far, near_one, near_two, biases, self_grad, rows_late = fence(
        (q_came, w_far, near_one, near_two, biases, self_grad, rows_late)
    )
    for step in range(1, line_bits):
        q_sum = merge(place, q_sum, q_came)
        q_came = line_swap(q_sum, step)
    near_three = plane_swap(near_one, 0)
    far_one, far_two = plane_swap(w_far, 1), plane_swap(w_far, 0)
    q_came, far_one = fence((q_came, far_one))
    q_own, biases["q"] = last_sum(q_sum, q_came)
    half = stay.shape[0] // 2
    upper = (stay[half:].astype(F32) + rows_go.astype(F32)).astype(BF16)
    q_own, upper = fence((q_own, upper))
    rows_next = line_swap(upper, 1)
    q_one, q_two = plane_swap(q_own, 1), plane_swap(q_own, 0)
    far_three = plane_swap(far_one, 0)
    w_all = [w_near, w_far, near_one, far_one, near_two, far_two, near_three]
    w_part = unpack(
        place, w_all, [(0, at // 2, at % 2) for at in range(2 * PLANE - 1)], lines
    )
    bias_other = trade(biases["q"][None])
    q_one, far_three, rows_next, biases, w_part, bias_other = fence(
        (q_one, far_three, rows_next, biases, w_part, bias_other)
    )
    q_three = plane_swap(q_one, 0)
    w_grad = unpack(place, [far_three], [(0, 3, 1)], lines, 1, w_part)
    w_bias_grad, q_bias_half = biases["w"], biases["q"][None]

    stay = stay[: stay.shape[0] // 2]
    for step in range(2, line_bits):
        half = rows_late.shape[0] // 2
        upper = stay[half:].astype(F32) + rows_late[half:] + rows_next[half:]
        rows_next = (rows_next[:half] + line_swap(upper.astype(BF16), step).astype(F32)).astype(BF16)
        stay, rows_late = stay[:half], rows_late[:half]
    row_half = row_sums(place, stay, rows_late, rows_next)
    row_other = trade(row_half)
    q_mine = [q_own, q_one, q_two]
    q_other = [trade(block) for block in q_mine]
    feature_grad, q_bias_grad = feature_step(
        place, self_grad, row_half, row_other, q_weight, q_bias_half, bias_other
    )
    q_three, q_other, w_grad, q_bias_grad, feature_grad = fence(
        (q_three, q_other, w_grad, q_bias_grad, feature_grad)
    )
    last_other = trade(q_three)
    q_part = unpack(place, q_mine + [q_three], [(0, at, 0) for at in range(PLANE)], 0, 2)
    q_part, last_other = fence((q_part, last_other))
    q_grad = unpack(
        place, q_other + [last_other], [(1, at, 0) for at in range(PLANE)], 0, 2, q_part
    )
    return (embeddings, feature_grad, q_grad, q_bias_grad[0], w_grad, w_bias_grad)


def solution(mesh):
    in_specs = (
        P("nodes", None),
        P("nodes", "stream"),
        P("nodes", "stream"),
        P("nodes", "stream"),
        P(),
        P(),
        P("stream", None),
        P(),
        P("nodes", None),
    )
    out_specs = (P("nodes", None), P("nodes", "stream"), P(), P(), P("stream", None), P())
    return jax.shard_map(
        on_device, mesh=mesh, in_specs=in_specs, out_specs=out_specs, check_vma=False
    )
```
